32 devices in a mesh: grp: 2 (over y), pre: 4 (over z), row: 4 (over x, core).
Axes of the slice: x: 2, y: 2, z: 4, core: 2. Of those that a mesh axis runs over, the one named last changes fastest.
Arguments:
- queries: bfloat16 [32, 2, 8192], P(('grp', 'row')), parts along dimension 0, may hold values from -200 to 200
- prefix_keys: bfloat16 [1024, 1024], P(('grp', 'pre')), parts along dimension 0, may hold values from -7 to 7
- prefix_values: bfloat16 [1024, 1024], P(('grp', 'pre')), parts along dimension 0, may hold values from -6 to 6
- suffix_keys: bfloat16 [32, 64, 1024], P(('grp', 'row'), 'pre'), parts along dimension 0, may hold values from -6 to 6
- suffix_values: bfloat16 [32, 64, 1024], P(('grp', 'row'), 'pre'), parts along dimension 0, may hold values from -6 to 6
- new_keys: bfloat16 [32, 2, 1024], P(('grp', 'row')), parts along dimension 0, may hold values from -6 to 6
- new_values: bfloat16 [32, 2, 1024], P(('grp', 'row')), parts along dimension 0, may hold values from -6 to 6
- hidden: bfloat16 [32, 2, 8192], P(('grp', 'pre'), None, 'row'), parts along dimension 0, may hold values from -6 to 6
- adapter_ids: int32 [32], P(('grp', 'row')), parts along dimension 0, may hold values from 0 to 127
- suffix_lengths: int32 [32], P(('grp', 'row')), parts along dimension 0, may hold values from 1 to 64
- kv_scales: bfloat16 [128, 2, 1024], replicated, may hold values from 0.25 to 1.75
- ffn_scales: bfloat16 [128, 14336], P(None, 'pre'), may hold values from 0.25 to 1.75
- out_weight: bfloat16 [8192, 8192], P('pre', 'row'), may hold values from -0.0625 to 0.0625
- norm_gain: bfloat16 [8192], P('row'), may hold values from 0.25 to 1.75
- gate_up: bfloat16 [8192, 2, 14336], P('row', None, 'pre'), may hold values from -0.0625 to 0.0625
Outputs:
- residual: bfloat16 [32, 2, 8192], P(('grp', 'pre'), None, 'row'), parts along dimension 0
- activation: bfloat16 [32, 2, 14336], P(('grp', 'row'), None, 'pre'), parts along dimension 0
The draws below stay inside these ranges and needn't reach their ends.
There are 2 independent parts, one for each index of `grp`. The reference program is written for one: setup_inputs(seed, part) draws one part's arguments, and reference() takes and returns one part's arrays. A program takes and returns all parts, laid end to end along the dimension named above; an argument that names none is the same for every part. Nothing has to cross between parts.
All inputs are finite; a program needn't handle non-finite values.
Results may differ from the reference program's by a relative error of at most 0.015.
Values may be sent and summed in bfloat16 or wider, within the bound.
A program may use at most 128 MiB of HBM per device.

```python
import jax
import jax.numpy as jnp
from jax import lax

D = 8192
HEADS = 64
KV_HEADS = 8
HD = 128
FFW = 14336
ADAPTERS = 128
STEPS = 2
ROWS = 16
PREFIX = 512
SUFFIX = 64


def shared_keys(key):
    prompt = jax.random.truncated_normal(jax.random.fold_in(key, 101), -6.0, 6.0, (PREFIX, KV_HEADS * HD), jnp.float32)
    fresh = jax.random.truncated_normal(jax.random.fold_in(key, 103), -6.0, 6.0, (ROWS, STEPS, KV_HEADS * HD), jnp.float32)
    return (prompt, fresh)


def draw_prefix_keys(key, part):
    return shared_keys(key)[0].astype(jnp.bfloat16)


def draw_new_keys(key, part):
    return shared_keys(key)[1].astype(jnp.bfloat16)


def draw_queries(key, part):
    prompt, fresh = shared_keys(key)
    group_size = HEADS // KV_HEADS
    noise = jax.random.truncated_normal(jax.random.fold_in(key, 104), -6.0, 6.0, (ROWS, STEPS, D), jnp.float32)
    running = jnp.cumsum(fresh, axis=1).reshape(ROWS, STEPS, KV_HEADS, 1, HD)
    spread = jnp.broadcast_to(running, (ROWS, STEPS, KV_HEADS, group_size, HD)).reshape(ROWS, STEPS, D)
    result = noise + 0.6 * spread
    return result.astype(jnp.bfloat16)


def with_ends(values, key, low, largest):
    extent = values.shape
    index_at = [jax.random.randint(jax.random.fold_in(key, axis), (), 0, extent[axis]) for axis in range(len(extent))]
    values = values.at[tuple(index_at)].set(low)
    longest = extent.index(max(extent))
    index_at[longest] = (index_at[longest] + 1) % extent[longest]
    return values.at[tuple(index_at)].set(largest)


def block_scale(own_key, dims, split, low, largest):
    def one(axis_at, shards_of):
        steps = jax.random.uniform(jax.random.fold_in(jax.random.fold_in(own_key, 6), axis_at), (shards_of,), jnp.float32, low / len(split), largest / len(split))
        return jnp.repeat(jnp.exp(steps), dims[axis_at] // shards_of).reshape((-1,) + (1,) * (len(dims) - axis_at - 1))

    factor_of = one(*split[0])
    for cut in split[1:]:
        factor_of = factor_of * one(*cut)
    return factor_of


def normal_values(key, dims, scale, most, shards=(), kind=jnp.bfloat16):
    drawn = jax.random.normal(key, dims, jnp.float32) * scale
    if len(shards) > 0:
        drawn = block_scale(key, dims, shards, -0.22, 0.18) * drawn
    return jnp.clip(drawn, min=-most, max=most).astype(kind)


def setup_inputs(seed: int = 0, part: int = 0) -> dict:
    key_of = jax.random.split(jax.random.key(seed), 16)
    own_keys = jax.random.split(jax.random.fold_in(key_of[15], part), 16)
    return {
        "queries": draw_queries(jax.random.fold_in(jax.random.fold_in(key_of[15], part), 71), part),
        "prefix_keys": draw_prefix_keys(jax.random.fold_in(jax.random.fold_in(key_of[15], part), 71), part),
        "prefix_values": normal_values(own_keys[2], (PREFIX, KV_HEADS * HD), 1.0, 6.0, ((0, 4),)),
        "suffix_keys": normal_values(own_keys[3], (ROWS, SUFFIX, KV_HEADS * HD), 1.0, 6.0, ((0, 4), (1, 4))),
        "suffix_values": normal_values(own_keys[4], (ROWS, SUFFIX, KV_HEADS * HD), 1.0, 6.0, ((0, 4), (1, 4))),
        "new_keys": draw_new_keys(jax.random.fold_in(jax.random.fold_in(key_of[15], part), 71), part),
        "new_values": normal_values(own_keys[6], (ROWS, STEPS, KV_HEADS * HD), 1.0, 6.0, ((0, 4),)),
        "hidden": normal_values(own_keys[7], (ROWS, STEPS, D), 1.0, 6.0, ((0, 4), (2, 4))),
        "adapter_ids": with_ends(jax.random.randint(own_keys[8], (ROWS,), 0, ADAPTERS), jax.random.fold_in(own_keys[8], 1), 0, ADAPTERS - 1).astype(jnp.int32),
        "suffix_lengths": with_ends(jax.random.randint(own_keys[9], (ROWS,), 1, SUFFIX + 1), jax.random.fold_in(own_keys[9], 1), 1, SUFFIX).astype(jnp.int32),
        "kv_scales": jnp.clip(1.0 + 0.15 * jax.random.normal(key_of[10], (ADAPTERS, 2, KV_HEADS * HD), jnp.float32), 0.25, 1.75).astype(jnp.bfloat16),
        "ffn_scales": jnp.clip(1.0 + 0.15 * jax.random.normal(key_of[11], (ADAPTERS, FFW), jnp.float32), 0.25, 1.75).astype(jnp.bfloat16),
        "out_weight": normal_values(key_of[12], (D, D), D ** -0.5, 0.0625, ((0, 4), (1, 4))),
        "norm_gain": jnp.clip(1.0 + 0.15 * jax.random.normal(key_of[13], (D,), jnp.float32), 0.25, 1.75).astype(jnp.bfloat16),
        "gate_up": normal_values(key_of[14], (D, 2, FFW), D ** -0.5, 0.0625, ((0, 4), (2, 4))),
    }


masked_score = -1e+30

def settle(values):
    return lax.optimization_barrier(values.astype(jnp.bfloat16)).astype(jnp.float32)

def reference(queries, prefix_keys, prefix_values, suffix_keys, suffix_values, new_keys, new_values, hidden, adapter_ids, suffix_lengths, kv_scales, ffn_scales, out_weight, norm_gain, gate_up):
    group_size = HEADS // KV_HEADS
    score_scale = HD ** (-0.5)
    chosen = jnp.take(kv_scales, adapter_ids, axis=0).astype(jnp.float32)
    key_scale = chosen[:, 0].reshape(ROWS, KV_HEADS, HD)
    value_scale = chosen[:, 1].reshape(ROWS, KV_HEADS, HD)
    query_heads = queries.astype(jnp.float32).reshape(ROWS, STEPS, KV_HEADS, group_size, HD)
    scaled_query = settle(query_heads * key_scale[:, None, :, None, :])
    fresh_key = settle(new_keys.astype(jnp.float32).reshape(ROWS, STEPS, KV_HEADS, HD) * key_scale[:, None])
    fresh_value = settle(new_values.astype(jnp.float32).reshape(ROWS, STEPS, KV_HEADS, HD) * value_scale[:, None])
    cached_key = prefix_keys.astype(jnp.float32).reshape(PREFIX, KV_HEADS, HD)
    cached_value = prefix_values.astype(jnp.float32).reshape(PREFIX, KV_HEADS, HD)
    recent_key = suffix_keys.astype(jnp.float32).reshape(ROWS, SUFFIX, KV_HEADS, HD)
    recent_value = suffix_values.astype(jnp.float32).reshape(ROWS, SUFFIX, KV_HEADS, HD)
    prefix_scores = jnp.einsum('rskgd,tkd->rskgt', scaled_query, cached_key) * score_scale
    in_suffix = (jnp.arange(SUFFIX, dtype=jnp.int32)[None, :] < suffix_lengths[:, None])[:, None, None, None, :]
    suffix_scores = jnp.einsum('rskgd,rtkd->rskgt', query_heads, recent_key) * score_scale
    suffix_scores = jnp.where(in_suffix, suffix_scores, masked_score)
    in_order = (jnp.arange(STEPS)[None, :] <= jnp.arange(STEPS)[:, None])[None, :, None, None, :]
    new_scores = jnp.einsum('rskgd,rnkd->rskgn', query_heads, fresh_key) * score_scale
    new_scores = jnp.where(in_order, new_scores, masked_score)
    peak_score = jnp.maximum(jnp.maximum(lax.optimization_barrier(jnp.max(prefix_scores, axis=-1)), lax.optimization_barrier(jnp.max(suffix_scores, axis=-1))), lax.optimization_barrier(jnp.max(new_scores, axis=-1)))
    prefix_weight = settle(jnp.exp(prefix_scores - peak_score[..., None]))
    suffix_weight = settle(jnp.where(in_suffix, jnp.exp(suffix_scores - peak_score[..., None]), 0.0))
    new_weight = settle(jnp.where(in_order, jnp.exp(new_scores - peak_score[..., None]), 0.0))
    weight_sum = lax.optimization_barrier(jnp.sum(prefix_weight, axis=-1)) + lax.optimization_barrier(jnp.sum(suffix_weight, axis=-1)) + lax.optimization_barrier(jnp.sum(new_weight, axis=-1))
    numerator = jnp.einsum('rskgt,tkd->rskgd', prefix_weight, cached_value) * value_scale[:, None, :, None, :]
    numerator = numerator + jnp.einsum('rskgt,rtkd->rskgd', suffix_weight, recent_value)
    numerator = numerator + jnp.einsum('rskgn,rnkd->rskgd', new_weight, fresh_value)
    mixed_heads = (numerator / weight_sum[..., None]).astype(jnp.bfloat16).reshape(ROWS * STEPS, D)
    projected = jnp.dot(mixed_heads, out_weight, preferred_element_type=jnp.float32)
    residual = (hidden.astype(jnp.float32).reshape(ROWS * STEPS, D) + projected).astype(jnp.bfloat16)
    widened = residual.astype(jnp.float32)
    inverse = lax.rsqrt(lax.optimization_barrier(jnp.sum(widened * widened, axis=1, keepdims=True)) / D + 1e-05)
    normed = (widened * norm_gain.astype(jnp.float32)).astype(jnp.bfloat16)
    gate_part = jnp.dot(normed, gate_up[:, 0, :], preferred_element_type=jnp.float32) * inverse
    up_part = jnp.dot(normed, gate_up[:, 1, :], preferred_element_type=jnp.float32) * inverse
    adapter_rows = jnp.take(ffn_scales, adapter_ids, axis=0).astype(jnp.float32)
    activation = (jax.nn.silu(gate_part) * up_part).reshape(ROWS, STEPS, FFW) * adapter_rows[:, None, :]
    return (residual.reshape(ROWS, STEPS, D), activation.astype(jnp.bfloat16))
```

```python
import functools

import jax
import jax.numpy as jnp
from jax import lax
from jax.experimental import pallas as pl
from jax.experimental.pallas import tpu as pltpu
from jax.sharding import PartitionSpec as P

D = 8192
HEADS = 64
KV_HEADS = 8
HD = 128
STEPS = 2
GROUP = HEADS // KV_HEADS
LANES = 128
FFN_GROUPS = 7

masked_score = -1e30
f32 = jnp.float32
bf16 = jnp.bfloat16


def iota(shape, axis):
    return lax.broadcasted_iota(jnp.int32, shape, axis)


def layer_kernel(
    sizes,
    ids_ref,
    lens_ref,
    q_ref,
    pk_ref,
    pv_ref,
    sk_ref,
    sv_ref,
    nk_ref,
    nv_ref,
    hid_ref,
    kvs_ref,
    gain_ref,
    ffs_hbm,
    ow_hbm,
    gu_hbm,
    res_out,
    act_out,
    ow,
    gu,
    ffs,
    q8,
    ks8,
    vs8,
    fk8,
    fv8,
    acc_s,
    acc_r,
    stat_s,
    stat_r,
    mix_g,
    mix_x,
    prod_s,
    prod_f,
    prod_r,
    res_g,
    x_exp,
    gate_s,
    gate_f,
    gate_r,
    sq_s,
    sq_r,
    ffn8,
    ow_sem,
    gu_sem,
    ffs_sem,
    acc_sem,
    stat_sem,
    mix_sem,
    prod_sem,
    res_sem,
    pass_sem,
    gate_sem,
    sq_sem,
):
    pre_n, row_n, split = sizes
    grp = lax.rem(lax.axis_index("grp"), split)
    pre = lax.axis_index("pre")
    row = lax.axis_index("row")
    row_local = q_ref.shape[0]
    rs = row_local * STEPS
    hid_local = hid_ref.shape[0]
    hs = hid_local * STEPS
    suffix_local = sk_ref.shape[1]
    kv_width = pk_ref.shape[1]
    adapters = kvs_ref.shape[0]
    block = D // pre_n
    heads_block = block // HD
    cols = ow_hbm.shape[1]
    depth = gu_hbm.shape[0]
    ff = gu_hbm.shape[2]
    score_scale = HD ** (-0.5)
    n_out, _, out_width = ow.shape
    n_tiles = gu.shape[0]
    share = n_tiles * LANES
    group_width = gate_s.shape[4]
    tiles_group = n_tiles // FFN_GROUPS
    everyone = row_n * rs

    gu_rows = gu_hbm.reshape(2 * depth, ff)

    def ow_copy(c):
        return pltpu.make_async_copy(
            ow_hbm.at[:, pl.ds(c * out_width, out_width)], ow.at[c], ow_sem.at[c]
        )

    def gu_copy(c):
        return pltpu.make_async_copy(
            gu_rows.at[:, pl.ds(pl.multiple_of(grp * share + c * LANES, LANES), LANES)], gu.at[c], gu_sem.at[c]
        )

    ffs_copy = pltpu.make_async_copy(ffs_hbm, ffs, ffs_sem)
    for c in range(n_out):
        ow_copy(c).start()
    ffs_copy.start()
    for c in range(n_tiles):
        gu_copy(c).start()

    barrier = pltpu.get_barrier_semaphore()
    for d in range(1, pre_n):
        pl.semaphore_signal(
            barrier,
            inc=1,
            device_id={"pre": lax.rem(pre + d, pre_n)},
            device_id_type=pl.DeviceIdType.MESH,
        )
    for d in range(1, row_n):
        pl.semaphore_signal(
            barrier,
            inc=1,
            device_id={"row": lax.rem(row + d, row_n)},
            device_id_type=pl.DeviceIdType.MESH,
        )
    for e in range(1, split):
        for d in range(row_n):
            pl.semaphore_signal(
                barrier,
                inc=1,
                device_id={"grp": lax.rem(grp + e, split), "row": lax.rem(row + d, row_n)},
                device_id_type=pl.DeviceIdType.MESH,
            )

    def remote(src, dst, sems, axis, target, group=None):
        return pltpu.make_async_remote_copy(
            src_ref=src,
            dst_ref=dst,
            send_sem=sems[0],
            recv_sem=sems[1],
            device_id={axis: target} if group is None else {"grp": group, axis: target},
            device_id_type=pl.DeviceIdType.MESH,
        )

    def pair(sem, *at):
        return sem.at[(0,) + at], sem.at[(1,) + at]

    def ahead(d):
        return lax.rem(pre + d, pre_n)

    def beside(d):
        return lax.rem(row + d, row_n)

    def acc_copy(d):
        return remote(acc_s.at[ahead(d)], acc_r.at[d - 1], pair(acc_sem, d - 1), "pre", ahead(d))

    def stat_copy(d):
        return remote(stat_s.at[ahead(d)], stat_r.at[d - 1], pair(stat_sem, d - 1), "pre", ahead(d))

    def mix_copy(d):
        return remote(mix_g.at[row], mix_g.at[row], pair(mix_sem, d - 1), "row", beside(d))

    def prod_copy(c, d):
        return remote(
            prod_s.at[c, ahead(d)], prod_r.at[c, d - 1], pair(prod_sem, c, d - 1), "pre", ahead(d)
        )

    def res_copy(d):
        block_at = res_g.at[grp, pre]
        return remote(block_at, block_at, pair(res_sem, d - 1), "pre", ahead(d))

    def across(e):
        return lax.rem(grp + e, split)

    def pass_copy(e, d):
        block_at = res_g.at[grp, lax.rem(pre + pre_n - d, pre_n)]
        return remote(block_at, block_at, pair(pass_sem, e - 1, d), "grp", across(e))

    def sq_copy(d):
        return remote(sq_s.at[beside(d)], sq_r.at[d - 1], pair(sq_sem, d - 1), "row", beside(d))

    def gate_copy(g, e, d):
        return remote(
            gate_s.at[g, e, beside(d)],
            gate_r.at[g, e, d],
            pair(gate_sem, g, e, d),
            "row",
            beside(d),
            across(e) if e > 0 else None,
        )

    others = [(e, d) for e in range(split) for d in range(row_n) if e + d > 0]

    def per_row(ref, shape):
        which = iota(shape, 0) // STEPS
        out = jnp.full(shape, ref[0], jnp.int32)
        for r in range(1, row_local):
            out = jnp.where(which == r, ref[r], out)
        return out

    adapter = per_row(ids_ref, (rs, 2 * adapters))
    lane = iota((rs, 2 * adapters), 1)
    pick_key = jnp.where(lane == 2 * adapter, 1.0, 0.0)
    pick_value = jnp.where(lane == 2 * adapter + 1, 1.0, 0.0)
    pick = jnp.concatenate([pick_key, pick_value], axis=0).astype(bf16)
    scales = jnp.dot(
        pick, kvs_ref[...].reshape(2 * adapters, kv_width), preferred_element_type=f32
    )
    ks8[...] = scales[:rs]
    vs8[...] = scales[rs:]
    fk8[...] = nk_ref[...].astype(f32).reshape(rs, kv_width) * scales[:rs]
    fv8[...] = nv_ref[...].astype(f32).reshape(rs, kv_width) * scales[rs:]
    q8[...] = q_ref[...].astype(f32).reshape(rs, D)

    unit_heads = min(GROUP, heads_block)
    units = heads_block // unit_heads
    unit_rows = unit_heads * rs
    suffix_rows = row_local * suffix_local
    own_rows = -(-(suffix_rows + rs) // LANES) * LANES
    pad = own_rows - suffix_rows - rs
    at_row = lax.rem(iota((unit_rows, own_rows), 0), rs)
    at_col = iota((unit_rows, own_rows), 1)
    lens = per_row(lens_ref, (rs, own_rows))
    lens = jnp.concatenate([lens] * unit_heads, axis=0)
    query_row = at_row // STEPS
    query_step = lax.rem(at_row, STEPS)
    position = pre * suffix_local + lax.rem(at_col, suffix_local)
    fresh_at = at_col - suffix_rows
    in_suffix = (at_col < suffix_rows) & (at_col // suffix_local == query_row) & (position < lens)
    in_new = (
        (fresh_at >= 0)
        & (fresh_at < rs)
        & (fresh_at // STEPS == query_row)
        & (lax.rem(fresh_at, STEPS) <= query_step)
        & (pre == 0)
    )
    mask = in_suffix | in_new
    stat_lane = iota((rs, LANES), 1)
    transposed = (((1,), (1,)), ((), ()))

    def with_fresh(old, fresh):
        tail = jnp.concatenate([fresh, jnp.zeros((pad, HD), f32)], axis=0) if pad else fresh
        return jnp.concatenate([old.reshape(suffix_rows, HD), tail.astype(bf16)], axis=0)

    def attend(b, finish):
        peaks = jnp.zeros((rs, LANES), f32)
        totals = jnp.ones((rs, LANES), f32)
        for i in range(units):
            first = b * heads_block + i * unit_heads
            kv = pl.ds(pl.multiple_of(first // GROUP * HD, HD), HD)
            pieces = [
                q8[:, pl.ds(pl.multiple_of((first + g) * HD, HD), HD)] for g in range(unit_heads)
            ]
            key_scale = ks8[:, kv]
            value_scale = vs8[:, kv]
            query = jnp.concatenate(pieces, axis=0).astype(bf16)
            scaled = jnp.concatenate([piece * key_scale for piece in pieces], axis=0).astype(bf16)
            own_keys = with_fresh(sk_ref[:, :, kv], fk8[:, kv])
            own_values = with_fresh(sv_ref[:, :, kv], fv8[:, kv])
            prefix_scores = (
                lax.dot_general(scaled, pk_ref[:, kv], transposed, preferred_element_type=f32)
                * score_scale
            )
            own_scores = (
                lax.dot_general(query, own_keys, transposed, preferred_element_type=f32)
                * score_scale
            )
            own_scores = jnp.where(mask, own_scores, masked_score)
            peak = jnp.maximum(
                jnp.max(prefix_scores, axis=1, keepdims=True),
                jnp.max(own_scores, axis=1, keepdims=True),
            )
            prefix_weight = jnp.exp(prefix_scores - peak).astype(bf16)
            own_weight = jnp.where(mask, jnp.exp(own_scores - peak), 0.0).astype(bf16)
            total = jnp.sum(prefix_weight.astype(f32), axis=1, keepdims=True) + jnp.sum(
                own_weight.astype(f32), axis=1, keepdims=True
            )
            numerator = jnp.dot(prefix_weight, pv_ref[:, kv], preferred_element_type=f32)
            numerator = numerator * jnp.concatenate([value_scale] * unit_heads, axis=0)
            numerator = numerator + jnp.dot(own_weight, own_values, preferred_element_type=f32)
            for g in range(unit_heads):
                j = i * unit_heads + g
                part = slice(g * rs, (g + 1) * rs)
                peaks = jnp.where(stat_lane == j, peak[part], peaks)
                totals = jnp.where(stat_lane == j, total[part], totals)
                acc_s[b, :, j * HD : (j + 1) * HD] = numerator[part].astype(bf16)
        stat_s[b, 0] = peaks
        stat_s[b, 1] = totals
        finish()

    for d in list(range(1, pre_n)) + [0]:

        def finish(d=d):
            if d == 1:
                pl.semaphore_wait(barrier, pre_n + row_n - 2 + (split - 1) * row_n)
            if d > 0:
                stat_copy(d).start()
                acc_copy(d).start()

        attend(ahead(d), finish)

    for d in range(1, pre_n):
        stat_copy(d).wait_recv()
    peak_of = [stat_s[pre, 0]] + [stat_r[d - 1, 0] for d in range(1, pre_n)]
    total_of = [stat_s[pre, 1]] + [stat_r[d - 1, 1] for d in range(1, pre_n)]
    highest = functools.reduce(jnp.maximum, peak_of)
    factor_of = [jnp.exp(peak - highest) for peak in peak_of]
    weight_sum = sum(factor * total for factor, total in zip(factor_of, total_of))
    factor_of = [factor / weight_sum for factor in factor_of]
    for d in range(1, pre_n):
        acc_copy(d).wait_recv()
    for j in range(heads_block):
        part = slice(j * HD, (j + 1) * HD)
        value = acc_s[pre, :, part].astype(f32) * factor_of[0][:, j : j + 1]
        for d in range(1, pre_n):
            value = value + acc_r[d - 1, :, part].astype(f32) * factor_of[d][:, j : j + 1]
        mix_g[row, :, part] = value.astype(bf16)
    for d in range(1, row_n):
        mix_copy(d).start()
    for c in range(n_out):
        ow_copy(c).wait()
    for d in range(1, row_n):
        mix_copy(d).wait_recv()
    mix_x[...] = mix_g[...].astype(f32).reshape(everyone, block).astype(bf16)

    def project(c, carry):
        product = jnp.dot(mix_x[...], ow[c], preferred_element_type=f32)
        for p in range(pre_n):
            part = product[p * hs : (p + 1) * hs]
            prod_f[c, p] = part
            prod_s[c, p] = part.astype(bf16)
        for d in range(1, pre_n):
            prod_copy(c, d).start()
        return carry

    lax.fori_loop(0, n_out, project, 0)
    for c in range(n_out):
        part = slice(c * out_width, (c + 1) * out_width)
        value = hid_ref[:, :, part].astype(f32).reshape(hs, out_width) + prod_f[c, pre]
        for d in range(1, pre_n):
            prod_copy(c, d).wait_recv()
            value = value + prod_r[c, d - 1].astype(f32)
        res_g[grp, pre, :, part] = value.astype(bf16)
        res_out[:, :, part] = value.reshape(hid_local, STEPS, out_width).astype(bf16)
    for d in range(1, pre_n):
        res_copy(d).start()
    for e in range(1, split):
        pass_copy(e, 0).start()
    ffs_copy.wait()
    ffn_pick = jnp.where(
        iota((rs, adapters), 1) == per_row(ids_ref, (rs, adapters)), 1.0, 0.0
    ).astype(bf16)
    ffn8[...] = jnp.dot(ffn_pick, ffs[...], preferred_element_type=f32)

    for d in range(1, pre_n):
        res_copy(d).wait_recv()
        for e in range(1, split):
            pass_copy(e, d).start()

    spread_from = iota((LANES, 4 * LANES), 0)
    spread_to = iota((LANES, 4 * LANES), 1)
    spread = jnp.where(
        spread_to
        == jnp.where(spread_to < 2 * LANES, 2 * spread_from, 2 * LANES + 2 * spread_from + 1),
        1.0,
        0.0,
    ).astype(bf16)

    def spread_rows(e, residual):
        normed = (residual * gain_ref[...].astype(f32).reshape(1, depth)).astype(bf16)
        gate_rows = slice(e * everyone, (e + 1) * everyone)
        up_rows = slice((split + e) * everyone, (split + e + 1) * everyone)
        for j in range(depth // LANES):
            part = jnp.dot(
                normed[:, j * LANES : (j + 1) * LANES], spread, preferred_element_type=f32
            ).astype(bf16)
            x_exp[gate_rows, 2 * j * LANES : 2 * (j + 1) * LANES] = part[:, : 2 * LANES]
            x_exp[up_rows, 2 * j * LANES : 2 * (j + 1) * LANES] = part[:, 2 * LANES :]

    residual = res_g[grp].astype(f32).reshape(everyone, depth)
    squares = jnp.sum(residual * residual, axis=1, keepdims=True)
    for r in range(row_n):
        sq_s[r] = jnp.broadcast_to(squares[r * rs : (r + 1) * rs], (rs, LANES))
    for d in range(1, row_n):
        sq_copy(d).start()
    spread_rows(0, residual)
    for e in range(1, split):
        for d in range(pre_n):
            pass_copy(e, d).wait_recv()
    for e in range(1, split):
        spread_rows(e, res_g[across(e)].astype(f32).reshape(everyone, depth))

    tile_step = 2 if tiles_group % 2 == 0 else 1

    def gate_up_group(g, carry):
        for t in range(0, tiles_group, tile_step):
            tiles = [g * tiles_group + t + i for i in range(tile_step)]
            for tile in tiles:
                gu_copy(tile).wait()
            weights = [gu[tile] for tile in tiles]
            weight = jnp.concatenate(weights, axis=1) if tile_step > 1 else weights[0]
            product = jnp.dot(x_exp[...], weight, preferred_element_type=f32)
            part = slice(t * LANES, (t + tile_step) * LANES)
            for e in range(split):
                for r in range(row_n):
                    at = e * everyone + r * rs
                    up_at = split * everyone + at
                    both = jnp.concatenate(
                        [product[at : at + rs], product[up_at : up_at + rs]], axis=0
                    )
                    if e == 0:
                        gate_f[g, r, :, part] = both
                    gate_s[g, e, r, :, part] = both.astype(bf16)
        for e, d in others:
            gate_copy(g, e, d).start()
        return carry

    lax.fori_loop(0, FFN_GROUPS, gate_up_group, 0)

    square_sum = sq_s[row]
    for d in range(1, row_n):
        sq_copy(d).wait_recv()
        square_sum = square_sum + sq_r[d - 1]
    inverse = lax.rsqrt(square_sum[:, :1] / D + 1e-05)

    def activate(g, carry):
        for e in range(split):
            both = gate_f[g, row] if e == 0 else jnp.zeros((2 * rs, group_width), f32)
            for d in range(1 if e == 0 else 0, row_n):
                gate_copy(g, e, d).wait_recv()
                both = both + gate_r[g, e, d].astype(f32)
            gate = both[:rs] * inverse
            up = both[rs:] * inverse
            start = lax.rem(grp + split - e, split) * share + g * group_width
            part = pl.ds(pl.multiple_of(start, LANES), group_width)
            value = gate / (1.0 + jnp.exp(-gate)) * up * ffn8[:, part]
            act_out[:, :, part] = value.reshape(row_local, STEPS, group_width).astype(bf16)
        for e, d in others:
            gate_copy(g, e, d).wait_send()
        return carry

    lax.fori_loop(0, FFN_GROUPS, activate, 0)

    for d in range(1, pre_n):
        stat_copy(d).wait_send()
        acc_copy(d).wait_send()
        res_copy(d).wait_send()
        for c in range(n_out):
            prod_copy(c, d).wait_send()
    for e in range(1, split):
        for d in range(pre_n):
            pass_copy(e, d).wait_send()
    for d in range(1, row_n):
        mix_copy(d).wait_send()
        sq_copy(d).wait_send()


def hand_on(residual_ref, activation_ref, residual_out, activation_out):
    residual_out[...] = residual_ref[...]
    activation_out[...] = activation_ref[...]


def per_device(
    queries,
    prefix_keys,
    prefix_values,
    suffix_keys,
    suffix_values,
    new_keys,
    new_values,
    hidden,
    adapter_ids,
    suffix_lengths,
    kv_scales,
    ffn_scales,
    out_weight,
    norm_gain,
    gate_up,
):
    pre_n = lax.axis_size("pre")
    row_n = lax.axis_size("row")
    row_local = queries.shape[0]
    rs = row_local * STEPS
    hs = hidden.shape[0] * STEPS
    kv_width = prefix_keys.shape[1]
    adapters, ff = ffn_scales.shape
    block, cols = out_weight.shape
    depth = gate_up.shape[0]
    out_width = min(cols, 512)
    n_out = cols // out_width
    grp_n = lax.axis_size("grp")
    fits = ff % (grp_n * FFN_GROUPS * LANES) == 0
    split = grp_n if fits else 1
    n_tiles = ff // LANES // split
    group_width = ff // split // FFN_GROUPS
    everyone = row_n * rs
    dma = pltpu.SemaphoreType.DMA
    vmem = pl.BlockSpec(memory_space=pltpu.VMEM)
    smem = pl.BlockSpec(memory_space=pltpu.SMEM)
    hbm = pl.BlockSpec(memory_space=pl.ANY)
    scratch = [
        pltpu.VMEM((n_out, block, out_width), bf16),
        pltpu.VMEM((n_tiles, 2 * depth, LANES), bf16),
        pltpu.VMEM((adapters, ff), bf16),
        pltpu.VMEM((rs, D), f32),
        pltpu.VMEM((rs, kv_width), f32),
        pltpu.VMEM((rs, kv_width), f32),
        pltpu.VMEM((rs, kv_width), f32),
        pltpu.VMEM((rs, kv_width), f32),
        pltpu.VMEM((pre_n, rs, block), bf16),
        pltpu.VMEM((pre_n - 1, rs, block), bf16),
        pltpu.VMEM((pre_n, 2, rs, LANES), f32),
        pltpu.VMEM((pre_n - 1, 2, rs, LANES), f32),
        pltpu.VMEM((row_n, rs, block), bf16),
        pltpu.VMEM((everyone, block), bf16),
        pltpu.VMEM((n_out, pre_n, hs, out_width), bf16),
        pltpu.VMEM((n_out, pre_n, hs, out_width), f32),
        pltpu.VMEM((n_out, pre_n - 1, hs, out_width), bf16),
        pltpu.VMEM((split, pre_n, hs, cols), bf16),
        pltpu.VMEM((2 * split * everyone, 2 * depth), bf16),
        pltpu.VMEM((FFN_GROUPS, split, row_n, 2 * rs, group_width), bf16),
        pltpu.VMEM((FFN_GROUPS, row_n, 2 * rs, group_width), f32),
        pltpu.VMEM((FFN_GROUPS, split, row_n, 2 * rs, group_width), bf16),
        pltpu.VMEM((row_n, rs, LANES), f32),
        pltpu.VMEM((row_n - 1, rs, LANES), f32),
        pltpu.VMEM((rs, ff), f32),
        dma((n_out,)),
        dma((n_tiles,)),
        dma,
        dma((2, pre_n - 1)),
        dma((2, pre_n - 1)),
        dma((2, row_n - 1)),
        dma((2, n_out, pre_n - 1)),
        dma((2, pre_n - 1)),
        dma((2, max(split - 1, 1), pre_n)),
        dma((2, FFN_GROUPS, split, row_n)),
        dma((2, row_n - 1)),
    ]
    outputs = pl.pallas_call(
        functools.partial(layer_kernel, (pre_n, row_n, split)),
        out_shape=(
            jax.ShapeDtypeStruct(hidden.shape, bf16),
            jax.ShapeDtypeStruct((row_local, STEPS, ff), bf16),
        ),
        in_specs=[smem, smem] + [vmem] * 10 + [hbm] * 3,
        out_specs=(vmem, vmem),
        scratch_shapes=scratch,
        compiler_params=pltpu.CompilerParams(
            collective_id=0, has_side_effects=True, vmem_limit_bytes=56 * 1024 * 1024
        ),
    )(
        adapter_ids,
        suffix_lengths,
        queries,
        prefix_keys,
        prefix_values,
        suffix_keys,
        suffix_values,
        new_keys,
        new_values,
        hidden,
        kv_scales,
        norm_gain,
        ffn_scales,
        out_weight,
        gate_up,
    )
    return pl.pallas_call(
        hand_on,
        out_shape=tuple(jax.ShapeDtypeStruct(value.shape, value.dtype) for value in outputs),
        in_specs=[vmem, vmem],
        out_specs=(vmem, vmem),
    )(*outputs)


def solution(mesh):
    placed = (
        P(("grp", "row"), None, None),
        P(("grp", "pre"), None),
        P(("grp", "pre"), None),
        P(("grp", "row"), "pre", None),
        P(("grp", "row"), "pre", None),
        P(("grp", "row"), None, None),
        P(("grp", "row"), None, None),
        P(("grp", "pre"), None, "row"),
        P(("grp", "row")),
        P(("grp", "row")),
        P(),
        P(None, "pre"),
        P("pre", "row"),
        P("row"),
        P("row", None, "pre"),
    )
    return jax.shard_map(
        per_device,
        mesh=mesh,
        in_specs=placed,
        out_specs=(P(("grp", "pre"), None, "row"), P(("grp", "row"), None, "pre")),
        check_vma=False,
    )
```

```python
import functools

import jax
import jax.numpy as jnp
from jax import lax
from jax.experimental import pallas as pl
from jax.experimental.pallas import tpu as pltpu
from jax.sharding import PartitionSpec as P

D = 8192
HEADS = 64
KV_HEADS = 8
HD = 128
STEPS = 2
GROUP = HEADS // KV_HEADS
LANES = 128
FFN_GROUPS = 7

GRANT = 40

masked_score = -1e30
f32 = jnp.float32
bf16 = jnp.bfloat16


def iota(shape, axis):
    return lax.broadcasted_iota(jnp.int32, shape, axis)


def layer_kernel(
    sizes,
    ids_hbm,
    lens_hbm,
    q_hbm,
    pk_hbm,
    pv_hbm,
    sk_hbm,
    sv_hbm,
    nk_hbm,
    nv_hbm,
    hid_hbm,
    kvs_hbm,
    gain_hbm,
    ffs_hbm,
    ow_hbm,
    gu_hbm,
    res_out,
    act_out,
    ids_ref,
    lens_ref,
    q_ref,
    pk_ref,
    pv_ref,
    sk_ref,
    sv_ref,
    nk_ref,
    nv_ref,
    hid_ref,
    kvs_ref,
    gain_ref,
    ow,
    gu,
    ffs,
    q8,
    ks8,
    vs8,
    fk8,
    fv8,
    acc_s,
    acc_r,
    stat_s,
    stat_r,
    mix_g,
    mix_x,
    prod_s,
    prod_f,
    prod_r,
    res_g,
    x_exp,
    gate_s,
    gate_f,
    gate_r,
    sq_s,
    sq_r,
    ffn8,
    in_sem,
    ow_sem,
    gu_sem,
    ffs_sem,
    acc_sem,
    stat_sem,
    mix_sem,
    prod_sem,
    res_sem,
    pass_sem,
    gate_sem,
    sq_sem,
):
    pre_n, row_n, split = sizes
    grp = lax.rem(lax.axis_index("grp"), split)
    pre = lax.axis_index("pre")
    row = lax.axis_index("row")
    row_local = q_hbm.shape[0]
    rs = row_local * STEPS
    hid_local = hid_ref.shape[0]
    hs = hid_local * STEPS
    suffix_local = sk_ref.shape[1]
    kv_width = pk_ref.shape[1]
    adapters = kvs_ref.shape[0]
    block = D // pre_n
    heads_block = block // HD
    cols = ow_hbm.shape[1]
    depth = gu_hbm.shape[0]
    ff = gu_hbm.shape[2]
    score_scale = HD ** (-0.5)
    n_out, _, out_width = ow.shape
    n_tiles = gu.shape[0]
    share = n_tiles * LANES
    group_width = gate_s.shape[4]
    tiles_group = n_tiles // FFN_GROUPS
    everyone = row_n * rs

    gu_rows = gu_hbm.reshape(2 * depth, ff)

    def ow_copy(c):
        return pltpu.make_async_copy(
            ow_hbm.at[:, pl.ds(c * out_width, out_width)], ow.at[c], ow_sem.at[c]
        )

    def gu_copy(c):
        return pltpu.make_async_copy(
            gu_rows.at[:, pl.ds(pl.multiple_of(grp * share + c * LANES, LANES), LANES)], gu.at[c], gu_sem.at[c]
        )

    staged = [
        (ids_hbm, ids_ref),
        (lens_hbm, lens_ref),
        (kvs_hbm, kvs_ref),
        (q_hbm, q_ref),
        (nk_hbm, nk_ref),
        (nv_hbm, nv_ref),
        (sk_hbm, sk_ref),
        (pk_hbm, pk_ref),
        (sv_hbm, sv_ref),
        (pv_hbm, pv_ref),
        (hid_hbm, hid_ref),
        (gain_hbm, gain_ref),
    ]
    staged = [
        pltpu.make_async_copy(source, target, in_sem.at[i])
        for i, (source, target) in enumerate(staged)
    ]
    for copy in staged:
        copy.start()
    ffs_copy = pltpu.make_async_copy(ffs_hbm, ffs, ffs_sem)
    for c in range(n_out):
        ow_copy(c).start()
    ffs_copy.start()
    for c in range(n_tiles):
        gu_copy(c).start()

    barrier = pltpu.get_barrier_semaphore()
    for d in range(1, pre_n):
        pl.semaphore_signal(
            barrier,
            inc=1,
            device_id={"pre": lax.rem(pre + d, pre_n)},
            device_id_type=pl.DeviceIdType.MESH,
        )
    for d in range(1, row_n):
        pl.semaphore_signal(
            barrier,
            inc=1,
            device_id={"row": lax.rem(row + d, row_n)},
            device_id_type=pl.DeviceIdType.MESH,
        )
    for e in range(1, split):
        for d in range(row_n):
            pl.semaphore_signal(
                barrier,
                inc=1,
                device_id={"grp": lax.rem(grp + e, split), "row": lax.rem(row + d, row_n)},
                device_id_type=pl.DeviceIdType.MESH,
            )

    def remote(src, dst, sems, axis, target, group=None):
        return pltpu.make_async_remote_copy(
            src_ref=src,
            dst_ref=dst,
            send_sem=sems[0],
            recv_sem=sems[1],
            device_id={axis: target} if group is None else {"grp": group, axis: target},
            device_id_type=pl.DeviceIdType.MESH,
        )

    def pair(sem, *at):
        return sem.at[(0,) + at], sem.at[(1,) + at]

    def ahead(d):
        return lax.rem(pre + d, pre_n)

    def beside(d):
        return lax.rem(row + d, row_n)

    def acc_copy(d):
        return remote(acc_s.at[ahead(d)], acc_r.at[d - 1], pair(acc_sem, d - 1), "pre", ahead(d))

    def stat_copy(d):
        return remote(stat_s.at[ahead(d)], stat_r.at[d - 1], pair(stat_sem, d - 1), "pre", ahead(d))

    def mix_copy(d):
        return remote(mix_g.at[row], mix_g.at[row], pair(mix_sem, d - 1), "row", beside(d))

    def prod_copy(c, d):
        return remote(
            prod_s.at[c, ahead(d)], prod_r.at[c, d - 1], pair(prod_sem, c, d - 1), "pre", ahead(d)
        )

    def res_copy(d):
        block_at = res_g.at[grp, pre]
        return remote(block_at, block_at, pair(res_sem, d - 1), "pre", ahead(d))

    def across(e):
        return lax.rem(grp + e, split)

    def pass_copy(e, d):
        block_at = res_g.at[grp, lax.rem(pre + pre_n - d, pre_n)]
        return remote(block_at, block_at, pair(pass_sem, e - 1, d), "grp", across(e))

    def sq_copy(d):
        return remote(sq_s.at[beside(d)], sq_r.at[d - 1], pair(sq_sem, d - 1), "row", beside(d))

    def gate_copy(g, e, d):
        return remote(
            gate_s.at[g, e, beside(d)],
            gate_r.at[g, e, d],
            pair(gate_sem, g, e, d),
            "row",
            beside(d),
            across(e) if e > 0 else None,
        )

    others = [(e, d) for e in range(split) for d in range(row_n) if e + d > 0]

    def per_row(ref, shape):
        which = iota(shape, 0) // STEPS
        out = jnp.full(shape, ref[0], jnp.int32)
        for r in range(1, row_local):
            out = jnp.where(which == r, ref[r], out)
        return out

    for copy in staged[:6]:
        copy.wait()
    adapter = per_row(ids_ref, (rs, 2 * adapters))
    lane = iota((rs, 2 * adapters), 1)
    pick_key = jnp.where(lane == 2 * adapter, 1.0, 0.0)
    pick_value = jnp.where(lane == 2 * adapter + 1, 1.0, 0.0)
    pick = jnp.concatenate([pick_key, pick_value], axis=0).astype(bf16)
    scales = jnp.dot(
        pick, kvs_ref[...].reshape(2 * adapters, kv_width), preferred_element_type=f32
    )
    ks8[...] = scales[:rs]
    vs8[...] = scales[rs:]
    fk8[...] = nk_ref[...].astype(f32).reshape(rs, kv_width) * scales[:rs]
    fv8[...] = nv_ref[...].astype(f32).reshape(rs, kv_width) * scales[rs:]
    q8[...] = q_ref[...].astype(f32).reshape(rs, D)

    unit_heads = min(GROUP, heads_block)
    units = heads_block // unit_heads
    unit_rows = unit_heads * rs
    suffix_rows = row_local * suffix_local
    own_rows = -(-(suffix_rows + rs) // LANES) * LANES
    pad = own_rows - suffix_rows - rs
    at_row = lax.rem(iota((unit_rows, own_rows), 0), rs)
    at_col = iota((unit_rows, own_rows), 1)
    lens = per_row(lens_ref, (rs, own_rows))
    lens = jnp.concatenate([lens] * unit_heads, axis=0)
    query_row = at_row // STEPS
    query_step = lax.rem(at_row, STEPS)
    position = pre * suffix_local + lax.rem(at_col, suffix_local)
    fresh_at = at_col - suffix_rows
    in_suffix = (at_col < suffix_rows) & (at_col // suffix_local == query_row) & (position < lens)
    in_new = (
        (fresh_at >= 0)
        & (fresh_at < rs)
        & (fresh_at // STEPS == query_row)
        & (lax.rem(fresh_at, STEPS) <= query_step)
        & (pre == 0)
    )
    mask = in_suffix | in_new
    stat_lane = iota((rs, LANES), 1)
    transposed = (((1,), (1,)), ((), ()))

    def with_fresh(old, fresh):
        tail = jnp.concatenate([fresh, jnp.zeros((pad, HD), f32)], axis=0) if pad else fresh
        return jnp.concatenate([old.reshape(suffix_rows, HD), tail.astype(bf16)], axis=0)

    def attend(b, finish):
        peaks = jnp.zeros((rs, LANES), f32)
        totals = jnp.ones((rs, LANES), f32)
        for i in range(units):
            first = b * heads_block + i * unit_heads
            kv = pl.ds(pl.multiple_of(first // GROUP * HD, HD), HD)
            pieces = [
                q8[:, pl.ds(pl.multiple_of((first + g) * HD, HD), HD)] for g in range(unit_heads)
            ]
            key_scale = ks8[:, kv]
            value_scale = vs8[:, kv]
            query = jnp.concatenate(pieces, axis=0).astype(bf16)
            scaled = jnp.concatenate([piece * key_scale for piece in pieces], axis=0).astype(bf16)
            own_keys = with_fresh(sk_ref[:, :, kv], fk8[:, kv])
            own_values = with_fresh(sv_ref[:, :, kv], fv8[:, kv])
            prefix_scores = (
                lax.dot_general(scaled, pk_ref[:, kv], transposed, preferred_element_type=f32)
                * score_scale
            )
            own_scores = (
                lax.dot_general(query, own_keys, transposed, preferred_element_type=f32)
                * score_scale
            )
            own_scores = jnp.where(mask, own_scores, masked_score)
            peak = jnp.maximum(
                jnp.max(prefix_scores, axis=1, keepdims=True),
                jnp.max(own_scores, axis=1, keepdims=True),
            )
            prefix_weight = jnp.exp(prefix_scores - peak).astype(bf16)
            own_weight = jnp.where(mask, jnp.exp(own_scores - peak), 0.0).astype(bf16)
            total = jnp.sum(prefix_weight.astype(f32), axis=1, keepdims=True) + jnp.sum(
                own_weight.astype(f32), axis=1, keepdims=True
            )
            numerator = jnp.dot(prefix_weight, pv_ref[:, kv], preferred_element_type=f32)
            numerator = numerator * jnp.concatenate([value_scale] * unit_heads, axis=0)
            numerator = numerator + jnp.dot(own_weight, own_values, preferred_element_type=f32)
            for g in range(unit_heads):
                j = i * unit_heads + g
                part = slice(g * rs, (g + 1) * rs)
                peaks = jnp.where(stat_lane == j, peak[part], peaks)
                totals = jnp.where(stat_lane == j, total[part], totals)
                acc_s[b, :, j * HD : (j + 1) * HD] = numerator[part].astype(bf16)
        stat_s[b, 0] = peaks
        stat_s[b, 1] = totals
        finish()

    for copy in staged[6:]:
        copy.wait()
    for d in list(range(1, pre_n)) + [0]:

        def finish(d=d):
            if d == 1:
                pl.semaphore_wait(barrier, pre_n + row_n - 2 + (split - 1) * row_n)
            if d > 0:
                stat_copy(d).start()
                acc_copy(d).start()

        attend(ahead(d), finish)

    for d in range(1, pre_n):
        stat_copy(d).wait_recv()
    peak_of = [stat_s[pre, 0]] + [stat_r[d - 1, 0] for d in range(1, pre_n)]
    total_of = [stat_s[pre, 1]] + [stat_r[d - 1, 1] for d in range(1, pre_n)]
    highest = functools.reduce(jnp.maximum, peak_of)
    factor_of = [jnp.exp(peak - highest) for peak in peak_of]
    weight_sum = sum(factor * total for factor, total in zip(factor_of, total_of))
    factor_of = [factor / weight_sum for factor in factor_of]
    for d in range(1, pre_n):
        acc_copy(d).wait_recv()
    for j in range(heads_block):
        part = slice(j * HD, (j + 1) * HD)
        value = acc_s[pre, :, part].astype(f32) * factor_of[0][:, j : j + 1]
        for d in range(1, pre_n):
            value = value + acc_r[d - 1, :, part].astype(f32) * factor_of[d][:, j : j + 1]
        mix_g[row, :, part] = value.astype(bf16)
    for d in range(1, row_n):
        mix_copy(d).start()
    for c in range(n_out):
        ow_copy(c).wait()
    for d in range(1, row_n):
        mix_copy(d).wait_recv()
    mix_x[...] = mix_g[...].astype(f32).reshape(everyone, block).astype(bf16)

    def project(c, carry):
        product = jnp.dot(mix_x[...], ow[c], preferred_element_type=f32)
        for p in range(pre_n):
            part = product[p * hs : (p + 1) * hs]
            prod_f[c, p] = part
            prod_s[c, p] = part.astype(bf16)
        for d in range(1, pre_n):
            prod_copy(c, d).start()
        return carry

    lax.fori_loop(0, n_out, project, 0)
    for c in range(n_out):
        part = slice(c * out_width, (c + 1) * out_width)
        value = hid_ref[:, :, part].astype(f32).reshape(hs, out_width) + prod_f[c, pre]
        for d in range(1, pre_n):
            prod_copy(c, d).wait_recv()
            value = value + prod_r[c, d - 1].astype(f32)
        res_g[grp, pre, :, part] = value.astype(bf16)
        res_out[:, :, part] = value.reshape(hid_local, STEPS, out_width).astype(bf16)
    for d in range(1, pre_n):
        res_copy(d).start()
    for e in range(1, split):
        pass_copy(e, 0).start()
    ffs_copy.wait()
    ffn_pick = jnp.where(
        iota((rs, adapters), 1) == per_row(ids_ref, (rs, adapters)), 1.0, 0.0
    ).astype(bf16)
    ffn8[...] = jnp.dot(ffn_pick, ffs[...], preferred_element_type=f32)

    for d in range(1, pre_n):
        res_copy(d).wait_recv()
        for e in range(1, split):
            pass_copy(e, d).start()

    spread_from = iota((LANES, 4 * LANES), 0)
    spread_to = iota((LANES, 4 * LANES), 1)
    spread = jnp.where(
        spread_to
        == jnp.where(spread_to < 2 * LANES, 2 * spread_from, 2 * LANES + 2 * spread_from + 1),
        1.0,
        0.0,
    ).astype(bf16)

    def spread_rows(e, residual):
        normed = (residual * gain_ref[...].astype(f32).reshape(1, depth)).astype(bf16)
        gate_rows = slice(e * everyone, (e + 1) * everyone)
        up_rows = slice((split + e) * everyone, (split + e + 1) * everyone)
        for j in range(depth // LANES):
            part = jnp.dot(
                normed[:, j * LANES : (j + 1) * LANES], spread, preferred_element_type=f32
            ).astype(bf16)
            x_exp[gate_rows, 2 * j * LANES : 2 * (j + 1) * LANES] = part[:, : 2 * LANES]
            x_exp[up_rows, 2 * j * LANES : 2 * (j + 1) * LANES] = part[:, 2 * LANES :]

    residual = res_g[grp].astype(f32).reshape(everyone, depth)
    squares = jnp.sum(residual * residual, axis=1, keepdims=True)
    for r in range(row_n):
        sq_s[r] = jnp.broadcast_to(squares[r * rs : (r + 1) * rs], (rs, LANES))
    for d in range(1, row_n):
        sq_copy(d).start()
    spread_rows(0, residual)
    for e in range(1, split):
        for d in range(pre_n):
            pass_copy(e, d).wait_recv()
    for e in range(1, split):
        spread_rows(e, res_g[across(e)].astype(f32).reshape(everyone, depth))

    tile_step = 2 if tiles_group % 2 == 0 else 1

    def gate_up_group(g, carry):
        for t in range(0, tiles_group, tile_step):
            tiles = [g * tiles_group + t + i for i in range(tile_step)]
            for tile in tiles:
                gu_copy(tile).wait()
            weights = [gu[tile] for tile in tiles]
            weight = jnp.concatenate(weights, axis=1) if tile_step > 1 else weights[0]
            product = jnp.dot(x_exp[...], weight, preferred_element_type=f32)
            part = slice(t * LANES, (t + tile_step) * LANES)
            for e in range(split):
                for r in range(row_n):
                    at = e * everyone + r * rs
                    up_at = split * everyone + at
                    both = jnp.concatenate(
                        [product[at : at + rs], product[up_at : up_at + rs]], axis=0
                    )
                    if e == 0:
                        gate_f[g, r, :, part] = both
                    gate_s[g, e, r, :, part] = both.astype(bf16)
        for e, d in others:
            gate_copy(g, e, d).start()
        return carry

    lax.fori_loop(0, FFN_GROUPS, gate_up_group, 0)

    square_sum = sq_s[row]
    for d in range(1, row_n):
        sq_copy(d).wait_recv()
        square_sum = square_sum + sq_r[d - 1]
    inverse = lax.rsqrt(square_sum[:, :1] / D + 1e-05)

    def activate(g, carry):
        for e in range(split):
            both = gate_f[g, row] if e == 0 else jnp.zeros((2 * rs, group_width), f32)
            for d in range(1 if e == 0 else 0, row_n):
                gate_copy(g, e, d).wait_recv()
                both = both + gate_r[g, e, d].astype(f32)
            gate = both[:rs] * inverse
            up = both[rs:] * inverse
            start = lax.rem(grp + split - e, split) * share + g * group_width
            part = pl.ds(pl.multiple_of(start, LANES), group_width)
            value = gate / (1.0 + jnp.exp(-gate)) * up * ffn8[:, part]
            act_out[:, :, part] = value.reshape(row_local, STEPS, group_width).astype(bf16)
        for e, d in others:
            gate_copy(g, e, d).wait_send()
        return carry

    lax.fori_loop(0, FFN_GROUPS, activate, 0)

    for d in range(1, pre_n):
        stat_copy(d).wait_send()
        acc_copy(d).wait_send()
        res_copy(d).wait_send()
        for c in range(n_out):
            prod_copy(c, d).wait_send()
    for e in range(1, split):
        for d in range(pre_n):
            pass_copy(e, d).wait_send()
    for d in range(1, row_n):
        mix_copy(d).wait_send()
        sq_copy(d).wait_send()


def hand_on(residual_ref, activation_ref, residual_out, activation_out, sem):
    residual = pltpu.make_async_copy(residual_ref, residual_out, sem.at[0])
    activation = pltpu.make_async_copy(activation_ref, activation_out, sem.at[1])
    residual.start()
    activation.start()
    residual.wait()
    activation.wait()


def per_device(
    queries,
    prefix_keys,
    prefix_values,
    suffix_keys,
    suffix_values,
    new_keys,
    new_values,
    hidden,
    adapter_ids,
    suffix_lengths,
    kv_scales,
    ffn_scales,
    out_weight,
    norm_gain,
    gate_up,
):
    pre_n = lax.axis_size("pre")
    row_n = lax.axis_size("row")
    row_local = queries.shape[0]
    rs = row_local * STEPS
    hs = hidden.shape[0] * STEPS
    kv_width = prefix_keys.shape[1]
    adapters, ff = ffn_scales.shape
    block, cols = out_weight.shape
    depth = gate_up.shape[0]
    out_width = min(cols, 512)
    n_out = cols // out_width
    grp_n = lax.axis_size("grp")
    fits = ff % (grp_n * FFN_GROUPS * LANES) == 0
    split = grp_n if fits else 1
    n_tiles = ff // LANES // split
    group_width = ff // split // FFN_GROUPS
    everyone = row_n * rs
    dma = pltpu.SemaphoreType.DMA
    vmem = pl.BlockSpec(memory_space=pltpu.VMEM)
    hbm = pl.BlockSpec(memory_space=pltpu.HBM)
    scratch = [
        pltpu.SMEM(adapter_ids.shape, jnp.int32),
        pltpu.SMEM(suffix_lengths.shape, jnp.int32),
        pltpu.VMEM(queries.shape, bf16),
        pltpu.VMEM(prefix_keys.shape, bf16),
        pltpu.VMEM(prefix_values.shape, bf16),
        pltpu.VMEM(suffix_keys.shape, bf16),
        pltpu.VMEM(suffix_values.shape, bf16),
        pltpu.VMEM(new_keys.shape, bf16),
        pltpu.VMEM(new_values.shape, bf16),
        pltpu.VMEM(hidden.shape, bf16),
        pltpu.VMEM(kv_scales.shape, bf16),
        pltpu.VMEM(norm_gain.shape, bf16),
        pltpu.VMEM((n_out, block, out_width), bf16),
        pltpu.VMEM((n_tiles, 2 * depth, LANES), bf16),
        pltpu.VMEM((adapters, ff), bf16),
        pltpu.VMEM((rs, D), f32),
        pltpu.VMEM((rs, kv_width), f32),
        pltpu.VMEM((rs, kv_width), f32),
        pltpu.VMEM((rs, kv_width), f32),
        pltpu.VMEM((rs, kv_width), f32),
        pltpu.VMEM((pre_n, rs, block), bf16),
        pltpu.VMEM((pre_n - 1, rs, block), bf16),
        pltpu.VMEM((pre_n, 2, rs, LANES), f32),
        pltpu.VMEM((pre_n - 1, 2, rs, LANES), f32),
        pltpu.VMEM((row_n, rs, block), bf16),
        pltpu.VMEM((everyone, block), bf16),
        pltpu.VMEM((n_out, pre_n, hs, out_width), bf16),
        pltpu.VMEM((n_out, pre_n, hs, out_width), f32),
        pltpu.VMEM((n_out, pre_n - 1, hs, out_width), bf16),
        pltpu.VMEM((split, pre_n, hs, cols), bf16),
        pltpu.VMEM((2 * split * everyone, 2 * depth), bf16),
        pltpu.VMEM((FFN_GROUPS, split, row_n, 2 * rs, group_width), bf16),
        pltpu.VMEM((FFN_GROUPS, row_n, 2 * rs, group_width), f32),
        pltpu.VMEM((FFN_GROUPS, split, row_n, 2 * rs, group_width), bf16),
        pltpu.VMEM((row_n, rs, LANES), f32),
        pltpu.VMEM((row_n - 1, rs, LANES), f32),
        pltpu.VMEM((rs, ff), f32),
        dma((12,)),
        dma((n_out,)),
        dma((n_tiles,)),
        dma,
        dma((2, pre_n - 1)),
        dma((2, pre_n - 1)),
        dma((2, row_n - 1)),
        dma((2, n_out, pre_n - 1)),
        dma((2, pre_n - 1)),
        dma((2, max(split - 1, 1), pre_n)),
        dma((2, FFN_GROUPS, split, row_n)),
        dma((2, row_n - 1)),
    ]
    outputs = pl.pallas_call(
        functools.partial(layer_kernel, (pre_n, row_n, split)),
        out_shape=(
            jax.ShapeDtypeStruct(hidden.shape, bf16),
            jax.ShapeDtypeStruct((row_local, STEPS, ff), bf16),
        ),
        in_specs=[hbm] * 15,
        out_specs=(vmem, vmem),
        scratch_shapes=scratch,
        compiler_params=pltpu.CompilerParams(
            collective_id=0, has_side_effects=True, vmem_limit_bytes=GRANT * 1024 * 1024
        ),
    )(
        *(
            pltpu.with_memory_space_constraint(operand, pltpu.HBM)
            for operand in (
                adapter_ids,
                suffix_lengths,
                queries,
                prefix_keys,
                prefix_values,
                suffix_keys,
                suffix_values,
                new_keys,
                new_values,
                hidden,
                kv_scales,
                norm_gain,
                ffn_scales,
                out_weight,
                gate_up,
            )
        )
    )
    return pl.pallas_call(
        hand_on,
        out_shape=tuple(jax.ShapeDtypeStruct(value.shape, value.dtype) for value in outputs),
        in_specs=[vmem, vmem],
        out_specs=(hbm, hbm),
        scratch_shapes=[dma((2,))],
        compiler_params=pltpu.CompilerParams(vmem_limit_bytes=1024 * 1024),
    )(*outputs)


def solution(mesh):
    placed = (
        P(("grp", "row"), None, None),
        P(("grp", "pre"), None),
        P(("grp", "pre"), None),
        P(("grp", "row"), "pre", None),
        P(("grp", "row"), "pre", None),
        P(("grp", "row"), None, None),
        P(("grp", "row"), None, None),
        P(("grp", "pre"), None, "row"),
        P(("grp", "row")),
        P(("grp", "row")),
        P(),
        P(None, "pre"),
        P("pre", "row"),
        P("row"),
        P("row", None, "pre"),
    )
    return jax.shard_map(
        per_device,
        mesh=mesh,
        in_specs=placed,
        out_specs=(P(("grp", "pre"), None, "row"), P(("grp", "row"), None, "pre")),
        check_vma=False,
    )
```

```python
import functools

import jax
import jax.numpy as jnp
from jax import lax
from jax.experimental import pallas as pl
from jax.experimental.pallas import tpu as pltpu
from jax.sharding import PartitionSpec as P

D = 8192
HEADS = 64
KV_HEADS = 8
HD = 128
STEPS = 2
GROUP = HEADS // KV_HEADS
LANES = 128
FFN_GROUPS = 7

GRANT = 40

masked_score = -1e30
f32 = jnp.float32
bf16 = jnp.bfloat16


def iota(shape, axis):
    return lax.broadcasted_iota(jnp.int32, shape, axis)


def layer_kernel(
    sizes,
    ids_hbm,
    lens_hbm,
    q_hbm,
    pk_hbm,
    pv_hbm,
    sk_hbm,
    sv_hbm,
    nk_hbm,
    nv_hbm,
    hid_hbm,
    kvs_hbm,
    gain_hbm,
    ffs_hbm,
    ow_hbm,
    gu_hbm,
    res_out,
    act_out,
    ids_ref,
    lens_ref,
    q_ref,
    pk_ref,
    pv_ref,
    sk_ref,
    sv_ref,
    nk_ref,
    nv_ref,
    hid_ref,
    kvs_ref,
    gain_ref,
    ow,
    gu,
    ffs,
    q8,
    ks8,
    vs8,
    fk8,
    fv8,
    acc_s,
    acc_r,
    stat_s,
    stat_r,
    mix_g,
    mix_x,
    prod_s,
    prod_f,
    prod_r,
    res_g,
    x_exp,
    gate_s,
    gate_f,
    gate_r,
    sq_s,
    sq_r,
    ffn8,
    in_sem,
    ow_sem,
    gu_sem,
    ffs_sem,
    acc_sem,
    stat_sem,
    mix_sem,
    prod_sem,
    res_sem,
    pass_sem,
    gate_sem,
    sq_sem,
):
    pre_n, row_n, split = sizes
    grp = lax.rem(lax.axis_index("grp"), split)
    pre = lax.axis_index("pre")
    row = lax.axis_index("row")
    row_local = q_hbm.shape[0]
    rs = row_local * STEPS
    hid_local = hid_ref.shape[0]
    hs = hid_local * STEPS
    suffix_local = sk_ref.shape[1]
    kv_width = pk_ref.shape[1]
    adapters = kvs_ref.shape[0]
    block = D // pre_n
    heads_block = block // HD
    cols = ow_hbm.shape[1]
    depth = gu_hbm.shape[0]
    ff = gu_hbm.shape[2]
    score_scale = HD ** (-0.5)
    n_out, _, out_width = ow.shape
    n_tiles = gu.shape[0]
    share = n_tiles * LANES
    group_width = gate_s.shape[4]
    tiles_group = n_tiles // FFN_GROUPS
    everyone = row_n * rs

    gu_rows = gu_hbm.reshape(2 * depth, ff)

    def ow_copy(c):
        return pltpu.make_async_copy(
            ow_hbm.at[:, pl.ds(c * out_width, out_width)], ow.at[c], ow_sem
        )

    def gu_copy(c):
        return pltpu.make_async_copy(
            gu_rows.at[:, pl.ds(pl.multiple_of(grp * share + c * LANES, LANES), LANES)], gu.at[c], gu_sem
        )

    staged = [
        (ids_hbm, ids_ref),
        (lens_hbm, lens_ref),
        (kvs_hbm, kvs_ref),
        (q_hbm, q_ref),
        (nk_hbm, nk_ref),
        (nv_hbm, nv_ref),
        (sk_hbm, sk_ref),
        (pk_hbm, pk_ref),
        (sv_hbm, sv_ref),
        (pv_hbm, pv_ref),
        (hid_hbm, hid_ref),
        (gain_hbm, gain_ref),
    ]
    staged = [
        pltpu.make_async_copy(source, target, in_sem.at[i])
        for i, (source, target) in enumerate(staged)
    ]
    for copy in staged:
        copy.start()
    ffs_copy = pltpu.make_async_copy(ffs_hbm, ffs, ffs_sem)

    def landed(ref, sem):
        pltpu.make_async_copy(ref, ref, sem).wait()

    barrier = pltpu.get_barrier_semaphore()
    for d in range(1, pre_n):
        pl.semaphore_signal(
            barrier,
            inc=1,
            device_id={"pre": lax.rem(pre + d, pre_n)},
            device_id_type=pl.DeviceIdType.MESH,
        )
    for d in range(1, row_n):
        pl.semaphore_signal(
            barrier,
            inc=1,
            device_id={"row": lax.rem(row + d, row_n)},
            device_id_type=pl.DeviceIdType.MESH,
        )
    for e in range(1, split):
        for d in range(row_n):
            pl.semaphore_signal(
                barrier,
                inc=1,
                device_id={"grp": lax.rem(grp + e, split), "row": lax.rem(row + d, row_n)},
                device_id_type=pl.DeviceIdType.MESH,
            )

    def remote(src, dst, sems, axis, target, group=None):
        return pltpu.make_async_remote_copy(
            src_ref=src,
            dst_ref=dst,
            send_sem=sems[0],
            recv_sem=sems[1],
            device_id={axis: target} if group is None else {"grp": group, axis: target},
            device_id_type=pl.DeviceIdType.MESH,
        )

    def pair(sem, at=0):
        return sem.at[0], sem.at[1 + at]

    def ahead(d):
        return lax.rem(pre + d, pre_n)

    def beside(d):
        return lax.rem(row + d, row_n)

    def acc_copy(d):
        return remote(acc_s.at[ahead(d)], acc_r.at[d - 1], pair(acc_sem), "pre", ahead(d))

    def stat_copy(d):
        return remote(stat_s.at[ahead(d)], stat_r.at[d - 1], pair(stat_sem), "pre", ahead(d))

    def mix_copy(d):
        return remote(mix_g.at[row], mix_g.at[row], pair(mix_sem), "row", beside(d))

    def prod_copy(c, d):
        return remote(
            prod_s.at[c, ahead(d)], prod_r.at[c, d - 1], pair(prod_sem, c), "pre", ahead(d)
        )

    def res_copy(d):
        block_at = res_g.at[grp, pre]
        return remote(block_at, block_at, pair(res_sem, d - 1), "pre", ahead(d))

    def across(e):
        return lax.rem(grp + e, split)

    def pass_copy(e, d):
        block_at = res_g.at[grp, lax.rem(pre + pre_n - d, pre_n)]
        return remote(block_at, block_at, pair(pass_sem), "grp", across(e))

    def sq_copy(d):
        return remote(sq_s.at[beside(d)], sq_r.at[d - 1], pair(sq_sem), "row", beside(d))

    def gate_copy(g, e, d):
        return remote(
            gate_s.at[g, e, beside(d)],
            gate_r.at[g, e * row_n + d - 1],
            pair(gate_sem, g),
            "row",
            beside(d),
            across(e) if e > 0 else None,
        )

    others = [(e, d) for e in range(split) for d in range(row_n) if e + d > 0]

    def per_row(ref, shape):
        which = iota(shape, 0) // STEPS
        out = jnp.full(shape, ref[0], jnp.int32)
        for r in range(1, row_local):
            out = jnp.where(which == r, ref[r], out)
        return out

    for copy in staged:
        copy.wait()
    for c in range(n_out):
        ow_copy(c).start()
    adapter = per_row(ids_ref, (rs, 2 * adapters))
    lane = iota((rs, 2 * adapters), 1)
    pick_key = jnp.where(lane == 2 * adapter, 1.0, 0.0)
    pick_value = jnp.where(lane == 2 * adapter + 1, 1.0, 0.0)
    pick = jnp.concatenate([pick_key, pick_value], axis=0).astype(bf16)
    scales = jnp.dot(
        pick, kvs_ref[...].reshape(2 * adapters, kv_width), preferred_element_type=f32
    )
    ks8[...] = scales[:rs]
    vs8[...] = scales[rs:]
    fk8[...] = nk_ref[...].astype(f32).reshape(rs, kv_width) * scales[:rs]
    fv8[...] = nv_ref[...].astype(f32).reshape(rs, kv_width) * scales[rs:]
    q8[...] = q_ref[...].astype(f32).reshape(rs, D)

    unit_heads = min(GROUP, heads_block)
    units = heads_block // unit_heads
    unit_rows = unit_heads * rs
    suffix_rows = row_local * suffix_local
    own_rows = -(-(suffix_rows + rs) // LANES) * LANES
    pad = own_rows - suffix_rows - rs
    at_row = lax.rem(iota((unit_rows, own_rows), 0), rs)
    at_col = iota((unit_rows, own_rows), 1)
    lens = per_row(lens_ref, (rs, own_rows))
    lens = jnp.concatenate([lens] * unit_heads, axis=0)
    query_row = at_row // STEPS
    query_step = lax.rem(at_row, STEPS)
    position = pre * suffix_local + lax.rem(at_col, suffix_local)
    fresh_at = at_col - suffix_rows
    in_suffix = (at_col < suffix_rows) & (at_col // suffix_local == query_row) & (position < lens)
    in_new = (
        (fresh_at >= 0)
        & (fresh_at < rs)
        & (fresh_at // STEPS == query_row)
        & (lax.rem(fresh_at, STEPS) <= query_step)
        & (pre == 0)
    )
    mask = in_suffix | in_new
    stat_lane = iota((rs, LANES), 1)
    transposed = (((1,), (1,)), ((), ()))

    def with_fresh(old, fresh):
        tail = jnp.concatenate([fresh, jnp.zeros((pad, HD), f32)], axis=0) if pad else fresh
        return jnp.concatenate([old.reshape(suffix_rows, HD), tail.astype(bf16)], axis=0)

    def attend(b, finish):
        peaks = jnp.zeros((rs, LANES), f32)
        totals = jnp.ones((rs, LANES), f32)
        for i in range(units):
            first = b * heads_block + i * unit_heads
            kv = pl.ds(pl.multiple_of(first // GROUP * HD, HD), HD)
            pieces = [
                q8[:, pl.ds(pl.multiple_of((first + g) * HD, HD), HD)] for g in range(unit_heads)
            ]
            key_scale = ks8[:, kv]
            value_scale = vs8[:, kv]
            query = jnp.concatenate(pieces, axis=0).astype(bf16)
            scaled = jnp.concatenate([piece * key_scale for piece in pieces], axis=0).astype(bf16)
            own_keys = with_fresh(sk_ref[:, :, kv], fk8[:, kv])
            own_values = with_fresh(sv_ref[:, :, kv], fv8[:, kv])
            prefix_scores = (
                lax.dot_general(scaled, pk_ref[:, kv], transposed, preferred_element_type=f32)
                * score_scale
            )
            own_scores = (
                lax.dot_general(query, own_keys, transposed, preferred_element_type=f32)
                * score_scale
            )
            own_scores = jnp.where(mask, own_scores, masked_score)
            peak = jnp.maximum(
                jnp.max(prefix_scores, axis=1, keepdims=True),
                jnp.max(own_scores, axis=1, keepdims=True),
            )
            prefix_weight = jnp.exp(prefix_scores - peak).astype(bf16)
            own_weight = jnp.where(mask, jnp.exp(own_scores - peak), 0.0).astype(bf16)
            total = jnp.sum(prefix_weight.astype(f32), axis=1, keepdims=True) + jnp.sum(
                own_weight.astype(f32), axis=1, keepdims=True
            )
            numerator = jnp.dot(prefix_weight, pv_ref[:, kv], preferred_element_type=f32)
            numerator = numerator * jnp.concatenate([value_scale] * unit_heads, axis=0)
            numerator = numerator + jnp.dot(own_weight, own_values, preferred_element_type=f32)
            for g in range(unit_heads):
                j = i * unit_heads + g
                part = slice(g * rs, (g + 1) * rs)
                peaks = jnp.where(stat_lane == j, peak[part], peaks)
                totals = jnp.where(stat_lane == j, total[part], totals)
                acc_s[b, :, j * HD : (j + 1) * HD] = numerator[part].astype(bf16)
        stat_s[b, 0] = peaks
        stat_s[b, 1] = totals
        finish()

    def farthest(k):
        down = jnp.where(pre_n - 1 - k > pre, pre_n - 1 - k, pre_n - 2 - k)
        up = jnp.where(k < pre, k, k + 1)
        target = jnp.where(2 * pre < pre_n, down, up)
        return lax.rem(target - pre + pre_n, pre_n)

    for k in range(pre_n):

        def finish(k=k):
            if k == 0:
                pl.semaphore_wait(barrier, pre_n + row_n - 2 + (split - 1) * row_n)
            if k < pre_n - 1:
                stat_copy(farthest(k)).start()
                acc_copy(farthest(k)).start()

        attend(ahead(farthest(k)) if k < pre_n - 1 else pre, finish)

    ffs_copy.start()
    for c in range(n_tiles):
        gu_copy(c).start()
    landed(stat_r, stat_sem.at[1])
    peak_of = [stat_s[pre, 0]] + [stat_r[d - 1, 0] for d in range(1, pre_n)]
    total_of = [stat_s[pre, 1]] + [stat_r[d - 1, 1] for d in range(1, pre_n)]
    highest = functools.reduce(jnp.maximum, peak_of)
    factor_of = [jnp.exp(peak - highest) for peak in peak_of]
    weight_sum = sum(factor * total for factor, total in zip(factor_of, total_of))
    factor_of = [factor / weight_sum for factor in factor_of]
    landed(acc_r, acc_sem.at[1])
    for j in range(heads_block):
        part = slice(j * HD, (j + 1) * HD)
        value = acc_s[pre, :, part].astype(f32) * factor_of[0][:, j : j + 1]
        for d in range(1, pre_n):
            value = value + acc_r[d - 1, :, part].astype(f32) * factor_of[d][:, j : j + 1]
        mix_g[row, :, part] = value.astype(bf16)
    for d in range(1, row_n):
        mix_copy(d).start()
    landed(ow, ow_sem)
    landed(mix_g.at[pl.ds(0, row_n - 1)], mix_sem.at[1])
    mix_x[...] = mix_g[...].astype(f32).reshape(everyone, block).astype(bf16)

    def project(c, carry):
        product = jnp.dot(mix_x[...], ow[c], preferred_element_type=f32)
        for p in range(pre_n):
            part = product[p * hs : (p + 1) * hs]
            prod_f[c, p] = part
            prod_s[c, p] = part.astype(bf16)
        for d in range(1, pre_n):
            prod_copy(c, d).start()
        return carry

    lax.fori_loop(0, n_out, project, 0)
    for c in range(n_out):
        part = slice(c * out_width, (c + 1) * out_width)
        value = hid_ref[:, :, part].astype(f32).reshape(hs, out_width) + prod_f[c, pre]
        landed(prod_r.at[c], prod_sem.at[1 + c])
        for d in range(1, pre_n):
            value = value + prod_r[c, d - 1].astype(f32)
        res_g[grp, pre, :, part] = value.astype(bf16)
        res_out[:, :, part] = value.reshape(hid_local, STEPS, out_width).astype(bf16)
    for d in range(1, pre_n):
        res_copy(d).start()
    for e in range(1, split):
        pass_copy(e, 0).start()
    ffs_copy.wait()
    ffn_pick = jnp.where(
        iota((rs, adapters), 1) == per_row(ids_ref, (rs, adapters)), 1.0, 0.0
    ).astype(bf16)
    ffn8[...] = jnp.dot(ffn_pick, ffs[...], preferred_element_type=f32)

    for d in range(1, pre_n):
        res_copy(d).wait_recv()
        for e in range(1, split):
            pass_copy(e, d).start()

    spread_from = iota((LANES, 4 * LANES), 0)
    spread_to = iota((LANES, 4 * LANES), 1)
    spread = jnp.where(
        spread_to
        == jnp.where(spread_to < 2 * LANES, 2 * spread_from, 2 * LANES + 2 * spread_from + 1),
        1.0,
        0.0,
    ).astype(bf16)

    def spread_rows(e, residual):
        normed = (residual * gain_ref[...].astype(f32).reshape(1, depth)).astype(bf16)
        gate_rows = slice(e * everyone, (e + 1) * everyone)
        up_rows = slice((split + e) * everyone, (split + e + 1) * everyone)
        for j in range(depth // LANES):
            part = jnp.dot(
                normed[:, j * LANES : (j + 1) * LANES], spread, preferred_element_type=f32
            ).astype(bf16)
            x_exp[gate_rows, 2 * j * LANES : 2 * (j + 1) * LANES] = part[:, : 2 * LANES]
            x_exp[up_rows, 2 * j * LANES : 2 * (j + 1) * LANES] = part[:, 2 * LANES :]

    residual = res_g[grp].astype(f32).reshape(everyone, depth)
    squares = jnp.sum(residual * residual, axis=1, keepdims=True)
    for r in range(row_n):
        sq_s[r] = jnp.broadcast_to(squares[r * rs : (r + 1) * rs], (rs, LANES))
    for d in range(1, row_n):
        sq_copy(d).start()
    spread_rows(0, residual)
    if split > 1:
        landed(res_g.at[pl.ds(0, split - 1)], pass_sem.at[1])
    for e in range(1, split):
        spread_rows(e, res_g[across(e)].astype(f32).reshape(everyone, depth))

    landed(gu, gu_sem)
    tile_step = 2 if tiles_group % 2 == 0 else 1

    def gate_up_group(g, carry):
        for t in range(0, tiles_group, tile_step):
            tiles = [g * tiles_group + t + i for i in range(tile_step)]
            weights = [gu[tile] for tile in tiles]
            weight = jnp.concatenate(weights, axis=1) if tile_step > 1 else weights[0]
            product = jnp.dot(x_exp[...], weight, preferred_element_type=f32)
            part = slice(t * LANES, (t + tile_step) * LANES)
            for e in range(split):
                for r in range(row_n):
                    at = e * everyone + r * rs
                    up_at = split * everyone + at
                    both = jnp.concatenate(
                        [product[at : at + rs], product[up_at : up_at + rs]], axis=0
                    )
                    if e == 0:
                        gate_f[g, r, :, part] = both
                    gate_s[g, e, r, :, part] = both.astype(bf16)
        for e, d in others:
            gate_copy(g, e, d).start()
        return carry

    lax.fori_loop(0, FFN_GROUPS, gate_up_group, 0)

    square_sum = sq_s[row]
    landed(sq_r, sq_sem.at[1])
    for d in range(1, row_n):
        square_sum = square_sum + sq_r[d - 1]
    inverse = lax.rsqrt(square_sum[:, :1] / D + 1e-05)

    def activate(g, carry):
        landed(gate_r.at[g], gate_sem.at[1 + g])
        for e in range(split):
            both = gate_f[g, row] if e == 0 else jnp.zeros((2 * rs, group_width), f32)
            for d in range(1 if e == 0 else 0, row_n):
                both = both + gate_r[g, e * row_n + d - 1].astype(f32)
            gate = both[:rs] * inverse
            up = both[rs:] * inverse
            start = lax.rem(grp + split - e, split) * share + g * group_width
            part = pl.ds(pl.multiple_of(start, LANES), group_width)
            value = gate / (1.0 + jnp.exp(-gate)) * up * ffn8[:, part]
            act_out[:, :, part] = value.reshape(row_local, STEPS, group_width).astype(bf16)
        return carry

    lax.fori_loop(0, FFN_GROUPS, activate, 0)

    landed(stat_r, stat_sem.at[0])
    landed(acc_r, acc_sem.at[0])
    landed(mix_g.at[pl.ds(0, row_n - 1)], mix_sem.at[0])
    landed(prod_r, prod_sem.at[0])
    landed(res_g.at[0, pl.ds(0, pre_n - 1)], res_sem.at[0])
    if split > 1:
        landed(res_g.at[pl.ds(0, split - 1)], pass_sem.at[0])
    landed(sq_r, sq_sem.at[0])
    landed(gate_r, gate_sem.at[0])


def hand_on(residual_ref, activation_ref, residual_out, activation_out, sem):
    residual = pltpu.make_async_copy(residual_ref, residual_out, sem.at[0])
    activation = pltpu.make_async_copy(activation_ref, activation_out, sem.at[1])
    residual.start()
    activation.start()
    residual.wait()
    activation.wait()


def per_device(
    queries,
    prefix_keys,
    prefix_values,
    suffix_keys,
    suffix_values,
    new_keys,
    new_values,
    hidden,
    adapter_ids,
    suffix_lengths,
    kv_scales,
    ffn_scales,
    out_weight,
    norm_gain,
    gate_up,
):
    pre_n = lax.axis_size("pre")
    row_n = lax.axis_size("row")
    row_local = queries.shape[0]
    rs = row_local * STEPS
    hs = hidden.shape[0] * STEPS
    kv_width = prefix_keys.shape[1]
    adapters, ff = ffn_scales.shape
    block, cols = out_weight.shape
    depth = gate_up.shape[0]
    out_width = min(cols, 512)
    n_out = cols // out_width
    grp_n = lax.axis_size("grp")
    fits = ff % (grp_n * FFN_GROUPS * LANES) == 0
    split = grp_n if fits else 1
    n_tiles = ff // LANES // split
    group_width = ff // split // FFN_GROUPS
    everyone = row_n * rs
    dma = pltpu.SemaphoreType.DMA
    vmem = pl.BlockSpec(memory_space=pltpu.VMEM)
    hbm = pl.BlockSpec(memory_space=pltpu.HBM)
    scratch = [
        pltpu.SMEM(adapter_ids.shape, jnp.int32),
        pltpu.SMEM(suffix_lengths.shape, jnp.int32),
        pltpu.VMEM(queries.shape, bf16),
        pltpu.VMEM(prefix_keys.shape, bf16),
        pltpu.VMEM(prefix_values.shape, bf16),
        pltpu.VMEM(suffix_keys.shape, bf16),
        pltpu.VMEM(suffix_values.shape, bf16),
        pltpu.VMEM(new_keys.shape, bf16),
        pltpu.VMEM(new_values.shape, bf16),
        pltpu.VMEM(hidden.shape, bf16),
        pltpu.VMEM(kv_scales.shape, bf16),
        pltpu.VMEM(norm_gain.shape, bf16),
        pltpu.VMEM((n_out, block, out_width), bf16),
        pltpu.VMEM((n_tiles, 2 * depth, LANES), bf16),
        pltpu.VMEM((adapters, ff), bf16),
        pltpu.VMEM((rs, D), f32),
        pltpu.VMEM((rs, kv_width), f32),
        pltpu.VMEM((rs, kv_width), f32),
        pltpu.VMEM((rs, kv_width), f32),
        pltpu.VMEM((rs, kv_width), f32),
        pltpu.VMEM((pre_n, rs, block), bf16),
        pltpu.VMEM((pre_n - 1, rs, block), bf16),
        pltpu.VMEM((pre_n, 2, rs, LANES), f32),
        pltpu.VMEM((pre_n - 1, 2, rs, LANES), f32),
        pltpu.VMEM((row_n, rs, block), bf16),
        pltpu.VMEM((everyone, block), bf16),
        pltpu.VMEM((n_out, pre_n, hs, out_width), bf16),
        pltpu.VMEM((n_out, pre_n, hs, out_width), f32),
        pltpu.VMEM((n_out, pre_n - 1, hs, out_width), bf16),
        pltpu.VMEM((split, pre_n, hs, cols), bf16),
        pltpu.VMEM((2 * split * everyone, 2 * depth), bf16),
        pltpu.VMEM((FFN_GROUPS, split, row_n, 2 * rs, group_width), bf16),
        pltpu.VMEM((FFN_GROUPS, row_n, 2 * rs, group_width), f32),
        pltpu.VMEM((FFN_GROUPS, split * row_n - 1, 2 * rs, group_width), bf16),
        pltpu.VMEM((row_n, rs, LANES), f32),
        pltpu.VMEM((row_n - 1, rs, LANES), f32),
        pltpu.VMEM((rs, ff), f32),
        dma((12,)),
        dma,
        dma,
        dma,
        dma((2,)),
        dma((2,)),
        dma((2,)),
        dma((1 + n_out,)),
        dma((pre_n,)),
        dma((2,)),
        dma((1 + FFN_GROUPS,)),
        dma((2,)),
    ]
    outputs = pl.pallas_call(
        functools.partial(layer_kernel, (pre_n, row_n, split)),
        out_shape=(
            jax.ShapeDtypeStruct(hidden.shape, bf16),
            jax.ShapeDtypeStruct((row_local, STEPS, ff), bf16),
        ),
        in_specs=[hbm] * 15,
        out_specs=(vmem, vmem),
        scratch_shapes=scratch,
        compiler_params=pltpu.CompilerParams(
            collective_id=0, has_side_effects=True, vmem_limit_bytes=GRANT * 1024 * 1024
        ),
    )(
        *(
            pltpu.with_memory_space_constraint(operand, pltpu.HBM)
            for operand in (
                adapter_ids,
                suffix_lengths,
                queries,
                prefix_keys,
                prefix_values,
                suffix_keys,
                suffix_values,
                new_keys,
                new_values,
                hidden,
                kv_scales,
                norm_gain,
                ffn_scales,
                out_weight,
                gate_up,
            )
        )
    )
    return pl.pallas_call(
        hand_on,
        out_shape=tuple(jax.ShapeDtypeStruct(value.shape, value.dtype) for value in outputs),
        in_specs=[vmem, vmem],
        out_specs=(hbm, hbm),
        scratch_shapes=[dma((2,))],
        compiler_params=pltpu.CompilerParams(vmem_limit_bytes=1024 * 1024),
    )(*outputs)


def solution(mesh):
    placed = (
        P(("grp", "row"), None, None),
        P(("grp", "pre"), None),
        P(("grp", "pre"), None),
        P(("grp", "row"), "pre", None),
        P(("grp", "row"), "pre", None),
        P(("grp", "row"), None, None),
        P(("grp", "row"), None, None),
        P(("grp", "pre"), None, "row"),
        P(("grp", "row")),
        P(("grp", "row")),
        P(),
        P(None, "pre"),
        P("pre", "row"),
        P("row"),
        P("row", None, "pre"),
    )
    return jax.shard_map(
        per_device,
        mesh=mesh,
        in_specs=placed,
        out_specs=(P(("grp", "pre"), None, "row"), P(("grp", "row"), None, "pre")),
        check_vma=False,
    )
```

```python
import functools

import jax
import jax.numpy as jnp
from jax import lax
from jax.experimental import pallas as pl
from jax.experimental.pallas import tpu as pltpu
from jax.sharding import PartitionSpec as P

D = 8192
HEADS = 64
KV_HEADS = 8
HD = 128
STEPS = 2
GROUP = HEADS // KV_HEADS
LANES = 128
OWN_SHARE = 0.4

GRANT = 40

masked_score = -1e30
f32 = jnp.float32
bf16 = jnp.bfloat16


def iota(shape, axis):
    return lax.broadcasted_iota(jnp.int32, shape, axis)


def layer_kernel(
    sizes,
    ids_hbm,
    lens_hbm,
    q_hbm,
    pk_hbm,
    pv_hbm,
    sk_hbm,
    sv_hbm,
    nk_hbm,
    nv_hbm,
    hid_hbm,
    kvs_hbm,
    gain_hbm,
    ffs_hbm,
    ow_hbm,
    gu_hbm,
    res_out,
    act_out,
    ids_ref,
    lens_ref,
    q_ref,
    pk_ref,
    pv_ref,
    sk_ref,
    sv_ref,
    nk_ref,
    nv_ref,
    hid_ref,
    kvs_ref,
    gain_ref,
    ow,
    gu,
    ffs,
    q8,
    ks8,
    vs8,
    fk8,
    fv8,
    acc_s,
    acc_r,
    stat_s,
    stat_r,
    mix_g,
    mix_x,
    prod_s,
    prod_f,
    prod_r,
    res_g,
    x_exp,
    gate_s,
    gate_f,
    gate_r,
    gate_b,
    sq_s,
    sq_r,
    ffn8,
    in_sem,
    ow_sem,
    gu_sem,
    ffs_sem,
    acc_sem,
    stat_sem,
    mix_sem,
    prod_sem,
    res_sem,
    pass_sem,
    gate_sem,
    both_sem,
    sq_sem,
):
    pre_n, row_n, split, own, shared = sizes
    grp = lax.axis_index("grp")
    pre = lax.axis_index("pre")
    row = lax.axis_index("row")
    row_local = q_hbm.shape[0]
    rs = row_local * STEPS
    hid_local = hid_ref.shape[0]
    hs = hid_local * STEPS
    suffix_local = sk_ref.shape[1]
    kv_width = pk_ref.shape[1]
    adapters = kvs_ref.shape[0]
    block = D // pre_n
    heads_block = block // HD
    cols = ow_hbm.shape[1]
    depth = gu_hbm.shape[0]
    ff = gu_hbm.shape[2]
    score_scale = HD ** (-0.5)
    n_out, _, out_width = ow.shape
    n_tiles = gu.shape[0]
    unit = gate_s.shape[3]
    unit_tiles = unit // LANES
    everyone = row_n * rs

    gu_rows = gu_hbm.reshape(2 * depth, ff)

    def ow_copy(c):
        return pltpu.make_async_copy(
            ow_hbm.at[:, pl.ds(c * out_width, out_width)], ow.at[c], ow_sem
        )

    def gu_copy(c):
        return pltpu.make_async_copy(
            gu_rows.at[:, pl.ds(start(c // unit_tiles) + c % unit_tiles * LANES, LANES)],
            gu.at[c],
            gu_sem,
        )

    def start(slot):
        if slot < own:
            return slot * unit
        return pl.multiple_of((own + grp * shared + slot - own) * unit, LANES)

    staged = [
        (ids_hbm, ids_ref),
        (lens_hbm, lens_ref),
        (kvs_hbm, kvs_ref),
        (q_hbm, q_ref),
        (nk_hbm, nk_ref),
        (nv_hbm, nv_ref),
        (sk_hbm, sk_ref),
        (pk_hbm, pk_ref),
        (sv_hbm, sv_ref),
        (pv_hbm, pv_ref),
        (hid_hbm, hid_ref),
        (gain_hbm, gain_ref),
    ]
    staged = [
        pltpu.make_async_copy(source, target, in_sem.at[i])
        for i, (source, target) in enumerate(staged)
    ]
    for copy in staged:
        copy.start()
    ffs_copy = pltpu.make_async_copy(ffs_hbm, ffs, ffs_sem)

    def landed(ref, sem):
        pltpu.make_async_copy(ref, ref, sem).wait()

    barrier = pltpu.get_barrier_semaphore()
    for d in range(1, pre_n):
        pl.semaphore_signal(
            barrier,
            inc=1,
            device_id={"pre": lax.rem(pre + d, pre_n)},
            device_id_type=pl.DeviceIdType.MESH,
        )
    for d in range(1, row_n):
        pl.semaphore_signal(
            barrier,
            inc=1,
            device_id={"row": lax.rem(row + d, row_n)},
            device_id_type=pl.DeviceIdType.MESH,
        )
    for e in range(1, split):
        for d in range(row_n):
            pl.semaphore_signal(
                barrier,
                inc=1,
                device_id={"grp": lax.rem(grp + e, split), "row": lax.rem(row + d, row_n)},
                device_id_type=pl.DeviceIdType.MESH,
            )

    def remote(src, dst, sems, axis, target, group=None):
        return pltpu.make_async_remote_copy(
            src_ref=src,
            dst_ref=dst,
            send_sem=sems[0],
            recv_sem=sems[1],
            device_id={axis: target} if group is None else {"grp": group, axis: target},
            device_id_type=pl.DeviceIdType.MESH,
        )

    def pair(sem, at=0):
        return sem.at[0], sem.at[1 + at]

    def ahead(d):
        return lax.rem(pre + d, pre_n)

    def beside(d):
        return lax.rem(row + d, row_n)

    def acc_copy(d):
        return remote(acc_s.at[ahead(d)], acc_r.at[d - 1], pair(acc_sem), "pre", ahead(d))

    def stat_copy(d):
        return remote(stat_s.at[ahead(d)], stat_r.at[d - 1], pair(stat_sem), "pre", ahead(d))

    def mix_copy(d):
        return remote(mix_g.at[row], mix_g.at[row], pair(mix_sem), "row", beside(d))

    def prod_copy(c, d):
        return remote(
            prod_s.at[c, ahead(d)], prod_r.at[c, d - 1], pair(prod_sem, c), "pre", ahead(d)
        )

    def res_copy(c, d):
        block_at = res_g.at[grp, pre, :, pl.ds(c * out_width, out_width)]
        return remote(block_at, block_at, pair(res_sem, c * (pre_n - 1) + d - 1), "pre", ahead(d))

    def across(e):
        return lax.rem(grp + e, split)

    def pass_copy(c, e, d):
        source = lax.rem(pre + pre_n - d, pre_n)
        block_at = res_g.at[grp, source, :, pl.ds(c * out_width, out_width)]
        return remote(block_at, block_at, pair(pass_sem), "grp", across(e))

    def sq_copy(d):
        return remote(sq_s.at[beside(d)], sq_r.at[d - 1], pair(sq_sem), "row", beside(d))

    def gate_copy(g, d):
        return remote(
            gate_s.at[g, beside(d)], gate_r.at[g, d - 1], pair(gate_sem, g), "row", beside(d)
        )

    def both_copy(i, e, d):
        return remote(
            gate_s.at[own + i * split + e, beside(d)],
            gate_b.at[i, e * row_n + d - 1],
            pair(both_sem, i),
            "row",
            beside(d),
            across(e) if e > 0 else None,
        )

    others = [(e, d) for e in range(split) for d in range(row_n) if e + d > 0]

    def per_row(ref, shape):
        which = iota(shape, 0) // STEPS
        out = jnp.full(shape, ref[0], jnp.int32)
        for r in range(1, row_local):
            out = jnp.where(which == r, ref[r], out)
        return out

    for copy in staged:
        copy.wait()
    for c in range(n_out):
        ow_copy(c).start()
    adapter = per_row(ids_ref, (rs, 2 * adapters))
    lane = iota((rs, 2 * adapters), 1)
    pick_key = jnp.where(lane == 2 * adapter, 1.0, 0.0)
    pick_value = jnp.where(lane == 2 * adapter + 1, 1.0, 0.0)
    pick = jnp.concatenate([pick_key, pick_value], axis=0).astype(bf16)
    scales = jnp.dot(
        pick, kvs_ref[...].reshape(2 * adapters, kv_width), preferred_element_type=f32
    )
    ks8[...] = scales[:rs]
    vs8[...] = scales[rs:]
    fk8[...] = nk_ref[...].astype(f32).reshape(rs, kv_width) * scales[:rs]
    fv8[...] = nv_ref[...].astype(f32).reshape(rs, kv_width) * scales[rs:]
    q8[...] = q_ref[...].astype(f32).reshape(rs, D)

    unit_heads = min(GROUP, heads_block)
    units = heads_block // unit_heads
    unit_rows = unit_heads * rs
    suffix_rows = row_local * suffix_local
    own_rows = -(-(suffix_rows + rs) // LANES) * LANES
    pad = own_rows - suffix_rows - rs
    at_row = lax.rem(iota((unit_rows, own_rows), 0), rs)
    at_col = iota((unit_rows, own_rows), 1)
    lens = per_row(lens_ref, (rs, own_rows))
    lens = jnp.concatenate([lens] * unit_heads, axis=0)
    query_row = at_row // STEPS
    query_step = lax.rem(at_row, STEPS)
    position = pre * suffix_local + lax.rem(at_col, suffix_local)
    fresh_at = at_col - suffix_rows
    in_suffix = (at_col < suffix_rows) & (at_col // suffix_local == query_row) & (position < lens)
    in_new = (
        (fresh_at >= 0)
        & (fresh_at < rs)
        & (fresh_at // STEPS == query_row)
        & (lax.rem(fresh_at, STEPS) <= query_step)
        & (pre == 0)
    )
    mask = in_suffix | in_new
    stat_lane = iota((rs, LANES), 1)
    transposed = (((1,), (1,)), ((), ()))

    def with_fresh(old, fresh):
        tail = jnp.concatenate([fresh, jnp.zeros((pad, HD), f32)], axis=0) if pad else fresh
        return jnp.concatenate([old.reshape(suffix_rows, HD), tail.astype(bf16)], axis=0)

    def attend(b, finish):
        peaks = jnp.zeros((rs, LANES), f32)
        totals = jnp.ones((rs, LANES), f32)
        for i in range(units):
            first = b * heads_block + i * unit_heads
            kv = pl.ds(pl.multiple_of(first // GROUP * HD, HD), HD)
            pieces = [
                q8[:, pl.ds(pl.multiple_of((first + g) * HD, HD), HD)] for g in range(unit_heads)
            ]
            key_scale = ks8[:, kv]
            value_scale = vs8[:, kv]
            query = jnp.concatenate(pieces, axis=0).astype(bf16)
            scaled = jnp.concatenate([piece * key_scale for piece in pieces], axis=0).astype(bf16)
            own_keys = with_fresh(sk_ref[:, :, kv], fk8[:, kv])
            own_values = with_fresh(sv_ref[:, :, kv], fv8[:, kv])
            prefix_scores = (
                lax.dot_general(scaled, pk_ref[:, kv], transposed, preferred_element_type=f32)
                * score_scale
            )
            own_scores = (
                lax.dot_general(query, own_keys, transposed, preferred_element_type=f32)
                * score_scale
            )
            own_scores = jnp.where(mask, own_scores, masked_score)
            peak = jnp.maximum(
                jnp.max(prefix_scores, axis=1, keepdims=True),
                jnp.max(own_scores, axis=1, keepdims=True),
            )
            prefix_weight = jnp.exp(prefix_scores - peak).astype(bf16)
            own_weight = jnp.where(mask, jnp.exp(own_scores - peak), 0.0).astype(bf16)
            total = jnp.sum(prefix_weight.astype(f32), axis=1, keepdims=True) + jnp.sum(
                own_weight.astype(f32), axis=1, keepdims=True
            )
            numerator = jnp.dot(prefix_weight, pv_ref[:, kv], preferred_element_type=f32)
            numerator = numerator * jnp.concatenate([value_scale] * unit_heads, axis=0)
            numerator = numerator + jnp.dot(own_weight, own_values, preferred_element_type=f32)
            for g in range(unit_heads):
                j = i * unit_heads + g
                part = slice(g * rs, (g + 1) * rs)
                peaks = jnp.where(stat_lane == j, peak[part], peaks)
                totals = jnp.where(stat_lane == j, total[part], totals)
                acc_s[b, :, j * HD : (j + 1) * HD] = numerator[part].astype(bf16)
        stat_s[b, 0] = peaks
        stat_s[b, 1] = totals
        finish()

    def farthest(k):
        down = jnp.where(pre_n - 1 - k > pre, pre_n - 1 - k, pre_n - 2 - k)
        up = jnp.where(k < pre, k, k + 1)
        target = jnp.where(2 * pre < pre_n, down, up)
        return lax.rem(target - pre + pre_n, pre_n)

    for k in range(pre_n):

        def finish(k=k):
            if k == 0:
                pl.semaphore_wait(barrier, pre_n + row_n - 2 + (split - 1) * row_n)
            if k < pre_n - 1:
                stat_copy(farthest(k)).start()
                acc_copy(farthest(k)).start()

        attend(ahead(farthest(k)) if k < pre_n - 1 else pre, finish)

    ffs_copy.start()
    for c in range(n_tiles):
        gu_copy(c).start()
    landed(stat_r, stat_sem.at[1])
    peak_of = [stat_s[pre, 0]] + [stat_r[d - 1, 0] for d in range(1, pre_n)]
    total_of = [stat_s[pre, 1]] + [stat_r[d - 1, 1] for d in range(1, pre_n)]
    highest = functools.reduce(jnp.maximum, peak_of)
    factor_of = [jnp.exp(peak - highest) for peak in peak_of]
    weight_sum = sum(factor * total for factor, total in zip(factor_of, total_of))
    factor_of = [factor / weight_sum for factor in factor_of]
    landed(acc_r, acc_sem.at[1])
    for j in range(heads_block):
        part = slice(j * HD, (j + 1) * HD)
        value = acc_s[pre, :, part].astype(f32) * factor_of[0][:, j : j + 1]
        for d in range(1, pre_n):
            value = value + acc_r[d - 1, :, part].astype(f32) * factor_of[d][:, j : j + 1]
        mix_g[row, :, part] = value.astype(bf16)
    for d in range(1, row_n):
        mix_copy(d).start()
    landed(ow, ow_sem)
    landed(mix_g.at[pl.ds(0, row_n - 1)], mix_sem.at[1])
    mix_x[...] = mix_g[...].astype(f32).reshape(everyone, block).astype(bf16)

    def project(c, carry):
        product = jnp.dot(mix_x[...], ow[c], preferred_element_type=f32)
        for p in range(pre_n):
            part = product[p * hs : (p + 1) * hs]
            prod_f[c, p] = part
            prod_s[c, p] = part.astype(bf16)
        for d in range(1, pre_n):
            prod_copy(c, d).start()
        return carry

    lax.fori_loop(0, n_out, project, 0)
    for c in range(n_out):
        part = slice(c * out_width, (c + 1) * out_width)
        value = hid_ref[:, :, part].astype(f32).reshape(hs, out_width) + prod_f[c, pre]
        landed(prod_r.at[c], prod_sem.at[1 + c])
        for d in range(1, pre_n):
            value = value + prod_r[c, d - 1].astype(f32)
        res_g[grp, pre, :, part] = value.astype(bf16)
        for d in range(1, pre_n):
            res_copy(c, d).start()
        for e in range(1, split):
            pass_copy(c, e, 0).start()
        res_out[:, :, part] = value.reshape(hid_local, STEPS, out_width).astype(bf16)
    ffs_copy.wait()
    ffn_pick = jnp.where(
        iota((rs, adapters), 1) == per_row(ids_ref, (rs, adapters)), 1.0, 0.0
    ).astype(bf16)
    ffn8[...] = jnp.dot(ffn_pick, ffs[...], preferred_element_type=f32)

    for c in range(n_out):
        for d in range(1, pre_n):
            res_copy(c, d).wait_recv()
            for e in range(1, split):
                pass_copy(c, e, d).start()

    spread_from = iota((LANES, 4 * LANES), 0)
    spread_to = iota((LANES, 4 * LANES), 1)
    spread = jnp.where(
        spread_to
        == jnp.where(spread_to < 2 * LANES, 2 * spread_from, 2 * LANES + 2 * spread_from + 1),
        1.0,
        0.0,
    ).astype(bf16)

    def spread_rows(e, residual):
        normed = (residual * gain_ref[...].astype(f32).reshape(1, depth)).astype(bf16)
        first = 2 * e * everyone
        gate_rows = slice(first, first + everyone)
        up_rows = slice(first + everyone, first + 2 * everyone)
        blocks = depth // LANES
        batch = min(blocks, 4)
        for j in range(0, blocks, batch):
            stacked = jnp.concatenate(
                [normed[:, k * LANES : (k + 1) * LANES] for k in range(j, j + batch)], axis=0
            )
            parts = jnp.dot(stacked, spread, preferred_element_type=f32).astype(bf16)
            for k in range(batch):
                part = parts[k * everyone : (k + 1) * everyone]
                at = slice(2 * (j + k) * LANES, 2 * (j + k + 1) * LANES)
                x_exp[gate_rows, at] = part[:, : 2 * LANES]
                x_exp[up_rows, at] = part[:, 2 * LANES :]

    residual = res_g[grp].astype(f32).reshape(everyone, depth)
    squares = jnp.sum(residual * residual, axis=1, keepdims=True)
    for r in range(row_n):
        sq_s[r] = jnp.broadcast_to(squares[r * rs : (r + 1) * rs], (rs, LANES))
    for d in range(1, row_n):
        sq_copy(d).start()
    spread_rows(0, residual)
    def unit_product(g, rows):
        weights = [gu[g * unit_tiles + t] for t in range(unit_tiles)]
        weight = jnp.concatenate(weights, axis=1) if unit_tiles > 1 else weights[0]
        return jnp.dot(x_exp[:rows], weight, preferred_element_type=f32)

    def gate_and_up(product, e, r):
        at = 2 * e * everyone + r * rs
        up_at = at + everyone
        return jnp.concatenate([product[at : at + rs], product[up_at : up_at + rs]], axis=0)

    def own_unit(g, carry):
        product = unit_product(g, 2 * everyone)
        for r in range(row_n):
            both = gate_and_up(product, 0, r)
            gate_f[g, r] = both
            gate_s[g, r] = both.astype(bf16)
        for d in range(1, row_n):
            gate_copy(g, d).start()
        return carry

    def shared_unit(i, carry):
        product = unit_product(own + i, 2 * split * everyone)
        for e in range(split):
            for r in range(row_n):
                both = gate_and_up(product, e, r)
                if e == 0:
                    gate_f[own + i, r] = both
                gate_s[own + i * split + e, r] = both.astype(bf16)
        for e, d in others:
            both_copy(i, e, d).start()
        return carry

    landed(gu, gu_sem)
    lax.fori_loop(0, own, own_unit, 0)
    if split > 1:
        landed(res_g.at[pl.ds(0, split - 1)], pass_sem.at[1])
    for e in range(1, split):
        spread_rows(e, res_g[across(e)].astype(f32).reshape(everyone, depth))
    lax.fori_loop(0, shared, shared_unit, 0)

    square_sum = sq_s[row]
    landed(sq_r, sq_sem.at[1])
    for d in range(1, row_n):
        square_sum = square_sum + sq_r[d - 1]
    inverse = lax.rsqrt(square_sum[:, :1] / D + 1e-05)

    def activate(both, at):
        gate = both[:rs] * inverse
        up = both[rs:] * inverse
        part = pl.ds(pl.multiple_of(at, LANES), unit)
        value = gate / (1.0 + jnp.exp(-gate)) * up * ffn8[:, part]
        act_out[:, :, part] = value.reshape(row_local, STEPS, unit).astype(bf16)

    def finish_own(g, carry):
        landed(gate_r.at[g], gate_sem.at[1 + g])
        both = gate_f[g, row]
        for d in range(1, row_n):
            both = both + gate_r[g, d - 1].astype(f32)
        activate(both, g * unit)
        return carry

    def finish_shared(i, carry):
        landed(gate_b.at[i], both_sem.at[1 + i])
        for e in range(split):
            both = gate_f[own + i, row] if e == 0 else jnp.zeros((2 * rs, unit), f32)
            for d in range(1 if e == 0 else 0, row_n):
                both = both + gate_b[i, e * row_n + d - 1].astype(f32)
            owner = lax.rem(grp + split - e, split)
            activate(both, (own + owner * shared + i) * unit)
        return carry

    lax.fori_loop(0, own, finish_own, 0)
    lax.fori_loop(0, shared, finish_shared, 0)

    landed(stat_r, stat_sem.at[0])
    landed(acc_r, acc_sem.at[0])
    landed(mix_g.at[pl.ds(0, row_n - 1)], mix_sem.at[0])
    landed(prod_r, prod_sem.at[0])
    landed(res_g.at[0, pl.ds(0, pre_n - 1)], res_sem.at[0])
    if split > 1:
        landed(res_g.at[pl.ds(0, split - 1)], pass_sem.at[0])
    landed(sq_r, sq_sem.at[0])
    landed(gate_r, gate_sem.at[0])
    landed(gate_b, both_sem.at[0])


def hand_on(residual_ref, activation_ref, residual_out, activation_out, sem):
    residual = pltpu.make_async_copy(residual_ref, residual_out, sem.at[0])
    activation = pltpu.make_async_copy(activation_ref, activation_out, sem.at[1])
    residual.start()
    activation.start()
    residual.wait()
    activation.wait()


def per_device(
    queries,
    prefix_keys,
    prefix_values,
    suffix_keys,
    suffix_values,
    new_keys,
    new_values,
    hidden,
    adapter_ids,
    suffix_lengths,
    kv_scales,
    ffn_scales,
    out_weight,
    norm_gain,
    gate_up,
):
    pre_n = lax.axis_size("pre")
    row_n = lax.axis_size("row")
    row_local = queries.shape[0]
    rs = row_local * STEPS
    hs = hidden.shape[0] * STEPS
    kv_width = prefix_keys.shape[1]
    adapters, ff = ffn_scales.shape
    block, cols = out_weight.shape
    depth = gate_up.shape[0]
    out_width = min(cols, 512)
    n_out = cols // out_width
    split = lax.axis_size("grp")
    unit = 2 * LANES if ff % (2 * LANES) == 0 else LANES
    units = ff // unit
    shared = int(units * (1 - OWN_SHARE)) // split
    own = units - shared * split
    n_tiles = (own + shared) * unit // LANES
    everyone = row_n * rs
    dma = pltpu.SemaphoreType.DMA
    vmem = pl.BlockSpec(memory_space=pltpu.VMEM)
    hbm = pl.BlockSpec(memory_space=pltpu.HBM)
    scratch = [
        pltpu.SMEM(adapter_ids.shape, jnp.int32),
        pltpu.SMEM(suffix_lengths.shape, jnp.int32),
        pltpu.VMEM(queries.shape, bf16),
        pltpu.VMEM(prefix_keys.shape, bf16),
        pltpu.VMEM(prefix_values.shape, bf16),
        pltpu.VMEM(suffix_keys.shape, bf16),
        pltpu.VMEM(suffix_values.shape, bf16),
        pltpu.VMEM(new_keys.shape, bf16),
        pltpu.VMEM(new_values.shape, bf16),
        pltpu.VMEM(hidden.shape, bf16),
        pltpu.VMEM(kv_scales.shape, bf16),
        pltpu.VMEM(norm_gain.shape, bf16),
        pltpu.VMEM((n_out, block, out_width), bf16),
        pltpu.VMEM((n_tiles, 2 * depth, LANES), bf16),
        pltpu.VMEM((adapters, ff), bf16),
        pltpu.VMEM((rs, D), f32),
        pltpu.VMEM((rs, kv_width), f32),
        pltpu.VMEM((rs, kv_width), f32),
        pltpu.VMEM((rs, kv_width), f32),
        pltpu.VMEM((rs, kv_width), f32),
        pltpu.VMEM((pre_n, rs, block), bf16),
        pltpu.VMEM((pre_n - 1, rs, block), bf16),
        pltpu.VMEM((pre_n, 2, rs, LANES), f32),
        pltpu.VMEM((pre_n - 1, 2, rs, LANES), f32),
        pltpu.VMEM((row_n, rs, block), bf16),
        pltpu.VMEM((everyone, block), bf16),
        pltpu.VMEM((n_out, pre_n, hs, out_width), bf16),
        pltpu.VMEM((n_out, pre_n, hs, out_width), f32),
        pltpu.VMEM((n_out, pre_n - 1, hs, out_width), bf16),
        pltpu.VMEM((split, pre_n, hs, cols), bf16),
        pltpu.VMEM((2 * split * everyone, 2 * depth), bf16),
        pltpu.VMEM((own + shared * split, row_n, 2 * rs, unit), bf16),
        pltpu.VMEM((own + shared, row_n, 2 * rs, unit), f32),
        pltpu.VMEM((own, row_n - 1, 2 * rs, unit), bf16),
        pltpu.VMEM((shared, split * row_n - 1, 2 * rs, unit), bf16),
        pltpu.VMEM((row_n, rs, LANES), f32),
        pltpu.VMEM((row_n - 1, rs, LANES), f32),
        pltpu.VMEM((rs, ff), f32),
        dma((12,)),
        dma,
        dma,
        dma,
        dma((2,)),
        dma((2,)),
        dma((2,)),
        dma((1 + n_out,)),
        dma((1 + n_out * (pre_n - 1),)),
        dma((2,)),
        dma((1 + own,)),
        dma((1 + shared,)),
        dma((2,)),
    ]
    outputs = pl.pallas_call(
        functools.partial(layer_kernel, (pre_n, row_n, split, own, shared)),
        out_shape=(
            jax.ShapeDtypeStruct(hidden.shape, bf16),
            jax.ShapeDtypeStruct((row_local, STEPS, ff), bf16),
        ),
        in_specs=[hbm] * 15,
        out_specs=(vmem, vmem),
        scratch_shapes=scratch,
        compiler_params=pltpu.CompilerParams(
            collective_id=0, has_side_effects=True, vmem_limit_bytes=GRANT * 1024 * 1024
        ),
    )(
        *(
            pltpu.with_memory_space_constraint(operand, pltpu.HBM)
            for operand in (
                adapter_ids,
                suffix_lengths,
                queries,
                prefix_keys,
                prefix_values,
                suffix_keys,
                suffix_values,
                new_keys,
                new_values,
                hidden,
                kv_scales,
                norm_gain,
                ffn_scales,
                out_weight,
                gate_up,
            )
        )
    )
    return pl.pallas_call(
        hand_on,
        out_shape=tuple(jax.ShapeDtypeStruct(value.shape, value.dtype) for value in outputs),
        in_specs=[vmem, vmem],
        out_specs=(hbm, hbm),
        scratch_shapes=[dma((2,))],
        compiler_params=pltpu.CompilerParams(vmem_limit_bytes=1024 * 1024),
    )(*outputs)


def solution(mesh):
    placed = (
        P(("grp", "row"), None, None),
        P(("grp", "pre"), None),
        P(("grp", "pre"), None),
        P(("grp", "row"), "pre", None),
        P(("grp", "row"), "pre", None),
        P(("grp", "row"), None, None),
        P(("grp", "row"), None, None),
        P(("grp", "pre"), None, "row"),
        P(("grp", "row")),
        P(("grp", "row")),
        P(),
        P(None, "pre"),
        P("pre", "row"),
        P("row"),
        P("row", None, "pre"),
    )
    return jax.shard_map(
        per_device,
        mesh=mesh,
        in_specs=placed,
        out_specs=(P(("grp", "pre"), None, "row"), P(("grp", "row"), None, "pre")),
        check_vma=False,
    )
```

```python
import functools

import jax
import jax.numpy as jnp
from jax import lax
from jax.experimental import pallas as pl
from jax.experimental.pallas import tpu as pltpu
from jax.sharding import PartitionSpec as P

D = 8192
HEADS = 64
KV_HEADS = 8
HD = 128
STEPS = 2
GROUP = HEADS // KV_HEADS
LANES = 128
OWN_SHARE = 0.4

GRANT = 40

masked_score = -1e30
f32 = jnp.float32
bf16 = jnp.bfloat16


def iota(shape, axis):
    return lax.broadcasted_iota(jnp.int32, shape, axis)


def layer_kernel(
    sizes,
    ids_hbm,
    lens_hbm,
    q_hbm,
    pk_hbm,
    pv_hbm,
    sk_hbm,
    sv_hbm,
    nk_hbm,
    nv_hbm,
    hid_hbm,
    kvs_hbm,
    gain_hbm,
    ffs_hbm,
    ow_hbm,
    gu_hbm,
    res_out,
    act_out,
    ids_ref,
    lens_ref,
    q_ref,
    pk_ref,
    pv_ref,
    sk_ref,
    sv_ref,
    nk_ref,
    nv_ref,
    hid_ref,
    kvs_ref,
    gain_ref,
    ow,
    gu,
    ffs,
    q8,
    ks8,
    vs8,
    fk8,
    fv8,
    acc_s,
    acc_r,
    stat_s,
    stat_r,
    mix_g,
    mix_x,
    prod_s,
    prod_f,
    prod_r,
    res_g,
    x_exp,
    gate_s,
    gate_f,
    gate_r,
    gate_b,
    sq_s,
    sq_r,
    ffn8,
    in_sem,
    ow_sem,
    gu_sem,
    ffs_sem,
    acc_sem,
    stat_sem,
    mix_sem,
    prod_sem,
    res_sem,
    pass_sem,
    gate_sem,
    both_sem,
    sq_sem,
):
    pre_n, row_n, split, own, shared = sizes
    grp = lax.axis_index("grp")
    pre = lax.axis_index("pre")
    row = lax.axis_index("row")
    row_local = q_hbm.shape[0]
    rs = row_local * STEPS
    hid_local = hid_ref.shape[0]
    hs = hid_local * STEPS
    suffix_local = sk_ref.shape[1]
    kv_width = pk_ref.shape[1]
    adapters = kvs_ref.shape[0]
    block = D // pre_n
    heads_block = block // HD
    cols = ow_hbm.shape[1]
    depth = gu_hbm.shape[0]
    ff = gu_hbm.shape[2]
    score_scale = HD ** (-0.5)
    n_out, _, out_width = ow.shape
    n_tiles = gu.shape[0]
    unit = gate_s.shape[3]
    unit_tiles = unit // LANES
    everyone = row_n * rs

    gu_rows = gu_hbm.reshape(2 * depth, ff)

    def ow_copy(c):
        return pltpu.make_async_copy(
            ow_hbm.at[:, pl.ds(c * out_width, out_width)], ow.at[c], ow_sem
        )

    def gu_copy(c):
        return pltpu.make_async_copy(
            gu_rows.at[:, pl.ds(start(c // unit_tiles) + c % unit_tiles * LANES, LANES)],
            gu.at[c],
            gu_sem,
        )

    def start(slot):
        if slot < own:
            return slot * unit
        return pl.multiple_of((own + grp * shared + slot - own) * unit, LANES)

    staged = [
        (ids_hbm, ids_ref),
        (lens_hbm, lens_ref),
        (kvs_hbm, kvs_ref),
        (q_hbm, q_ref),
        (nk_hbm, nk_ref),
        (nv_hbm, nv_ref),
        (sk_hbm, sk_ref),
        (pk_hbm, pk_ref),
        (sv_hbm, sv_ref),
        (pv_hbm, pv_ref),
        (hid_hbm, hid_ref),
        (gain_hbm, gain_ref),
    ]
    staged = [
        pltpu.make_async_copy(source, target, in_sem.at[i])
        for i, (source, target) in enumerate(staged)
    ]
    for copy in staged:
        copy.start()
    ffs_copy = pltpu.make_async_copy(ffs_hbm, ffs, ffs_sem)

    def landed(ref, sem):
        pltpu.make_async_copy(ref, ref, sem).wait()

    barrier = pltpu.get_barrier_semaphore()
    for d in range(1, pre_n):
        pl.semaphore_signal(
            barrier,
            inc=1,
            device_id={"pre": lax.rem(pre + d, pre_n)},
            device_id_type=pl.DeviceIdType.MESH,
        )
    for d in range(1, row_n):
        pl.semaphore_signal(
            barrier,
            inc=1,
            device_id={"row": lax.rem(row + d, row_n)},
            device_id_type=pl.DeviceIdType.MESH,
        )
    for e in range(1, split):
        for d in range(row_n):
            pl.semaphore_signal(
                barrier,
                inc=1,
                device_id={"grp": lax.rem(grp + e, split), "row": lax.rem(row + d, row_n)},
                device_id_type=pl.DeviceIdType.MESH,
            )

    def remote(src, dst, sems, axis, target, group=None):
        return pltpu.make_async_remote_copy(
            src_ref=src,
            dst_ref=dst,
            send_sem=sems[0],
            recv_sem=sems[1],
            device_id={axis: target} if group is None else {"grp": group, axis: target},
            device_id_type=pl.DeviceIdType.MESH,
        )

    def pair(sem, at=0):
        return sem.at[0], sem.at[1 + at]

    def ahead(d):
        return lax.rem(pre + d, pre_n)

    def beside(d):
        return lax.rem(row + d, row_n)

    def acc_copy(d):
        return remote(acc_s.at[ahead(d)], acc_r.at[d - 1], pair(acc_sem), "pre", ahead(d))

    def stat_copy(d):
        return remote(stat_s.at[ahead(d)], stat_r.at[d - 1], pair(stat_sem), "pre", ahead(d))

    def mix_copy(d):
        return remote(mix_g.at[row], mix_g.at[row], pair(mix_sem), "row", beside(d))

    def prod_copy(c, d):
        return remote(
            prod_s.at[c, ahead(d)], prod_r.at[c, d - 1], pair(prod_sem, c), "pre", ahead(d)
        )

    def res_copy(c, d):
        block_at = res_g.at[grp, pre, :, pl.ds(c * out_width, out_width)]
        return remote(block_at, block_at, pair(res_sem, c * (pre_n - 1) + d - 1), "pre", ahead(d))

    def across(e):
        return lax.rem(grp + e, split)

    def pass_copy(c, e, d):
        source = lax.rem(pre + pre_n - d, pre_n)
        block_at = res_g.at[grp, source, :, pl.ds(c * out_width, out_width)]
        return remote(block_at, block_at, pair(pass_sem), "grp", across(e))

    def sq_copy(d):
        return remote(sq_s.at[beside(d)], sq_r.at[d - 1], pair(sq_sem), "row", beside(d))

    def gate_copy(g, d):
        return remote(
            gate_s.at[g, beside(d)], gate_r.at[g, d - 1], pair(gate_sem, g), "row", beside(d)
        )

    def both_copy(i, e, d):
        return remote(
            gate_s.at[own + i * split + e, beside(d)],
            gate_b.at[i, e * row_n + d - 1],
            pair(both_sem, i),
            "row",
            beside(d),
            across(e) if e > 0 else None,
        )

    others = [(e, d) for e in range(split) for d in range(row_n) if e + d > 0]

    def per_row(ref, shape):
        which = iota(shape, 0) // STEPS
        out = jnp.full(shape, ref[0], jnp.int32)
        for r in range(1, row_local):
            out = jnp.where(which == r, ref[r], out)
        return out

    for copy in staged:
        copy.wait()
    for c in range(n_out):
        ow_copy(c).start()
    adapter = per_row(ids_ref, (rs, 2 * adapters))
    lane = iota((rs, 2 * adapters), 1)
    pick_key = jnp.where(lane == 2 * adapter, 1.0, 0.0)
    pick_value = jnp.where(lane == 2 * adapter + 1, 1.0, 0.0)
    pick = jnp.concatenate([pick_key, pick_value], axis=0).astype(bf16)
    scales = jnp.dot(
        pick, kvs_ref[...].reshape(2 * adapters, kv_width), preferred_element_type=f32
    )
    ks8[...] = scales[:rs]
    vs8[...] = scales[rs:]
    fk8[...] = nk_ref[...].astype(f32).reshape(rs, kv_width) * scales[:rs]
    fv8[...] = nv_ref[...].astype(f32).reshape(rs, kv_width) * scales[rs:]
    q8[...] = q_ref[...].astype(f32).reshape(rs, D)

    unit_heads = min(GROUP, heads_block)
    units = heads_block // unit_heads
    unit_rows = unit_heads * rs
    suffix_rows = row_local * suffix_local
    own_rows = -(-(suffix_rows + rs) // LANES) * LANES
    pad = own_rows - suffix_rows - rs
    at_row = lax.rem(iota((unit_rows, own_rows), 0), rs)
    at_col = iota((unit_rows, own_rows), 1)
    lens = per_row(lens_ref, (rs, own_rows))
    lens = jnp.concatenate([lens] * unit_heads, axis=0)
    query_row = at_row // STEPS
    query_step = lax.rem(at_row, STEPS)
    position = pre * suffix_local + lax.rem(at_col, suffix_local)
    fresh_at = at_col - suffix_rows
    in_suffix = (at_col < suffix_rows) & (at_col // suffix_local == query_row) & (position < lens)
    in_new = (
        (fresh_at >= 0)
        & (fresh_at < rs)
        & (fresh_at // STEPS == query_row)
        & (lax.rem(fresh_at, STEPS) <= query_step)
        & (pre == 0)
    )
    mask = in_suffix | in_new
    stat_lane = iota((rs, LANES), 1)
    transposed = (((1,), (1,)), ((), ()))

    def with_fresh(old, fresh):
        tail = jnp.concatenate([fresh, jnp.zeros((pad, HD), f32)], axis=0) if pad else fresh
        return jnp.concatenate([old.reshape(suffix_rows, HD), tail.astype(bf16)], axis=0)

    def scores_of(first):
        kv = pl.ds(pl.multiple_of(first // GROUP * HD, HD), HD)
        pieces = [
            q8[:, pl.ds(pl.multiple_of((first + g) * HD, HD), HD)] for g in range(unit_heads)
        ]
        key_scale = ks8[:, kv]
        query = jnp.concatenate(pieces, axis=0).astype(bf16)
        scaled = jnp.concatenate([piece * key_scale for piece in pieces], axis=0).astype(bf16)
        own_keys = with_fresh(sk_ref[:, :, kv], fk8[:, kv])
        prefix_scores = lax.dot_general(
            scaled, pk_ref[:, kv], transposed, preferred_element_type=f32
        )
        own_scores = lax.dot_general(query, own_keys, transposed, preferred_element_type=f32)
        return prefix_scores, own_scores

    def weights_of(prefix_scores, own_scores):
        prefix_scores = prefix_scores * score_scale
        own_scores = jnp.where(mask, own_scores * score_scale, masked_score)
        peak = jnp.maximum(
            jnp.max(prefix_scores, axis=1, keepdims=True),
            jnp.max(own_scores, axis=1, keepdims=True),
        )
        prefix_weight = jnp.exp(prefix_scores - peak).astype(bf16)
        own_weight = jnp.where(mask, jnp.exp(own_scores - peak), 0.0).astype(bf16)
        total = jnp.sum(prefix_weight.astype(f32), axis=1, keepdims=True) + jnp.sum(
            own_weight.astype(f32), axis=1, keepdims=True
        )
        return peak, total, prefix_weight, own_weight

    def values_of(first, prefix_weight, own_weight):
        kv = pl.ds(pl.multiple_of(first // GROUP * HD, HD), HD)
        own_values = with_fresh(sv_ref[:, :, kv], fv8[:, kv])
        value_scale = jnp.concatenate([vs8[:, kv]] * unit_heads, axis=0)
        prefix_part = jnp.dot(prefix_weight, pv_ref[:, kv], preferred_element_type=f32)
        own_part = jnp.dot(own_weight, own_values, preferred_element_type=f32)
        return prefix_part * value_scale + own_part

    def attend(b, finish):
        firsts = [b * heads_block + i * unit_heads for i in range(units)]
        scores = [scores_of(first) for first in firsts]
        weights = [weights_of(*score) for score in scores]
        numerators = [values_of(first, *w[2:]) for first, w in zip(firsts, weights)]
        peaks = jnp.zeros((rs, LANES), f32)
        totals = jnp.ones((rs, LANES), f32)
        for i in range(units):
            for g in range(unit_heads):
                j = i * unit_heads + g
                part = slice(g * rs, (g + 1) * rs)
                peaks = jnp.where(stat_lane == j, weights[i][0][part], peaks)
                totals = jnp.where(stat_lane == j, weights[i][1][part], totals)
                acc_s[b, :, j * HD : (j + 1) * HD] = numerators[i][part].astype(bf16)
        stat_s[b, 0] = peaks
        stat_s[b, 1] = totals
        finish()

    def farthest(k):
        down = jnp.where(pre_n - 1 - k > pre, pre_n - 1 - k, pre_n - 2 - k)
        up = jnp.where(k < pre, k, k + 1)
        target = jnp.where(2 * pre < pre_n, down, up)
        return lax.rem(target - pre + pre_n, pre_n)

    for k in range(pre_n):

        def finish(k=k):
            if k == 0:
                pl.semaphore_wait(barrier, pre_n + row_n - 2 + (split - 1) * row_n)
            if k < pre_n - 1:
                stat_copy(farthest(k)).start()
                acc_copy(farthest(k)).start()

        attend(ahead(farthest(k)) if k < pre_n - 1 else pre, finish)

    ffs_copy.start()
    for c in range(n_tiles):
        gu_copy(c).start()
    landed(stat_r, stat_sem.at[1])
    peak_of = [stat_s[pre, 0]] + [stat_r[d - 1, 0] for d in range(1, pre_n)]
    total_of = [stat_s[pre, 1]] + [stat_r[d - 1, 1] for d in range(1, pre_n)]
    highest = functools.reduce(jnp.maximum, peak_of)
    factor_of = [jnp.exp(peak - highest) for peak in peak_of]
    weight_sum = sum(factor * total for factor, total in zip(factor_of, total_of))
    factor_of = [factor / weight_sum for factor in factor_of]
    landed(acc_r, acc_sem.at[1])
    for j in range(heads_block):
        part = slice(j * HD, (j + 1) * HD)
        value = acc_s[pre, :, part].astype(f32) * factor_of[0][:, j : j + 1]
        for d in range(1, pre_n):
            value = value + acc_r[d - 1, :, part].astype(f32) * factor_of[d][:, j : j + 1]
        mix_g[row, :, part] = value.astype(bf16)
    for d in range(1, row_n):
        mix_copy(d).start()
    landed(ow, ow_sem)
    landed(mix_g.at[pl.ds(0, row_n - 1)], mix_sem.at[1])
    mix_x[...] = mix_g[...].astype(f32).reshape(everyone, block).astype(bf16)

    def project(c, carry):
        product = jnp.dot(mix_x[...], ow[c], preferred_element_type=f32)
        for p in range(pre_n):
            part = product[p * hs : (p + 1) * hs]
            prod_f[c, p] = part
            prod_s[c, p] = part.astype(bf16)
        for d in range(1, pre_n):
            prod_copy(c, d).start()
        return carry

    lax.fori_loop(0, n_out, project, 0)
    for c in range(n_out):
        part = slice(c * out_width, (c + 1) * out_width)
        value = hid_ref[:, :, part].astype(f32).reshape(hs, out_width) + prod_f[c, pre]
        landed(prod_r.at[c], prod_sem.at[1 + c])
        for d in range(1, pre_n):
            value = value + prod_r[c, d - 1].astype(f32)
        res_g[grp, pre, :, part] = value.astype(bf16)
        for d in range(1, pre_n):
            res_copy(c, d).start()
        for e in range(1, split):
            pass_copy(c, e, 0).start()
        res_out[:, :, part] = value.reshape(hid_local, STEPS, out_width).astype(bf16)
    ffs_copy.wait()
    ffn_pick = jnp.where(
        iota((rs, adapters), 1) == per_row(ids_ref, (rs, adapters)), 1.0, 0.0
    ).astype(bf16)
    ffn8[...] = jnp.dot(ffn_pick, ffs[...], preferred_element_type=f32)

    for c in range(n_out):
        for d in range(1, pre_n):
            res_copy(c, d).wait_recv()
            for e in range(1, split):
                pass_copy(c, e, d).start()

    spread_from = iota((LANES, 4 * LANES), 0)
    spread_to = iota((LANES, 4 * LANES), 1)
    spread = jnp.where(
        spread_to
        == jnp.where(spread_to < 2 * LANES, 2 * spread_from, 2 * LANES + 2 * spread_from + 1),
        1.0,
        0.0,
    ).astype(bf16)

    def spread_rows(e, residual):
        normed = (residual * gain_ref[...].astype(f32).reshape(1, depth)).astype(bf16)
        first = 2 * e * everyone
        gate_rows = slice(first, first + everyone)
        up_rows = slice(first + everyone, first + 2 * everyone)
        blocks = depth // LANES
        batch = min(blocks, 4)
        for j in range(0, blocks, batch):
            stacked = jnp.concatenate(
                [normed[:, k * LANES : (k + 1) * LANES] for k in range(j, j + batch)], axis=0
            )
            parts = jnp.dot(stacked, spread, preferred_element_type=f32).astype(bf16)
            for k in range(batch):
                part = parts[k * everyone : (k + 1) * everyone]
                at = slice(2 * (j + k) * LANES, 2 * (j + k + 1) * LANES)
                x_exp[gate_rows, at] = part[:, : 2 * LANES]
                x_exp[up_rows, at] = part[:, 2 * LANES :]

    residual = res_g[grp].astype(f32).reshape(everyone, depth)
    squares = jnp.sum(residual * residual, axis=1, keepdims=True)
    for r in range(row_n):
        sq_s[r] = jnp.broadcast_to(squares[r * rs : (r + 1) * rs], (rs, LANES))
    for d in range(1, row_n):
        sq_copy(d).start()
    spread_rows(0, residual)
    def unit_product(g, rows):
        weights = [gu[g * unit_tiles + t] for t in range(unit_tiles)]
        weight = jnp.concatenate(weights, axis=1) if unit_tiles > 1 else weights[0]
        return jnp.dot(x_exp[:rows], weight, preferred_element_type=f32)

    def gate_and_up(product, e, r):
        at = 2 * e * everyone + r * rs
        up_at = at + everyone
        return jnp.concatenate([product[at : at + rs], product[up_at : up_at + rs]], axis=0)

    own_step = 2 if own % 2 == 0 else 1
    shared_step = 2 if shared % 2 == 0 else 1

    def own_units(p, carry):
        slots = [p * own_step + k for k in range(own_step)]
        products = [unit_product(g, 2 * everyone) for g in slots]
        for g, product in zip(slots, products):
            for r in range(row_n):
                both = gate_and_up(product, 0, r)
                gate_f[g, r] = both
                gate_s[g, r] = both.astype(bf16)
            for d in range(1, row_n):
                gate_copy(g, d).start()
        return carry

    def shared_units(p, carry):
        slots = [p * shared_step + k for k in range(shared_step)]
        products = [unit_product(own + i, 2 * split * everyone) for i in slots]
        for i, product in zip(slots, products):
            for e in range(split):
                for r in range(row_n):
                    both = gate_and_up(product, e, r)
                    if e == 0:
                        gate_f[own + i, r] = both
                    gate_s[own + i * split + e, r] = both.astype(bf16)
            for e, d in others:
                both_copy(i, e, d).start()
        return carry

    landed(gu, gu_sem)
    lax.fori_loop(0, own // own_step, own_units, 0)
    if split > 1:
        landed(res_g.at[pl.ds(0, split - 1)], pass_sem.at[1])
    for e in range(1, split):
        spread_rows(e, res_g[across(e)].astype(f32).reshape(everyone, depth))
    lax.fori_loop(0, shared // shared_step, shared_units, 0)

    square_sum = sq_s[row]
    landed(sq_r, sq_sem.at[1])
    for d in range(1, row_n):
        square_sum = square_sum + sq_r[d - 1]
    inverse = lax.rsqrt(square_sum[:, :1] / D + 1e-05)

    def activate(both, at):
        gate = both[:rs] * inverse
        up = both[rs:] * inverse
        part = pl.ds(pl.multiple_of(at, LANES), unit)
        value = gate / (1.0 + jnp.exp(-gate)) * up * ffn8[:, part]
        act_out[:, :, part] = value.reshape(row_local, STEPS, unit).astype(bf16)

    def finish_own(g, carry):
        landed(gate_r.at[g], gate_sem.at[1 + g])
        both = gate_f[g, row]
        for d in range(1, row_n):
            both = both + gate_r[g, d - 1].astype(f32)
        activate(both, g * unit)
        return carry

    def finish_shared(i, carry):
        landed(gate_b.at[i], both_sem.at[1 + i])
        for e in range(split):
            both = gate_f[own + i, row] if e == 0 else jnp.zeros((2 * rs, unit), f32)
            for d in range(1 if e == 0 else 0, row_n):
                both = both + gate_b[i, e * row_n + d - 1].astype(f32)
            owner = lax.rem(grp + split - e, split)
            activate(both, (own + owner * shared + i) * unit)
        return carry

    lax.fori_loop(0, own, finish_own, 0)
    lax.fori_loop(0, shared, finish_shared, 0)

    landed(stat_r, stat_sem.at[0])
    landed(acc_r, acc_sem.at[0])
    landed(mix_g.at[pl.ds(0, row_n - 1)], mix_sem.at[0])
    landed(prod_r, prod_sem.at[0])
    landed(res_g.at[0, pl.ds(0, pre_n - 1)], res_sem.at[0])
    if split > 1:
        landed(res_g.at[pl.ds(0, split - 1)], pass_sem.at[0])
    landed(sq_r, sq_sem.at[0])
    landed(gate_r, gate_sem.at[0])
    landed(gate_b, both_sem.at[0])


def hand_on(residual_ref, activation_ref, residual_out, activation_out, sem):
    residual = pltpu.make_async_copy(residual_ref, residual_out, sem.at[0])
    activation = pltpu.make_async_copy(activation_ref, activation_out, sem.at[1])
    residual.start()
    activation.start()
    residual.wait()
    activation.wait()


def per_device(
    queries,
    prefix_keys,
    prefix_values,
    suffix_keys,
    suffix_values,
    new_keys,
    new_values,
    hidden,
    adapter_ids,
    suffix_lengths,
    kv_scales,
    ffn_scales,
    out_weight,
    norm_gain,
    gate_up,
):
    pre_n = lax.axis_size("pre")
    row_n = lax.axis_size("row")
    row_local = queries.shape[0]
    rs = row_local * STEPS
    hs = hidden.shape[0] * STEPS
    kv_width = prefix_keys.shape[1]
    adapters, ff = ffn_scales.shape
    block, cols = out_weight.shape
    depth = gate_up.shape[0]
    out_width = min(cols, 512)
    n_out = cols // out_width
    split = lax.axis_size("grp")
    unit = 2 * LANES if ff % (2 * LANES) == 0 else LANES
    units = ff // unit
    shared = int(units * (1 - OWN_SHARE)) // split
    own = units - shared * split
    n_tiles = (own + shared) * unit // LANES
    everyone = row_n * rs
    dma = pltpu.SemaphoreType.DMA
    vmem = pl.BlockSpec(memory_space=pltpu.VMEM)
    hbm = pl.BlockSpec(memory_space=pltpu.HBM)
    scratch = [
        pltpu.SMEM(adapter_ids.shape, jnp.int32),
        pltpu.SMEM(suffix_lengths.shape, jnp.int32),
        pltpu.VMEM(queries.shape, bf16),
        pltpu.VMEM(prefix_keys.shape, bf16),
        pltpu.VMEM(prefix_values.shape, bf16),
        pltpu.VMEM(suffix_keys.shape, bf16),
        pltpu.VMEM(suffix_values.shape, bf16),
        pltpu.VMEM(new_keys.shape, bf16),
        pltpu.VMEM(new_values.shape, bf16),
        pltpu.VMEM(hidden.shape, bf16),
        pltpu.VMEM(kv_scales.shape, bf16),
        pltpu.VMEM(norm_gain.shape, bf16),
        pltpu.VMEM((n_out, block, out_width), bf16),
        pltpu.VMEM((n_tiles, 2 * depth, LANES), bf16),
        pltpu.VMEM((adapters, ff), bf16),
        pltpu.VMEM((rs, D), f32),
        pltpu.VMEM((rs, kv_width), f32),
        pltpu.VMEM((rs, kv_width), f32),
        pltpu.VMEM((rs, kv_width), f32),
        pltpu.VMEM((rs, kv_width), f32),
        pltpu.VMEM((pre_n, rs, block), bf16),
        pltpu.VMEM((pre_n - 1, rs, block), bf16),
        pltpu.VMEM((pre_n, 2, rs, LANES), f32),
        pltpu.VMEM((pre_n - 1, 2, rs, LANES), f32),
        pltpu.VMEM((row_n, rs, block), bf16),
        pltpu.VMEM((everyone, block), bf16),
        pltpu.VMEM((n_out, pre_n, hs, out_width), bf16),
        pltpu.VMEM((n_out, pre_n, hs, out_width), f32),
        pltpu.VMEM((n_out, pre_n - 1, hs, out_width), bf16),
        pltpu.VMEM((split, pre_n, hs, cols), bf16),
        pltpu.VMEM((2 * split * everyone, 2 * depth), bf16),
        pltpu.VMEM((own + shared * split, row_n, 2 * rs, unit), bf16),
        pltpu.VMEM((own + shared, row_n, 2 * rs, unit), f32),
        pltpu.VMEM((own, row_n - 1, 2 * rs, unit), bf16),
        pltpu.VMEM((shared, split * row_n - 1, 2 * rs, unit), bf16),
        pltpu.VMEM((row_n, rs, LANES), f32),
        pltpu.VMEM((row_n - 1, rs, LANES), f32),
        pltpu.VMEM((rs, ff), f32),
        dma((12,)),
        dma,
        dma,
        dma,
        dma((2,)),
        dma((2,)),
        dma((2,)),
        dma((1 + n_out,)),
        dma((1 + n_out * (pre_n - 1),)),
        dma((2,)),
        dma((1 + own,)),
        dma((1 + shared,)),
        dma((2,)),
    ]
    outputs = pl.pallas_call(
        functools.partial(layer_kernel, (pre_n, row_n, split, own, shared)),
        out_shape=(
            jax.ShapeDtypeStruct(hidden.shape, bf16),
            jax.ShapeDtypeStruct((row_local, STEPS, ff), bf16),
        ),
        in_specs=[hbm] * 15,
        out_specs=(vmem, vmem),
        scratch_shapes=scratch,
        compiler_params=pltpu.CompilerParams(
            collective_id=0, has_side_effects=True, vmem_limit_bytes=GRANT * 1024 * 1024
        ),
    )(
        *(
            pltpu.with_memory_space_constraint(operand, pltpu.HBM)
            for operand in (
                adapter_ids,
                suffix_lengths,
                queries,
                prefix_keys,
                prefix_values,
                suffix_keys,
                suffix_values,
                new_keys,
                new_values,
                hidden,
                kv_scales,
                norm_gain,
                ffn_scales,
                out_weight,
                gate_up,
            )
        )
    )
    return pl.pallas_call(
        hand_on,
        out_shape=tuple(jax.ShapeDtypeStruct(value.shape, value.dtype) for value in outputs),
        in_specs=[vmem, vmem],
        out_specs=(hbm, hbm),
        scratch_shapes=[dma((2,))],
        compiler_params=pltpu.CompilerParams(vmem_limit_bytes=1024 * 1024),
    )(*outputs)


def solution(mesh):
    placed = (
        P(("grp", "row"), None, None),
        P(("grp", "pre"), None),
        P(("grp", "pre"), None),
        P(("grp", "row"), "pre", None),
        P(("grp", "row"), "pre", None),
        P(("grp", "row"), None, None),
        P(("grp", "row"), None, None),
        P(("grp", "pre"), None, "row"),
        P(("grp", "row")),
        P(("grp", "row")),
        P(),
        P(None, "pre"),
        P("pre", "row"),
        P("row"),
        P("row", None, "pre"),
    )
    return jax.shard_map(
        per_device,
        mesh=mesh,
        in_specs=placed,
        out_specs=(P(("grp", "pre"), None, "row"), P(("grp", "row"), None, "pre")),
        check_vma=False,
    )
```

```python
import functools

import jax
import jax.numpy as jnp
from jax import lax
from jax.experimental import pallas as pl
from jax.experimental.pallas import tpu as pltpu
from jax.sharding import PartitionSpec as P

D = 8192
HEADS = 64
KV_HEADS = 8
HD = 128
STEPS = 2
GROUP = HEADS // KV_HEADS
LANES = 128
UNIT_WIDTHS = (128, 256, 512)
EARLY_SHARE = 0.3

GRANT = 52

masked_score = -1e30
f32 = jnp.float32
bf16 = jnp.bfloat16


def iota(shape, axis):
    return lax.broadcasted_iota(jnp.int32, shape, axis)


def layer_kernel(
    sizes,
    ids_hbm,
    lens_hbm,
    q_hbm,
    pk_hbm,
    pv_hbm,
    sk_hbm,
    sv_hbm,
    nk_hbm,
    nv_hbm,
    hid_hbm,
    kvs_hbm,
    gain_hbm,
    ffs_hbm,
    ow_hbm,
    gu_hbm,
    res_out,
    act_out,
    ids_ref,
    lens_ref,
    q_ref,
    pk_ref,
    pv_ref,
    sk_ref,
    sv_ref,
    nk_ref,
    nv_ref,
    hid_ref,
    kvs_ref,
    gain_ref,
    ow,
    gu,
    ffs,
    q8,
    ks8,
    vs8,
    fk8,
    fv8,
    acc_s,
    acc_r,
    stat_s,
    stat_r,
    mix_g,
    mix_x,
    prod_s,
    prod_f,
    prod_r,
    res_g,
    x_exp,
    gate_s,
    gate_f,
    gate_r,
    gate_h,
    sq_s,
    sq_r,
    ffn8,
    in_sem,
    ow_sem,
    gu_sem,
    ffs_sem,
    acc_sem,
    stat_sem,
    mix_sem,
    prod_sem,
    res_sem,
    gate_sem,
    sq_sem,
):
    pre_n, row_n, units_ff, early = sizes
    pre = lax.axis_index("pre")
    row = lax.axis_index("row")
    row_local = q_hbm.shape[0]
    rs = row_local * STEPS
    hid_local = hid_ref.shape[0]
    hs = hid_local * STEPS
    suffix_local = sk_ref.shape[1]
    kv_width = pk_ref.shape[1]
    adapters = kvs_ref.shape[0]
    block = D // pre_n
    heads_block = block // HD
    cols = ow_hbm.shape[1]
    depth = gu_hbm.shape[0]
    ff = gu_hbm.shape[2]
    score_scale = HD ** (-0.5)
    n_out, _, out_width = ow.shape
    n_tiles = gu.shape[0]
    unit = gate_s.shape[3]
    unit_tiles = unit // LANES
    halves = 2 if n_out % 2 == 0 else 1
    half_chunks = n_out // halves
    half_depth = 2 * depth // halves
    everyone = row_n * rs

    gu_rows = gu_hbm.reshape(2 * depth, ff)

    def ow_copy(c):
        return pltpu.make_async_copy(
            ow_hbm.at[:, pl.ds(c * out_width, out_width)], ow.at[c], ow_sem
        )

    def gu_copy(c):
        return pltpu.make_async_copy(
            gu_rows.at[:, pl.ds(c * LANES, LANES)],
            gu.at[c],
            gu_sem,
        )

    staged = [
        (ids_hbm, ids_ref),
        (lens_hbm, lens_ref),
        (kvs_hbm, kvs_ref),
        (q_hbm, q_ref),
        (nk_hbm, nk_ref),
        (nv_hbm, nv_ref),
        (sk_hbm, sk_ref),
        (pk_hbm, pk_ref),
        (sv_hbm, sv_ref),
        (pv_hbm, pv_ref),
        (hid_hbm, hid_ref),
        (gain_hbm, gain_ref),
    ]
    staged = [
        pltpu.make_async_copy(source, target, in_sem.at[i])
        for i, (source, target) in enumerate(staged)
    ]
    for copy in staged:
        copy.start()
    ffs_copy = pltpu.make_async_copy(ffs_hbm, ffs, ffs_sem)

    def landed(ref, sem):
        pltpu.make_async_copy(ref, ref, sem).wait()

    barrier = pltpu.get_barrier_semaphore()
    for d in range(1, pre_n):
        pl.semaphore_signal(
            barrier,
            inc=1,
            device_id={"pre": lax.rem(pre + d, pre_n)},
            device_id_type=pl.DeviceIdType.MESH,
        )
    for d in range(1, row_n):
        pl.semaphore_signal(
            barrier,
            inc=1,
            device_id={"row": lax.rem(row + d, row_n)},
            device_id_type=pl.DeviceIdType.MESH,
        )
    def remote(src, dst, sems, axis, target):
        return pltpu.make_async_remote_copy(
            src_ref=src,
            dst_ref=dst,
            send_sem=sems[0],
            recv_sem=sems[1],
            device_id={axis: target},
            device_id_type=pl.DeviceIdType.MESH,
        )

    def pair(sem, at=0):
        return sem.at[0], sem.at[1 + at]

    def ahead(d):
        return lax.rem(pre + d, pre_n)

    def beside(d):
        return lax.rem(row + d, row_n)

    def acc_copy(d):
        return remote(acc_s.at[ahead(d)], acc_r.at[d - 1], pair(acc_sem), "pre", ahead(d))

    def stat_copy(d):
        return remote(stat_s.at[ahead(d)], stat_r.at[d - 1], pair(stat_sem), "pre", ahead(d))

    def mix_copy(d):
        return remote(mix_g.at[row], mix_g.at[row], pair(mix_sem), "row", beside(d))

    def prod_copy(c, d):
        return remote(
            prod_s.at[c, ahead(d)], prod_r.at[c, d - 1], pair(prod_sem, c), "pre", ahead(d)
        )

    def res_copy(c, d):
        block_at = res_g.at[pre, :, pl.ds(c * out_width, out_width)]
        return remote(block_at, block_at, pair(res_sem, c * (pre_n - 1) + d - 1), "pre", ahead(d))

    def sq_copy(d):
        return remote(sq_s.at[beside(d)], sq_r.at[d - 1], pair(sq_sem), "row", beside(d))

    def gate_copy(g, d):
        return remote(
            gate_s.at[g, beside(d)], gate_r.at[g, d - 1], pair(gate_sem, g), "row", beside(d)
        )

    def per_row(ref, shape):
        which = iota(shape, 0) // STEPS
        out = jnp.full(shape, ref[0], jnp.int32)
        for r in range(1, row_local):
            out = jnp.where(which == r, ref[r], out)
        return out

    for copy in staged[:6]:
        copy.wait()
    adapter = per_row(ids_ref, (rs, 2 * adapters))
    lane = iota((rs, 2 * adapters), 1)
    pick_key = jnp.where(lane == 2 * adapter, 1.0, 0.0)
    pick_value = jnp.where(lane == 2 * adapter + 1, 1.0, 0.0)
    pick = jnp.concatenate([pick_key, pick_value], axis=0).astype(bf16)
    scales = jnp.dot(
        pick, kvs_ref[...].reshape(2 * adapters, kv_width), preferred_element_type=f32
    )
    ks8[...] = scales[:rs]
    vs8[...] = scales[rs:]
    fk8[...] = nk_ref[...].astype(f32).reshape(rs, kv_width) * scales[:rs]
    fv8[...] = nv_ref[...].astype(f32).reshape(rs, kv_width) * scales[rs:]
    q8[...] = q_ref[...].astype(f32).reshape(rs, D)

    unit_heads = min(GROUP, heads_block)
    units = heads_block // unit_heads
    unit_rows = unit_heads * rs
    suffix_rows = row_local * suffix_local
    own_rows = -(-(suffix_rows + rs) // LANES) * LANES
    pad = own_rows - suffix_rows - rs
    at_row = lax.rem(iota((unit_rows, own_rows), 0), rs)
    at_col = iota((unit_rows, own_rows), 1)
    lens = per_row(lens_ref, (rs, own_rows))
    lens = jnp.concatenate([lens] * unit_heads, axis=0)
    query_row = at_row // STEPS
    query_step = lax.rem(at_row, STEPS)
    position = pre * suffix_local + lax.rem(at_col, suffix_local)
    fresh_at = at_col - suffix_rows
    in_suffix = (at_col < suffix_rows) & (at_col // suffix_local == query_row) & (position < lens)
    in_new = (
        (fresh_at >= 0)
        & (fresh_at < rs)
        & (fresh_at // STEPS == query_row)
        & (lax.rem(fresh_at, STEPS) <= query_step)
        & (pre == 0)
    )
    mask = in_suffix | in_new
    stat_lane = iota((rs, LANES), 1)
    transposed = (((1,), (1,)), ((), ()))

    def with_fresh(old, fresh):
        tail = jnp.concatenate([fresh, jnp.zeros((pad, HD), f32)], axis=0) if pad else fresh
        return jnp.concatenate([old.reshape(suffix_rows, HD), tail.astype(bf16)], axis=0)

    def scores_of(first):
        kv = pl.ds(pl.multiple_of(first // GROUP * HD, HD), HD)
        pieces = [
            q8[:, pl.ds(pl.multiple_of((first + g) * HD, HD), HD)] for g in range(unit_heads)
        ]
        key_scale = ks8[:, kv]
        query = jnp.concatenate(pieces, axis=0).astype(bf16)
        scaled = jnp.concatenate([piece * key_scale for piece in pieces], axis=0).astype(bf16)
        own_keys = with_fresh(sk_ref[:, :, kv], fk8[:, kv])
        prefix_scores = lax.dot_general(
            scaled, pk_ref[:, kv], transposed, preferred_element_type=f32
        )
        own_scores = lax.dot_general(query, own_keys, transposed, preferred_element_type=f32)
        return prefix_scores, own_scores

    def weights_of(prefix_scores, own_scores):
        prefix_scores = prefix_scores * score_scale
        own_scores = jnp.where(mask, own_scores * score_scale, masked_score)
        peak = jnp.maximum(
            jnp.max(prefix_scores, axis=1, keepdims=True),
            jnp.max(own_scores, axis=1, keepdims=True),
        )
        prefix_weight = jnp.exp(prefix_scores - peak).astype(bf16)
        own_weight = jnp.where(mask, jnp.exp(own_scores - peak), 0.0).astype(bf16)
        total = jnp.sum(prefix_weight.astype(f32), axis=1, keepdims=True) + jnp.sum(
            own_weight.astype(f32), axis=1, keepdims=True
        )
        return peak, total, prefix_weight, own_weight

    def values_of(first, prefix_weight, own_weight):
        kv = pl.ds(pl.multiple_of(first // GROUP * HD, HD), HD)
        own_values = with_fresh(sv_ref[:, :, kv], fv8[:, kv])
        value_scale = jnp.concatenate([vs8[:, kv]] * unit_heads, axis=0)
        prefix_part = jnp.dot(prefix_weight, pv_ref[:, kv], preferred_element_type=f32)
        own_part = jnp.dot(own_weight, own_values, preferred_element_type=f32)
        return prefix_part * value_scale + own_part

    def attend(b, finish):
        firsts = [b * heads_block + i * unit_heads for i in range(units)]
        scores = [scores_of(first) for first in firsts]
        weights = [weights_of(*score) for score in scores]
        numerators = [values_of(first, *w[2:]) for first, w in zip(firsts, weights)]
        peaks = jnp.zeros((rs, LANES), f32)
        totals = jnp.ones((rs, LANES), f32)
        for i in range(units):
            for g in range(unit_heads):
                j = i * unit_heads + g
                part = slice(g * rs, (g + 1) * rs)
                peaks = jnp.where(stat_lane == j, weights[i][0][part], peaks)
                totals = jnp.where(stat_lane == j, weights[i][1][part], totals)
                acc_s[b, :, j * HD : (j + 1) * HD] = numerators[i][part].astype(bf16)
        stat_s[b, 0] = peaks
        stat_s[b, 1] = totals
        finish()

    def farthest(k):
        down = jnp.where(pre_n - 1 - k > pre, pre_n - 1 - k, pre_n - 2 - k)
        up = jnp.where(k < pre, k, k + 1)
        target = jnp.where(2 * pre < pre_n, down, up)
        return lax.rem(target - pre + pre_n, pre_n)

    for copy in staged[6:10]:
        copy.wait()
    for c in range(n_out):
        ow_copy(c).start()
    for k in range(pre_n):

        def finish(k=k):
            if k == 0:
                pl.semaphore_wait(barrier, pre_n + row_n - 2)
            if k < pre_n - 1:
                stat_copy(farthest(k)).start()
                acc_copy(farthest(k)).start()

        attend(ahead(farthest(k)) if k < pre_n - 1 else pre, finish)

    ffs_copy.start()
    for c in range(n_tiles):
        gu_copy(c).start()
    landed(stat_r, stat_sem.at[1])
    peak_of = [stat_s[pre, 0]] + [stat_r[d - 1, 0] for d in range(1, pre_n)]
    total_of = [stat_s[pre, 1]] + [stat_r[d - 1, 1] for d in range(1, pre_n)]
    highest = functools.reduce(jnp.maximum, peak_of)
    factor_of = [jnp.exp(peak - highest) for peak in peak_of]
    weight_sum = sum(factor * total for factor, total in zip(factor_of, total_of))
    factor_of = [factor / weight_sum for factor in factor_of]
    landed(acc_r, acc_sem.at[1])
    for j in range(heads_block):
        part = slice(j * HD, (j + 1) * HD)
        value = acc_s[pre, :, part].astype(f32) * factor_of[0][:, j : j + 1]
        for d in range(1, pre_n):
            value = value + acc_r[d - 1, :, part].astype(f32) * factor_of[d][:, j : j + 1]
        mix_g[row, :, part] = value.astype(bf16)
    for d in range(1, row_n):
        mix_copy(d).start()
    landed(ow, ow_sem)
    landed(mix_g.at[pl.ds(0, row_n - 1)], mix_sem.at[1])
    mix_x[...] = mix_g[...].astype(f32).reshape(everyone, block).astype(bf16)

    def project(c, carry):
        product = jnp.dot(mix_x[...], ow[c], preferred_element_type=f32)
        for p in range(pre_n):
            part = product[p * hs : (p + 1) * hs]
            prod_f[c, p] = part
            prod_s[c, p] = part.astype(bf16)
        for d in range(1, pre_n):
            prod_copy(c, d).start()
        return carry

    lax.fori_loop(0, n_out, project, 0)
    for copy in staged[10:]:
        copy.wait()
    for c in range(n_out):
        part = slice(c * out_width, (c + 1) * out_width)
        value = hid_ref[:, :, part].astype(f32).reshape(hs, out_width) + prod_f[c, pre]
        landed(prod_r.at[c], prod_sem.at[1 + c])
        for d in range(1, pre_n):
            value = value + prod_r[c, d - 1].astype(f32)
        res_g[pre, :, part] = value.astype(bf16)
        for d in range(1, pre_n):
            res_copy(c, d).start()
        res_out[:, :, part] = value.reshape(hid_local, STEPS, out_width).astype(bf16)
    ffs_copy.wait()
    ffn_pick = jnp.where(
        iota((rs, adapters), 1) == per_row(ids_ref, (rs, adapters)), 1.0, 0.0
    ).astype(bf16)
    ffn8[...] = jnp.dot(ffn_pick, ffs[...], preferred_element_type=f32)

    spread_from = iota((LANES, 4 * LANES), 0)
    spread_to = iota((LANES, 4 * LANES), 1)
    spread = jnp.where(
        spread_to
        == jnp.where(spread_to < 2 * LANES, 2 * spread_from, 2 * LANES + 2 * spread_from + 1),
        1.0,
        0.0,
    ).astype(bf16)

    def spread_chunk(c):
        at = slice(c * out_width, (c + 1) * out_width)
        residual = res_g[:, :, at].astype(f32).reshape(everyone, out_width)
        gain = gain_ref[at].astype(f32).reshape(1, out_width)
        normed = (residual * gain).astype(bf16)
        blocks = out_width // LANES
        stacked = jnp.concatenate(
            [normed[:, k * LANES : (k + 1) * LANES] for k in range(blocks)], axis=0
        )
        parts = jnp.dot(stacked, spread, preferred_element_type=f32).astype(bf16)
        for k in range(blocks):
            part = parts[k * everyone : (k + 1) * everyone]
            to = 2 * (c * out_width + k * LANES)
            x_exp[:everyone, to : to + 2 * LANES] = part[:, : 2 * LANES]
            x_exp[everyone:, to : to + 2 * LANES] = part[:, 2 * LANES :]
        return jnp.sum(residual * residual, axis=1, keepdims=True)

    def gather_chunks(first, last):
        for c in range(first, last):
            for d in range(1, pre_n):
                res_copy(c, d).wait_recv()
        return sum(spread_chunk(c) for c in range(first, last))

    def unit_product(g, first, last):
        at = slice(first * half_depth, last * half_depth)
        weights = [gu[g * unit_tiles + t, at] for t in range(unit_tiles)]
        weight = jnp.concatenate(weights, axis=1) if unit_tiles > 1 else weights[0]
        return jnp.dot(x_exp[:, at], weight, preferred_element_type=f32)

    def first_half(g, carry):
        gate_h[g] = unit_product(g, 0, 1)
        return carry

    def send_unit(g, product):
        for r in range(row_n):
            gate = product[r * rs : (r + 1) * rs]
            up = product[everyone + r * rs : everyone + (r + 1) * rs]
            both = jnp.concatenate([gate, up], axis=0)
            gate_f[g, r] = both
            gate_s[g, r] = both.astype(bf16)
        for d in range(1, row_n):
            gate_copy(g, d).start()

    def second_half(g, carry):
        send_unit(g, gate_h[g] + unit_product(g, 1, 2))
        return carry

    def whole_unit(g, carry):
        send_unit(g, unit_product(g, 0, halves))
        return carry

    squares = gather_chunks(0, half_chunks)
    landed(gu, gu_sem)
    if early > 0:
        lax.fori_loop(0, early, first_half, 0)
        squares = squares + gather_chunks(half_chunks, n_out)
    for r in range(row_n):
        sq_s[r] = jnp.broadcast_to(squares[r * rs : (r + 1) * rs], (rs, LANES))
    for d in range(1, row_n):
        sq_copy(d).start()
    if early > 0:
        lax.fori_loop(0, early, second_half, 0)
    for g in range(early, units_ff):
        whole_unit(g, 0)

    square_sum = sq_s[row]
    landed(sq_r, sq_sem.at[1])
    for d in range(1, row_n):
        square_sum = square_sum + sq_r[d - 1]
    inverse = lax.rsqrt(square_sum[:, :1] / D + 1e-05)

    def activate(both, at):
        gate = both[:rs] * inverse
        up = both[rs:] * inverse
        part = pl.ds(pl.multiple_of(at, LANES), unit)
        value = gate / (1.0 + jnp.exp(-gate)) * up * ffn8[:, part]
        act_out[:, :, part] = value.reshape(row_local, STEPS, unit).astype(bf16)

    def finish_unit(g, carry):
        landed(gate_r.at[g], gate_sem.at[1 + g])
        both = gate_f[g, row]
        for d in range(1, row_n):
            both = both + gate_r[g, d - 1].astype(f32)
        activate(both, g * unit)
        return carry

    lax.fori_loop(0, units_ff, finish_unit, 0)

    landed(stat_r, stat_sem.at[0])
    landed(acc_r, acc_sem.at[0])
    landed(mix_g.at[pl.ds(0, row_n - 1)], mix_sem.at[0])
    landed(prod_r, prod_sem.at[0])
    landed(res_g.at[pl.ds(0, pre_n - 1)], res_sem.at[0])
    landed(sq_r, sq_sem.at[0])
    landed(gate_r, gate_sem.at[0])


def hand_on(residual_ref, activation_ref, residual_out, activation_out, sem):
    residual = pltpu.make_async_copy(residual_ref, residual_out, sem.at[0])
    activation = pltpu.make_async_copy(activation_ref, activation_out, sem.at[1])
    residual.start()
    activation.start()
    residual.wait()
    activation.wait()


def per_device(
    queries,
    prefix_keys,
    prefix_values,
    suffix_keys,
    suffix_values,
    new_keys,
    new_values,
    hidden,
    adapter_ids,
    suffix_lengths,
    kv_scales,
    ffn_scales,
    out_weight,
    norm_gain,
    gate_up,
):
    pre_n = lax.axis_size("pre")
    row_n = lax.axis_size("row")
    row_local = queries.shape[0]
    rs = row_local * STEPS
    hs = hidden.shape[0] * STEPS
    kv_width = prefix_keys.shape[1]
    adapters, ff = ffn_scales.shape
    block, cols = out_weight.shape
    depth = gate_up.shape[0]
    out_width = min(cols, 512)
    n_out = cols // out_width
    unit = max(width for width in UNIT_WIDTHS if ff % width == 0)
    units_ff = ff // unit
    early = int(units_ff * EARLY_SHARE) if n_out % 2 == 0 else 0
    n_tiles = ff // LANES
    everyone = row_n * rs
    dma = pltpu.SemaphoreType.DMA
    vmem = pl.BlockSpec(memory_space=pltpu.VMEM)
    hbm = pl.BlockSpec(memory_space=pltpu.HBM)
    scratch = [
        pltpu.SMEM(adapter_ids.shape, jnp.int32),
        pltpu.SMEM(suffix_lengths.shape, jnp.int32),
        pltpu.VMEM(queries.shape, bf16),
        pltpu.VMEM(prefix_keys.shape, bf16),
        pltpu.VMEM(prefix_values.shape, bf16),
        pltpu.VMEM(suffix_keys.shape, bf16),
        pltpu.VMEM(suffix_values.shape, bf16),
        pltpu.VMEM(new_keys.shape, bf16),
        pltpu.VMEM(new_values.shape, bf16),
        pltpu.VMEM(hidden.shape, bf16),
        pltpu.VMEM(kv_scales.shape, bf16),
        pltpu.VMEM(norm_gain.shape, bf16),
        pltpu.VMEM((n_out, block, out_width), bf16),
        pltpu.VMEM((n_tiles, 2 * depth, LANES), bf16),
        pltpu.VMEM((adapters, ff), bf16),
        pltpu.VMEM((rs, D), f32),
        pltpu.VMEM((rs, kv_width), f32),
        pltpu.VMEM((rs, kv_width), f32),
        pltpu.VMEM((rs, kv_width), f32),
        pltpu.VMEM((rs, kv_width), f32),
        pltpu.VMEM((pre_n, rs, block), bf16),
        pltpu.VMEM((pre_n - 1, rs, block), bf16),
        pltpu.VMEM((pre_n, 2, rs, LANES), f32),
        pltpu.VMEM((pre_n - 1, 2, rs, LANES), f32),
        pltpu.VMEM((row_n, rs, block), bf16),
        pltpu.VMEM((everyone, block), bf16),
        pltpu.VMEM((n_out, pre_n, hs, out_width), bf16),
        pltpu.VMEM((n_out, pre_n, hs, out_width), f32),
        pltpu.VMEM((n_out, pre_n - 1, hs, out_width), bf16),
        pltpu.VMEM((pre_n, hs, cols), bf16),
        pltpu.VMEM((2 * everyone, 2 * depth), bf16),
        pltpu.VMEM((units_ff, row_n, 2 * rs, unit), bf16),
        pltpu.VMEM((units_ff, row_n, 2 * rs, unit), f32),
        pltpu.VMEM((units_ff, row_n - 1, 2 * rs, unit), bf16),
        pltpu.VMEM((max(early, 1), 2 * everyone, unit), f32),
        pltpu.VMEM((row_n, rs, LANES), f32),
        pltpu.VMEM((row_n - 1, rs, LANES), f32),
        pltpu.VMEM((rs, ff), f32),
        dma((12,)),
        dma,
        dma,
        dma,
        dma((2,)),
        dma((2,)),
        dma((2,)),
        dma((1 + n_out,)),
        dma((1 + n_out * (pre_n - 1),)),
        dma((1 + units_ff,)),
        dma((2,)),
    ]
    outputs = pl.pallas_call(
        functools.partial(layer_kernel, (pre_n, row_n, units_ff, early)),
        out_shape=(
            jax.ShapeDtypeStruct(hidden.shape, bf16),
            jax.ShapeDtypeStruct((row_local, STEPS, ff), bf16),
        ),
        in_specs=[hbm] * 15,
        out_specs=(vmem, vmem),
        scratch_shapes=scratch,
        compiler_params=pltpu.CompilerParams(
            collective_id=0, has_side_effects=True, vmem_limit_bytes=GRANT * 1024 * 1024
        ),
    )(
        *(
            pltpu.with_memory_space_constraint(operand, pltpu.HBM)
            for operand in (
                adapter_ids,
                suffix_lengths,
                queries,
                prefix_keys,
                prefix_values,
                suffix_keys,
                suffix_values,
                new_keys,
                new_values,
                hidden,
                kv_scales,
                norm_gain,
                ffn_scales,
                out_weight,
                gate_up,
            )
        )
    )
    return pl.pallas_call(
        hand_on,
        out_shape=tuple(jax.ShapeDtypeStruct(value.shape, value.dtype) for value in outputs),
        in_specs=[vmem, vmem],
        out_specs=(hbm, hbm),
        scratch_shapes=[dma((2,))],
        compiler_params=pltpu.CompilerParams(vmem_limit_bytes=1024 * 1024),
    )(*outputs)


def solution(mesh):
    placed = (
        P(("grp", "row"), None, None),
        P(("grp", "pre"), None),
        P(("grp", "pre"), None),
        P(("grp", "row"), "pre", None),
        P(("grp", "row"), "pre", None),
        P(("grp", "row"), None, None),
        P(("grp", "row"), None, None),
        P(("grp", "pre"), None, "row"),
        P(("grp", "row")),
        P(("grp", "row")),
        P(),
        P(None, "pre"),
        P("pre", "row"),
        P("row"),
        P("row", None, "pre"),
    )
    return jax.shard_map(
        per_device,
        mesh=mesh,
        in_specs=placed,
        out_specs=(P(("grp", "pre"), None, "row"), P(("grp", "row"), None, "pre")),
        check_vma=False,
    )
```

```python
import functools

import jax
import jax.numpy as jnp
from jax import lax
from jax.experimental import pallas as pl
from jax.experimental.pallas import tpu as pltpu
from jax.sharding import PartitionSpec as P

D = 8192
HEADS = 64
KV_HEADS = 8
HD = 128
STEPS = 2
GROUP = HEADS // KV_HEADS
LANES = 128
UNIT_WIDTHS = (128, 256, 512)
EARLY_SHARE = 0.3

GRANT = 52

masked_score = -1e30
f32 = jnp.float32
bf16 = jnp.bfloat16


def iota(shape, axis):
    return lax.broadcasted_iota(jnp.int32, shape, axis)


def layer_kernel(
    sizes,
    ids_hbm,
    lens_hbm,
    q_hbm,
    pk_hbm,
    pv_hbm,
    sk_hbm,
    sv_hbm,
    nk_hbm,
    nv_hbm,
    hid_hbm,
    kvs_hbm,
    gain_hbm,
    ffs_hbm,
    ow_hbm,
    gu_hbm,
    res_out,
    act_out,
    ids_ref,
    lens_ref,
    q_ref,
    pk_ref,
    pv_ref,
    sk_ref,
    sv_ref,
    nk_ref,
    nv_ref,
    hid_ref,
    kvs_ref,
    gain_ref,
    ow,
    gu,
    ffs,
    q8,
    ks8,
    vs8,
    fk8,
    fv8,
    acc_s,
    acc_r,
    stat_s,
    stat_r,
    mix_g,
    mix_x,
    prod_s,
    prod_f,
    prod_r,
    res_g,
    x_exp,
    gate_s,
    gate_f,
    gate_r,
    gate_h,
    sq_s,
    sq_r,
    ffn8,
    in_sem,
    ow_sem,
    gu_sem,
    ffs_sem,
    acc_sem,
    stat_sem,
    mix_sem,
    prod_sem,
    res_sem,
    gate_sem,
    sq_sem,
):
    pre_n, row_n, units_ff, early = sizes
    pre = lax.axis_index("pre")
    row = lax.axis_index("row")
    row_local = q_hbm.shape[0]
    rs = row_local * STEPS
    hid_local = hid_ref.shape[0]
    hs = hid_local * STEPS
    suffix_local = sk_ref.shape[1]
    kv_width = pk_ref.shape[1]
    adapters = kvs_ref.shape[0]
    block = D // pre_n
    heads_block = block // HD
    cols = ow_hbm.shape[1]
    depth = gu_hbm.shape[0]
    ff = gu_hbm.shape[2]
    score_scale = HD ** (-0.5)
    n_out, _, out_width = ow.shape
    n_tiles = gu.shape[0]
    unit = gate_s.shape[3]
    unit_tiles = unit // LANES
    halves = 2 if n_out % 2 == 0 else 1
    half_chunks = n_out // halves
    half_depth = 2 * depth // halves
    everyone = row_n * rs

    gu_rows = gu_hbm.reshape(2 * depth, ff)

    def ow_copy(c):
        return pltpu.make_async_copy(
            ow_hbm.at[:, pl.ds(c * out_width, out_width)], ow.at[c], ow_sem
        )

    def gu_copy(c):
        return pltpu.make_async_copy(
            gu_rows.at[:, pl.ds(c * LANES, LANES)],
            gu.at[c],
            gu_sem,
        )

    staged = [
        (ids_hbm, ids_ref),
        (lens_hbm, lens_ref),
        (kvs_hbm, kvs_ref),
        (q_hbm, q_ref),
        (nk_hbm, nk_ref),
        (nv_hbm, nv_ref),
        (sk_hbm, sk_ref),
        (pk_hbm, pk_ref),
        (sv_hbm, sv_ref),
        (pv_hbm, pv_ref),
        (hid_hbm, hid_ref),
        (gain_hbm, gain_ref),
    ]
    staged = [
        pltpu.make_async_copy(source, target, in_sem.at[i])
        for i, (source, target) in enumerate(staged)
    ]
    for copy in staged:
        copy.start()
    ffs_copy = pltpu.make_async_copy(ffs_hbm, ffs, ffs_sem)

    def landed(ref, sem):
        pltpu.make_async_copy(ref, ref, sem).wait()

    barrier = pltpu.get_barrier_semaphore()
    for d in range(1, pre_n):
        pl.semaphore_signal(
            barrier,
            inc=1,
            device_id={"pre": lax.rem(pre + d, pre_n)},
            device_id_type=pl.DeviceIdType.MESH,
        )
    for d in range(1, row_n):
        pl.semaphore_signal(
            barrier,
            inc=1,
            device_id={"row": lax.rem(row + d, row_n)},
            device_id_type=pl.DeviceIdType.MESH,
        )
    def remote(src, dst, sems, axis, target):
        return pltpu.make_async_remote_copy(
            src_ref=src,
            dst_ref=dst,
            send_sem=sems[0],
            recv_sem=sems[1],
            device_id={axis: target},
            device_id_type=pl.DeviceIdType.MESH,
        )

    def pair(sem, at=0):
        return sem.at[0], sem.at[1 + at]

    def ahead(d):
        return lax.rem(pre + d, pre_n)

    def beside(d):
        return lax.rem(row + d, row_n)

    def acc_copy(d):
        return remote(acc_s.at[ahead(d)], acc_r.at[d - 1], pair(acc_sem), "pre", ahead(d))

    def stat_copy(d):
        return remote(stat_s.at[ahead(d)], stat_r.at[d - 1], pair(stat_sem), "pre", ahead(d))

    def mix_copy(d):
        return remote(mix_g.at[row], mix_g.at[row], pair(mix_sem), "row", beside(d))

    def prod_copy(c, d):
        return remote(
            prod_s.at[c, ahead(d)], prod_r.at[c, d - 1], pair(prod_sem, c), "pre", ahead(d)
        )

    def res_copy(c, d):
        block_at = res_g.at[pre, :, pl.ds(c * out_width, out_width)]
        return remote(block_at, block_at, pair(res_sem, c), "pre", ahead(d))

    def sq_copy(d):
        return remote(sq_s.at[beside(d)], sq_r.at[d - 1], pair(sq_sem), "row", beside(d))

    def gate_copy(g, d):
        return remote(
            gate_s.at[g, beside(d)], gate_r.at[g, d - 1], pair(gate_sem, g), "row", beside(d)
        )

    def per_row(ref, shape):
        which = iota(shape, 0) // STEPS
        out = jnp.full(shape, ref[0], jnp.int32)
        for r in range(1, row_local):
            out = jnp.where(which == r, ref[r], out)
        return out

    for copy in staged[:6]:
        copy.wait()
    adapter = per_row(ids_ref, (rs, 2 * adapters))
    lane = iota((rs, 2 * adapters), 1)
    pick_key = jnp.where(lane == 2 * adapter, 1.0, 0.0)
    pick_value = jnp.where(lane == 2 * adapter + 1, 1.0, 0.0)
    pick = jnp.concatenate([pick_key, pick_value], axis=0).astype(bf16)
    scales = jnp.dot(
        pick, kvs_ref[...].reshape(2 * adapters, kv_width), preferred_element_type=f32
    )
    ks8[...] = scales[:rs]
    vs8[...] = scales[rs:]
    fk8[...] = nk_ref[...].astype(f32).reshape(rs, kv_width) * scales[:rs]
    fv8[...] = nv_ref[...].astype(f32).reshape(rs, kv_width) * scales[rs:]
    q8[...] = q_ref[...].astype(f32).reshape(rs, D)

    unit_heads = min(GROUP, heads_block)
    units = heads_block // unit_heads
    unit_rows = unit_heads * rs
    suffix_rows = row_local * suffix_local
    own_rows = -(-(suffix_rows + rs) // LANES) * LANES
    pad = own_rows - suffix_rows - rs
    at_row = lax.rem(iota((unit_rows, own_rows), 0), rs)
    at_col = iota((unit_rows, own_rows), 1)
    lens = per_row(lens_ref, (rs, own_rows))
    lens = jnp.concatenate([lens] * unit_heads, axis=0)
    query_row = at_row // STEPS
    query_step = lax.rem(at_row, STEPS)
    position = pre * suffix_local + lax.rem(at_col, suffix_local)
    fresh_at = at_col - suffix_rows
    in_suffix = (at_col < suffix_rows) & (at_col // suffix_local == query_row) & (position < lens)
    in_new = (
        (fresh_at >= 0)
        & (fresh_at < rs)
        & (fresh_at // STEPS == query_row)
        & (lax.rem(fresh_at, STEPS) <= query_step)
        & (pre == 0)
    )
    mask = in_suffix | in_new
    stat_lane = iota((rs, LANES), 1)
    transposed = (((1,), (1,)), ((), ()))

    def with_fresh(old, fresh):
        tail = jnp.concatenate([fresh, jnp.zeros((pad, HD), f32)], axis=0) if pad else fresh
        return jnp.concatenate([old.reshape(suffix_rows, HD), tail.astype(bf16)], axis=0)

    def scores_of(first):
        kv = pl.ds(pl.multiple_of(first // GROUP * HD, HD), HD)
        pieces = [
            q8[:, pl.ds(pl.multiple_of((first + g) * HD, HD), HD)] for g in range(unit_heads)
        ]
        key_scale = ks8[:, kv]
        query = jnp.concatenate(pieces, axis=0).astype(bf16)
        scaled = jnp.concatenate([piece * key_scale for piece in pieces], axis=0).astype(bf16)
        own_keys = with_fresh(sk_ref[:, :, kv], fk8[:, kv])
        prefix_scores = lax.dot_general(
            scaled, pk_ref[:, kv], transposed, preferred_element_type=f32
        )
        own_scores = lax.dot_general(query, own_keys, transposed, preferred_element_type=f32)
        return prefix_scores, own_scores

    def weights_of(prefix_scores, own_scores):
        prefix_scores = prefix_scores * score_scale
        own_scores = jnp.where(mask, own_scores * score_scale, masked_score)
        peak = jnp.maximum(
            jnp.max(prefix_scores, axis=1, keepdims=True),
            jnp.max(own_scores, axis=1, keepdims=True),
        )
        prefix_weight = jnp.exp(prefix_scores - peak).astype(bf16)
        own_weight = jnp.where(mask, jnp.exp(own_scores - peak), 0.0).astype(bf16)
        total = jnp.sum(prefix_weight.astype(f32), axis=1, keepdims=True) + jnp.sum(
            own_weight.astype(f32), axis=1, keepdims=True
        )
        return peak, total, prefix_weight, own_weight

    def values_of(first, prefix_weight, own_weight):
        kv = pl.ds(pl.multiple_of(first // GROUP * HD, HD), HD)
        own_values = with_fresh(sv_ref[:, :, kv], fv8[:, kv])
        value_scale = jnp.concatenate([vs8[:, kv]] * unit_heads, axis=0)
        prefix_part = jnp.dot(prefix_weight, pv_ref[:, kv], preferred_element_type=f32)
        own_part = jnp.dot(own_weight, own_values, preferred_element_type=f32)
        return prefix_part * value_scale + own_part

    def attend(b, finish):
        firsts = [b * heads_block + i * unit_heads for i in range(units)]
        scores = [scores_of(first) for first in firsts]
        weights = [weights_of(*score) for score in scores]
        numerators = [values_of(first, *w[2:]) for first, w in zip(firsts, weights)]
        stat = jnp.ones((rs, LANES), f32)
        for i in range(units):
            for g in range(unit_heads):
                j = i * unit_heads + g
                part = slice(g * rs, (g + 1) * rs)
                stat = jnp.where(stat_lane == j, weights[i][0][part], stat)
                stat = jnp.where(stat_lane == heads_block + j, weights[i][1][part], stat)
                acc_s[b, :, j * HD : (j + 1) * HD] = numerators[i][part].astype(bf16)
        stat_s[b] = stat
        finish()

    def farthest(k):
        down = jnp.where(pre_n - 1 - k > pre, pre_n - 1 - k, pre_n - 2 - k)
        up = jnp.where(k < pre, k, k + 1)
        target = jnp.where(2 * pre < pre_n, down, up)
        return lax.rem(target - pre + pre_n, pre_n)

    for copy in staged[6:10]:
        copy.wait()
    for c in range(n_out):
        ow_copy(c).start()
    for k in range(pre_n):

        def finish(k=k):
            if k == 0:
                pl.semaphore_wait(barrier, pre_n + row_n - 2)
            if k < pre_n - 1:
                stat_copy(farthest(k)).start()
                acc_copy(farthest(k)).start()

        attend(ahead(farthest(k)) if k < pre_n - 1 else pre, finish)

    ffs_copy.start()
    for c in range(n_tiles):
        gu_copy(c).start()
    landed(stat_r, stat_sem.at[1])
    stat_of = [stat_s[pre]] + [stat_r[d - 1] for d in range(1, pre_n)]
    peak_of = [stat[:, :heads_block] for stat in stat_of]
    total_of = [stat[:, heads_block : 2 * heads_block] for stat in stat_of]
    highest = functools.reduce(jnp.maximum, peak_of)
    factor_of = [jnp.exp(peak - highest) for peak in peak_of]
    weight_sum = sum(factor * total for factor, total in zip(factor_of, total_of))
    factor_of = [factor / weight_sum for factor in factor_of]
    landed(acc_r, acc_sem.at[1])
    for j in range(heads_block):
        part = slice(j * HD, (j + 1) * HD)
        value = acc_s[pre, :, part].astype(f32) * factor_of[0][:, j : j + 1]
        for d in range(1, pre_n):
            value = value + acc_r[d - 1, :, part].astype(f32) * factor_of[d][:, j : j + 1]
        mix_g[row, :, part] = value.astype(bf16)
    for d in range(1, row_n):
        mix_copy(d).start()
    landed(ow, ow_sem)
    landed(mix_g.at[pl.ds(0, row_n - 1)], mix_sem.at[1])
    mix_x[...] = mix_g[...].astype(f32).reshape(everyone, block).astype(bf16)

    def project(c, carry):
        product = jnp.dot(mix_x[...], ow[c], preferred_element_type=f32)
        for p in range(pre_n):
            part = product[p * hs : (p + 1) * hs]
            prod_f[c, p] = part
            prod_s[c, p] = part.astype(bf16)
        for d in range(1, pre_n):
            prod_copy(c, d).start()
        return carry

    lax.fori_loop(0, n_out, project, 0)
    for copy in staged[10:]:
        copy.wait()
    for c in range(n_out):
        part = slice(c * out_width, (c + 1) * out_width)
        value = hid_ref[:, :, part].astype(f32).reshape(hs, out_width) + prod_f[c, pre]
        landed(prod_r.at[c], prod_sem.at[1 + c])
        for d in range(1, pre_n):
            value = value + prod_r[c, d - 1].astype(f32)
        res_g[pre, :, part] = value.astype(bf16)
        for d in range(1, pre_n):
            res_copy(c, d).start()
        res_out[:, :, part] = value.reshape(hid_local, STEPS, out_width).astype(bf16)
    ffs_copy.wait()
    ffn_pick = jnp.where(
        iota((rs, adapters), 1) == per_row(ids_ref, (rs, adapters)), 1.0, 0.0
    ).astype(bf16)
    ffn8[...] = jnp.dot(ffn_pick, ffs[...], preferred_element_type=f32)

    spread_from = iota((LANES, 4 * LANES), 0)
    spread_to = iota((LANES, 4 * LANES), 1)
    spread = jnp.where(
        spread_to
        == jnp.where(spread_to < 2 * LANES, 2 * spread_from, 2 * LANES + 2 * spread_from + 1),
        1.0,
        0.0,
    ).astype(bf16)

    def spread_chunk(c):
        at = slice(c * out_width, (c + 1) * out_width)
        residual = res_g[:, :, at].astype(f32).reshape(everyone, out_width)
        gain = gain_ref[at].astype(f32).reshape(1, out_width)
        normed = (residual * gain).astype(bf16)
        blocks = out_width // LANES
        stacked = jnp.concatenate(
            [normed[:, k * LANES : (k + 1) * LANES] for k in range(blocks)], axis=0
        )
        parts = jnp.dot(stacked, spread, preferred_element_type=f32).astype(bf16)
        for k in range(blocks):
            part = parts[k * everyone : (k + 1) * everyone]
            to = 2 * (c * out_width + k * LANES)
            x_exp[:everyone, to : to + 2 * LANES] = part[:, : 2 * LANES]
            x_exp[everyone:, to : to + 2 * LANES] = part[:, 2 * LANES :]
        return jnp.sum(residual * residual, axis=1, keepdims=True)

    def gather_chunks(first, last):
        for c in range(first, last):
            landed(
                res_g.at[pl.ds(0, pre_n - 1), :, pl.ds(0, out_width)], res_sem.at[1 + c]
            )
        return sum(spread_chunk(c) for c in range(first, last))

    def unit_product(g, first, last):
        at = slice(first * half_depth, last * half_depth)
        weights = [gu[g * unit_tiles + t, at] for t in range(unit_tiles)]
        weight = jnp.concatenate(weights, axis=1) if unit_tiles > 1 else weights[0]
        return jnp.dot(x_exp[:, at], weight, preferred_element_type=f32)

    def first_half(g, carry):
        gate_h[g] = unit_product(g, 0, 1)
        return carry

    def send_unit(g, product):
        for r in range(row_n):
            gate = product[r * rs : (r + 1) * rs]
            up = product[everyone + r * rs : everyone + (r + 1) * rs]
            both = jnp.concatenate([gate, up], axis=0)
            gate_f[g, r] = both
            gate_s[g, r] = both.astype(bf16)
        for d in range(1, row_n):
            gate_copy(g, d).start()

    def second_half(g, carry):
        send_unit(g, gate_h[g] + unit_product(g, 1, 2))
        return carry

    def whole_unit(g, carry):
        send_unit(g, unit_product(g, 0, halves))
        return carry

    squares = gather_chunks(0, half_chunks)
    landed(gu, gu_sem)
    if early > 0:
        lax.fori_loop(0, early, first_half, 0)
        squares = squares + gather_chunks(half_chunks, n_out)
    for r in range(row_n):
        sq_s[r] = jnp.broadcast_to(squares[r * rs : (r + 1) * rs], (rs, LANES))
    for d in range(1, row_n):
        sq_copy(d).start()
    if early > 0:
        lax.fori_loop(0, early, second_half, 0)
    for g in range(early, units_ff):
        whole_unit(g, 0)

    square_sum = sq_s[row]
    landed(sq_r, sq_sem.at[1])
    for d in range(1, row_n):
        square_sum = square_sum + sq_r[d - 1]
    inverse = lax.rsqrt(square_sum[:, :1] / D + 1e-05)

    def activate(both, at):
        gate = both[:rs] * inverse
        up = both[rs:] * inverse
        part = pl.ds(pl.multiple_of(at, LANES), unit)
        value = gate / (1.0 + jnp.exp(-gate)) * up * ffn8[:, part]
        act_out[:, :, part] = value.reshape(row_local, STEPS, unit).astype(bf16)

    def finish_unit(g, carry):
        landed(gate_r.at[g], gate_sem.at[1 + g])
        both = gate_f[g, row]
        for d in range(1, row_n):
            both = both + gate_r[g, d - 1].astype(f32)
        activate(both, g * unit)
        return carry

    lax.fori_loop(0, units_ff, finish_unit, 0)

    landed(stat_r, stat_sem.at[0])
    landed(acc_r, acc_sem.at[0])
    landed(mix_g.at[pl.ds(0, row_n - 1)], mix_sem.at[0])
    landed(prod_r, prod_sem.at[0])
    landed(res_g.at[pl.ds(0, pre_n - 1)], res_sem.at[0])
    landed(sq_r, sq_sem.at[0])
    landed(gate_r, gate_sem.at[0])


def hand_on(residual_ref, activation_ref, residual_out, activation_out, sem):
    residual = pltpu.make_async_copy(residual_ref, residual_out, sem.at[0])
    activation = pltpu.make_async_copy(activation_ref, activation_out, sem.at[1])
    residual.start()
    activation.start()
    residual.wait()
    activation.wait()


def per_device(
    queries,
    prefix_keys,
    prefix_values,
    suffix_keys,
    suffix_values,
    new_keys,
    new_values,
    hidden,
    adapter_ids,
    suffix_lengths,
    kv_scales,
    ffn_scales,
    out_weight,
    norm_gain,
    gate_up,
):
    pre_n = lax.axis_size("pre")
    row_n = lax.axis_size("row")
    row_local = queries.shape[0]
    rs = row_local * STEPS
    hs = hidden.shape[0] * STEPS
    kv_width = prefix_keys.shape[1]
    adapters, ff = ffn_scales.shape
    block, cols = out_weight.shape
    depth = gate_up.shape[0]
    out_width = min(cols, 512)
    n_out = cols // out_width
    unit = max(width for width in UNIT_WIDTHS if ff % width == 0)
    units_ff = ff // unit
    early = int(units_ff * EARLY_SHARE) if n_out % 2 == 0 else 0
    n_tiles = ff // LANES
    everyone = row_n * rs
    dma = pltpu.SemaphoreType.DMA
    vmem = pl.BlockSpec(memory_space=pltpu.VMEM)
    hbm = pl.BlockSpec(memory_space=pltpu.HBM)
    scratch = [
        pltpu.SMEM(adapter_ids.shape, jnp.int32),
        pltpu.SMEM(suffix_lengths.shape, jnp.int32),
        pltpu.VMEM(queries.shape, bf16),
        pltpu.VMEM(prefix_keys.shape, bf16),
        pltpu.VMEM(prefix_values.shape, bf16),
        pltpu.VMEM(suffix_keys.shape, bf16),
        pltpu.VMEM(suffix_values.shape, bf16),
        pltpu.VMEM(new_keys.shape, bf16),
        pltpu.VMEM(new_values.shape, bf16),
        pltpu.VMEM(hidden.shape, bf16),
        pltpu.VMEM(kv_scales.shape, bf16),
        pltpu.VMEM(norm_gain.shape, bf16),
        pltpu.VMEM((n_out, block, out_width), bf16),
        pltpu.VMEM((n_tiles, 2 * depth, LANES), bf16),
        pltpu.VMEM((adapters, ff), bf16),
        pltpu.VMEM((rs, D), f32),
        pltpu.VMEM((rs, kv_width), f32),
        pltpu.VMEM((rs, kv_width), f32),
        pltpu.VMEM((rs, kv_width), f32),
        pltpu.VMEM((rs, kv_width), f32),
        pltpu.VMEM((pre_n, rs, block), bf16),
        pltpu.VMEM((pre_n - 1, rs, block), bf16),
        pltpu.VMEM((pre_n, rs, LANES), f32),
        pltpu.VMEM((pre_n - 1, rs, LANES), f32),
        pltpu.VMEM((row_n, rs, block), bf16),
        pltpu.VMEM((everyone, block), bf16),
        pltpu.VMEM((n_out, pre_n, hs, out_width), bf16),
        pltpu.VMEM((n_out, pre_n, hs, out_width), f32),
        pltpu.VMEM((n_out, pre_n - 1, hs, out_width), bf16),
        pltpu.VMEM((pre_n, hs, cols), bf16),
        pltpu.VMEM((2 * everyone, 2 * depth), bf16),
        pltpu.VMEM((units_ff, row_n, 2 * rs, unit), bf16),
        pltpu.VMEM((units_ff, row_n, 2 * rs, unit), f32),
        pltpu.VMEM((units_ff, row_n - 1, 2 * rs, unit), bf16),
        pltpu.VMEM((max(early, 1), 2 * everyone, unit), f32),
        pltpu.VMEM((row_n, rs, LANES), f32),
        pltpu.VMEM((row_n - 1, rs, LANES), f32),
        pltpu.VMEM((rs, ff), f32),
        dma((12,)),
        dma,
        dma,
        dma,
        dma((2,)),
        dma((2,)),
        dma((2,)),
        dma((1 + n_out,)),
        dma((1 + n_out,)),
        dma((1 + units_ff,)),
        dma((2,)),
    ]
    outputs = pl.pallas_call(
        functools.partial(layer_kernel, (pre_n, row_n, units_ff, early)),
        out_shape=(
            jax.ShapeDtypeStruct(hidden.shape, bf16),
            jax.ShapeDtypeStruct((row_local, STEPS, ff), bf16),
        ),
        in_specs=[hbm] * 15,
        out_specs=(vmem, vmem),
        scratch_shapes=scratch,
        compiler_params=pltpu.CompilerParams(
            collective_id=0, has_side_effects=True, vmem_limit_bytes=GRANT * 1024 * 1024
        ),
    )(
        *(
            pltpu.with_memory_space_constraint(operand, pltpu.HBM)
            for operand in (
                adapter_ids,
                suffix_lengths,
                queries,
                prefix_keys,
                prefix_values,
                suffix_keys,
                suffix_values,
                new_keys,
                new_values,
                hidden,
                kv_scales,
                norm_gain,
                ffn_scales,
                out_weight,
                gate_up,
            )
        )
    )
    return pl.pallas_call(
        hand_on,
        out_shape=tuple(jax.ShapeDtypeStruct(value.shape, value.dtype) for value in outputs),
        in_specs=[vmem, vmem],
        out_specs=(hbm, hbm),
        scratch_shapes=[dma((2,))],
        compiler_params=pltpu.CompilerParams(vmem_limit_bytes=1024 * 1024),
    )(*outputs)


def solution(mesh):
    placed = (
        P(("grp", "row"), None, None),
        P(("grp", "pre"), None),
        P(("grp", "pre"), None),
        P(("grp", "row"), "pre", None),
        P(("grp", "row"), "pre", None),
        P(("grp", "row"), None, None),
        P(("grp", "row"), None, None),
        P(("grp", "pre"), None, "row"),
        P(("grp", "row")),
        P(("grp", "row")),
        P(),
        P(None, "pre"),
        P("pre", "row"),
        P("row"),
        P("row", None, "pre"),
    )
    return jax.shard_map(
        per_device,
        mesh=mesh,
        in_specs=placed,
        out_specs=(P(("grp", "pre"), None, "row"), P(("grp", "row"), None, "pre")),
        check_vma=False,
    )
```

```python
import functools

import jax
import jax.numpy as jnp
from jax import lax
from jax.experimental import pallas as pl
from jax.experimental.pallas import tpu as pltpu
from jax.sharding import PartitionSpec as P

D = 8192
HEADS = 64
KV_HEADS = 8
HD = 128
STEPS = 2
GROUP = HEADS // KV_HEADS
LANES = 128
UNIT_WIDTHS = (128, 256, 512)
EARLY_SHARE = 0.45

GRANT = 52

masked_score = -1e30
f32 = jnp.float32
bf16 = jnp.bfloat16


def iota(shape, axis):
    return lax.broadcasted_iota(jnp.int32, shape, axis)


def layer_kernel(
    sizes,
    ids_hbm,
    lens_hbm,
    q_hbm,
    pk_hbm,
    pv_hbm,
    sk_hbm,
    sv_hbm,
    nk_hbm,
    nv_hbm,
    hid_hbm,
    kvs_hbm,
    gain_hbm,
    ffs_hbm,
    ow_hbm,
    gu_hbm,
    res_out,
    act_out,
    ids_ref,
    lens_ref,
    q_ref,
    pk_ref,
    pv_ref,
    sk_ref,
    sv_ref,
    nk_ref,
    nv_ref,
    hid_ref,
    kvs_ref,
    gain_ref,
    ow,
    gu,
    ffs,
    q8,
    ks8,
    vs8,
    fk8,
    fv8,
    acc_s,
    acc_r,
    stat_s,
    stat_r,
    mix_g,
    mix_x,
    prod_s,
    prod_f,
    prod_r,
    res_g,
    x_exp,
    gate_s,
    gate_f,
    gate_r,
    gate_h,
    sq_s,
    sq_r,
    ffn8,
    in_sem,
    ow_sem,
    gu_sem,
    ffs_sem,
    acc_sem,
    stat_sem,
    mix_sem,
    prod_sem,
    res_sem,
    gate_sem,
    sq_sem,
):
    pre_n, row_n, units_ff, early = sizes
    pre = lax.axis_index("pre")
    row = lax.axis_index("row")
    row_local = q_hbm.shape[0]
    rs = row_local * STEPS
    hid_local = hid_ref.shape[0]
    hs = hid_local * STEPS
    suffix_local = sk_ref.shape[1]
    kv_width = pk_ref.shape[1]
    adapters = kvs_ref.shape[0]
    block = D // pre_n
    heads_block = block // HD
    cols = ow_hbm.shape[1]
    depth = gu_hbm.shape[0]
    ff = gu_hbm.shape[2]
    score_scale = HD ** (-0.5)
    n_out, _, out_width = ow.shape
    n_tiles = gu.shape[0]
    unit = gate_s.shape[3]
    unit_tiles = unit // LANES
    halves = 2 if n_out % 2 == 0 else 1
    half_chunks = n_out // halves
    half_depth = 2 * depth // halves
    everyone = row_n * rs

    gu_rows = gu_hbm.reshape(2 * depth, ff)

    def ow_copy(c):
        return pltpu.make_async_copy(
            ow_hbm.at[:, pl.ds(c * out_width, out_width)], ow.at[c], ow_sem
        )

    def gu_copy(c):
        return pltpu.make_async_copy(
            gu_rows.at[:, pl.ds(c * LANES, LANES)],
            gu.at[c],
            gu_sem,
        )

    staged = [
        (ids_hbm, ids_ref),
        (lens_hbm, lens_ref),
        (kvs_hbm, kvs_ref),
        (q_hbm, q_ref),
        (nk_hbm, nk_ref),
        (nv_hbm, nv_ref),
        (sk_hbm, sk_ref),
        (pk_hbm, pk_ref),
        (sv_hbm, sv_ref),
        (pv_hbm, pv_ref),
        (hid_hbm, hid_ref),
        (gain_hbm, gain_ref),
    ]
    staged = [
        pltpu.make_async_copy(source, target, in_sem.at[i])
        for i, (source, target) in enumerate(staged)
    ]
    for copy in staged:
        copy.start()
    ffs_copy = pltpu.make_async_copy(ffs_hbm, ffs, ffs_sem)

    def landed(ref, sem):
        pltpu.make_async_copy(ref, ref, sem).wait()

    barrier = pltpu.get_barrier_semaphore()
    for d in range(1, pre_n):
        pl.semaphore_signal(
            barrier,
            inc=1,
            device_id={"pre": lax.rem(pre + d, pre_n)},
            device_id_type=pl.DeviceIdType.MESH,
        )
    for d in range(1, row_n):
        pl.semaphore_signal(
            barrier,
            inc=1,
            device_id={"row": lax.rem(row + d, row_n)},
            device_id_type=pl.DeviceIdType.MESH,
        )
    def remote(src, dst, sems, axis, target):
        return pltpu.make_async_remote_copy(
            src_ref=src,
            dst_ref=dst,
            send_sem=sems[0],
            recv_sem=sems[1],
            device_id={axis: target},
            device_id_type=pl.DeviceIdType.MESH,
        )

    def pair(sem, at=0):
        return sem.at[0], sem.at[1 + at]

    def ahead(d):
        return lax.rem(pre + d, pre_n)

    def beside(d):
        return lax.rem(row + d, row_n)

    def farthest(at, count):
        order = []
        for k in range(count - 1):
            down = jnp.where(count - 1 - k > at, count - 1 - k, count - 2 - k)
            up = jnp.where(k < at, k, k + 1)
            target = jnp.where(2 * at < count, down, up)
            order.append(lax.rem(target - at + count, count))
        return order

    far_pre = farthest(pre, pre_n)
    far_row = farthest(row, row_n)

    def acc_copy(d):
        return remote(acc_s.at[ahead(d)], acc_r.at[d - 1], pair(acc_sem), "pre", ahead(d))

    def stat_copy(d):
        return remote(stat_s.at[ahead(d)], stat_r.at[d - 1], pair(stat_sem), "pre", ahead(d))

    def mix_copy(d):
        return remote(mix_g.at[row], mix_g.at[row], pair(mix_sem), "row", beside(d))

    def prod_copy(c, d):
        return remote(
            prod_s.at[c, ahead(d)], prod_r.at[c, d - 1], pair(prod_sem, c), "pre", ahead(d)
        )

    def res_copy(c, d):
        block_at = res_g.at[pre, :, pl.ds(c * out_width, out_width)]
        return remote(block_at, block_at, pair(res_sem, c), "pre", ahead(d))

    def sq_copy(d):
        return remote(sq_s.at[beside(d)], sq_r.at[d - 1], pair(sq_sem), "row", beside(d))

    def gate_copy(g, d):
        return remote(
            gate_s.at[g, beside(d)], gate_r.at[g, d - 1], pair(gate_sem, g), "row", beside(d)
        )

    def per_row(ref, shape):
        which = iota(shape, 0) // STEPS
        out = jnp.full(shape, ref[0], jnp.int32)
        for r in range(1, row_local):
            out = jnp.where(which == r, ref[r], out)
        return out

    for copy in staged[:6]:
        copy.wait()
    adapter = per_row(ids_ref, (rs, 2 * adapters))
    lane = iota((rs, 2 * adapters), 1)
    pick_key = jnp.where(lane == 2 * adapter, 1.0, 0.0)
    pick_value = jnp.where(lane == 2 * adapter + 1, 1.0, 0.0)
    pick = jnp.concatenate([pick_key, pick_value], axis=0).astype(bf16)
    scales = jnp.dot(
        pick, kvs_ref[...].reshape(2 * adapters, kv_width), preferred_element_type=f32
    )
    ks8[...] = scales[:rs]
    vs8[...] = scales[rs:]
    fk8[...] = nk_ref[...].astype(f32).reshape(rs, kv_width) * scales[:rs]
    fv8[...] = nv_ref[...].astype(f32).reshape(rs, kv_width) * scales[rs:]
    q8[...] = q_ref[...].astype(f32).reshape(rs, D)

    unit_heads = min(GROUP, heads_block)
    units = heads_block // unit_heads
    unit_rows = unit_heads * rs
    suffix_rows = row_local * suffix_local
    own_rows = -(-(suffix_rows + rs) // LANES) * LANES
    pad = own_rows - suffix_rows - rs
    at_row = lax.rem(iota((unit_rows, own_rows), 0), rs)
    at_col = iota((unit_rows, own_rows), 1)
    lens = per_row(lens_ref, (rs, own_rows))
    lens = jnp.concatenate([lens] * unit_heads, axis=0)
    query_row = at_row // STEPS
    query_step = lax.rem(at_row, STEPS)
    position = pre * suffix_local + lax.rem(at_col, suffix_local)
    fresh_at = at_col - suffix_rows
    in_suffix = (at_col < suffix_rows) & (at_col // suffix_local == query_row) & (position < lens)
    in_new = (
        (fresh_at >= 0)
        & (fresh_at < rs)
        & (fresh_at // STEPS == query_row)
        & (lax.rem(fresh_at, STEPS) <= query_step)
        & (pre == 0)
    )
    mask = in_suffix | in_new
    stat_lane = iota((rs, LANES), 1)
    transposed = (((1,), (1,)), ((), ()))

    def with_fresh(old, fresh):
        tail = jnp.concatenate([fresh, jnp.zeros((pad, HD), f32)], axis=0) if pad else fresh
        return jnp.concatenate([old.reshape(suffix_rows, HD), tail.astype(bf16)], axis=0)

    def scores_of(first):
        kv = pl.ds(pl.multiple_of(first // GROUP * HD, HD), HD)
        pieces = [
            q8[:, pl.ds(pl.multiple_of((first + g) * HD, HD), HD)] for g in range(unit_heads)
        ]
        key_scale = ks8[:, kv]
        query = jnp.concatenate(pieces, axis=0).astype(bf16)
        scaled = jnp.concatenate([piece * key_scale for piece in pieces], axis=0).astype(bf16)
        own_keys = with_fresh(sk_ref[:, :, kv], fk8[:, kv])
        prefix_scores = lax.dot_general(
            scaled, pk_ref[:, kv], transposed, preferred_element_type=f32
        )
        own_scores = lax.dot_general(query, own_keys, transposed, preferred_element_type=f32)
        return prefix_scores, own_scores

    def weights_of(prefix_scores, own_scores):
        prefix_scores = prefix_scores * score_scale
        own_scores = jnp.where(mask, own_scores * score_scale, masked_score)
        peak = jnp.maximum(
            jnp.max(prefix_scores, axis=1, keepdims=True),
            jnp.max(own_scores, axis=1, keepdims=True),
        )
        prefix_weight = jnp.exp(prefix_scores - peak).astype(bf16)
        own_weight = jnp.where(mask, jnp.exp(own_scores - peak), 0.0).astype(bf16)
        total = jnp.sum(prefix_weight.astype(f32), axis=1, keepdims=True) + jnp.sum(
            own_weight.astype(f32), axis=1, keepdims=True
        )
        return peak, total, prefix_weight, own_weight

    def values_of(first, prefix_weight, own_weight):
        kv = pl.ds(pl.multiple_of(first // GROUP * HD, HD), HD)
        own_values = with_fresh(sv_ref[:, :, kv], fv8[:, kv])
        value_scale = jnp.concatenate([vs8[:, kv]] * unit_heads, axis=0)
        prefix_part = jnp.dot(prefix_weight, pv_ref[:, kv], preferred_element_type=f32)
        own_part = jnp.dot(own_weight, own_values, preferred_element_type=f32)
        return prefix_part * value_scale + own_part

    def attend(b, finish):
        firsts = [b * heads_block + i * unit_heads for i in range(units)]
        scores = [scores_of(first) for first in firsts]
        weights = [weights_of(*score) for score in scores]
        numerators = [values_of(first, *w[2:]) for first, w in zip(firsts, weights)]
        stat = jnp.ones((rs, LANES), f32)
        for i in range(units):
            for g in range(unit_heads):
                j = i * unit_heads + g
                part = slice(g * rs, (g + 1) * rs)
                stat = jnp.where(stat_lane == j, weights[i][0][part], stat)
                stat = jnp.where(stat_lane == heads_block + j, weights[i][1][part], stat)
                acc_s[b, :, j * HD : (j + 1) * HD] = numerators[i][part].astype(bf16)
        stat_s[b] = stat
        finish()

    for copy in staged[6:10]:
        copy.wait()
    for c in range(n_out):
        ow_copy(c).start()
    for k in range(pre_n):

        def finish(k=k):
            if k == 0:
                pl.semaphore_wait(barrier, pre_n + row_n - 2)
            if k < pre_n - 1:
                stat_copy(far_pre[k]).start()
                acc_copy(far_pre[k]).start()

        attend(ahead(far_pre[k]) if k < pre_n - 1 else pre, finish)

    ffs_copy.start()
    for c in range(n_tiles):
        gu_copy(c).start()
    landed(stat_r, stat_sem.at[1])
    stat_of = [stat_s[pre]] + [stat_r[d - 1] for d in range(1, pre_n)]
    peak_of = [stat[:, :heads_block] for stat in stat_of]
    total_of = [stat[:, heads_block : 2 * heads_block] for stat in stat_of]
    highest = functools.reduce(jnp.maximum, peak_of)
    factor_of = [jnp.exp(peak - highest) for peak in peak_of]
    weight_sum = sum(factor * total for factor, total in zip(factor_of, total_of))
    factor_of = [factor / weight_sum for factor in factor_of]
    landed(acc_r, acc_sem.at[1])
    for j in range(heads_block):
        part = slice(j * HD, (j + 1) * HD)
        value = acc_s[pre, :, part].astype(f32) * factor_of[0][:, j : j + 1]
        for d in range(1, pre_n):
            value = value + acc_r[d - 1, :, part].astype(f32) * factor_of[d][:, j : j + 1]
        mix_g[row, :, part] = value.astype(bf16)
    for d in far_row:
        mix_copy(d).start()
    landed(ow, ow_sem)
    landed(mix_g.at[pl.ds(0, row_n - 1)], mix_sem.at[1])
    mix_x[...] = mix_g[...].astype(f32).reshape(everyone, block).astype(bf16)

    def project(c, carry):
        product = jnp.dot(mix_x[...], ow[c], preferred_element_type=f32)
        for p in range(pre_n):
            part = product[p * hs : (p + 1) * hs]
            prod_f[c, p] = part
            prod_s[c, p] = part.astype(bf16)
        for d in far_pre:
            prod_copy(c, d).start()
        return carry

    lax.fori_loop(0, n_out, project, 0)
    for copy in staged[10:]:
        copy.wait()
    for c in range(n_out):
        part = slice(c * out_width, (c + 1) * out_width)
        value = hid_ref[:, :, part].astype(f32).reshape(hs, out_width) + prod_f[c, pre]
        landed(prod_r.at[c], prod_sem.at[1 + c])
        for d in range(1, pre_n):
            value = value + prod_r[c, d - 1].astype(f32)
        res_g[pre, :, part] = value.astype(bf16)
        for d in far_pre:
            res_copy(c, d).start()
        res_out[:, :, part] = value.reshape(hid_local, STEPS, out_width).astype(bf16)
    ffs_copy.wait()
    ffn_pick = jnp.where(
        iota((rs, adapters), 1) == per_row(ids_ref, (rs, adapters)), 1.0, 0.0
    ).astype(bf16)
    ffn8[...] = jnp.dot(ffn_pick, ffs[...], preferred_element_type=f32)

    spread_from = iota((LANES, 4 * LANES), 0)
    spread_to = iota((LANES, 4 * LANES), 1)
    spread = jnp.where(
        spread_to
        == jnp.where(spread_to < 2 * LANES, 2 * spread_from, 2 * LANES + 2 * spread_from + 1),
        1.0,
        0.0,
    ).astype(bf16)

    def spread_chunk(c):
        at = slice(c * out_width, (c + 1) * out_width)
        residual = res_g[:, :, at].astype(f32).reshape(everyone, out_width)
        gain = gain_ref[at].astype(f32).reshape(1, out_width)
        normed = (residual * gain).astype(bf16)
        blocks = out_width // LANES
        stacked = jnp.concatenate(
            [normed[:, k * LANES : (k + 1) * LANES] for k in range(blocks)], axis=0
        )
        parts = jnp.dot(stacked, spread, preferred_element_type=f32).astype(bf16)
        for k in range(blocks):
            part = parts[k * everyone : (k + 1) * everyone]
            to = 2 * (c * out_width + k * LANES)
            x_exp[:everyone, to : to + 2 * LANES] = part[:, : 2 * LANES]
            x_exp[everyone:, to : to + 2 * LANES] = part[:, 2 * LANES :]
        return jnp.sum(residual * residual, axis=1, keepdims=True)

    def gather_chunks(first, last):
        for c in range(first, last):
            landed(
                res_g.at[pl.ds(0, pre_n - 1), :, pl.ds(0, out_width)], res_sem.at[1 + c]
            )
        return sum(spread_chunk(c) for c in range(first, last))

    def unit_product(g, first, last):
        at = slice(first * half_depth, last * half_depth)
        weights = [gu[g * unit_tiles + t, at] for t in range(unit_tiles)]
        weight = jnp.concatenate(weights, axis=1) if unit_tiles > 1 else weights[0]
        return jnp.dot(x_exp[:, at], weight, preferred_element_type=f32)

    def first_half(g, carry):
        gate_h[g] = unit_product(g, 0, 1)
        return carry

    def send_unit(g, product):
        for r in range(row_n):
            gate = product[r * rs : (r + 1) * rs]
            up = product[everyone + r * rs : everyone + (r + 1) * rs]
            both = jnp.concatenate([gate, up], axis=0)
            gate_f[g, r] = both
            gate_s[g, r] = both.astype(bf16)
        for d in far_row:
            gate_copy(g, d).start()

    def second_half(g, carry):
        send_unit(g, gate_h[g] + unit_product(g, 1, 2))
        return carry

    def whole_unit(g, carry):
        send_unit(g, unit_product(g, 0, halves))
        return carry

    squares = gather_chunks(0, half_chunks)
    landed(gu, gu_sem)
    if early > 0:
        lax.fori_loop(0, early, first_half, 0)
        squares = squares + gather_chunks(half_chunks, n_out)
    for r in range(row_n):
        sq_s[r] = jnp.broadcast_to(squares[r * rs : (r + 1) * rs], (rs, LANES))
    for d in range(1, row_n):
        sq_copy(d).start()
    if early > 0:
        lax.fori_loop(0, early, second_half, 0)
    for g in range(early, units_ff):
        whole_unit(g, 0)

    square_sum = sq_s[row]
    landed(sq_r, sq_sem.at[1])
    for d in range(1, row_n):
        square_sum = square_sum + sq_r[d - 1]
    inverse = lax.rsqrt(square_sum[:, :1] / D + 1e-05)

    def activate(both, at):
        gate = both[:rs] * inverse
        up = both[rs:] * inverse
        part = pl.ds(pl.multiple_of(at, LANES), unit)
        value = gate / (1.0 + jnp.exp(-gate)) * up * ffn8[:, part]
        act_out[:, :, part] = value.reshape(row_local, STEPS, unit).astype(bf16)

    def finish_unit(g, carry):
        landed(gate_r.at[g], gate_sem.at[1 + g])
        both = gate_f[g, row]
        for d in range(1, row_n):
            both = both + gate_r[g, d - 1].astype(f32)
        activate(both, g * unit)
        return carry

    lax.fori_loop(0, units_ff, finish_unit, 0)

    landed(stat_r, stat_sem.at[0])
    landed(acc_r, acc_sem.at[0])
    landed(mix_g.at[pl.ds(0, row_n - 1)], mix_sem.at[0])
    landed(prod_r, prod_sem.at[0])
    landed(res_g.at[pl.ds(0, pre_n - 1)], res_sem.at[0])
    landed(sq_r, sq_sem.at[0])
    landed(gate_r, gate_sem.at[0])


def hand_on(residual_ref, activation_ref, residual_out, activation_out, sem):
    residual = pltpu.make_async_copy(residual_ref, residual_out, sem.at[0])
    activation = pltpu.make_async_copy(activation_ref, activation_out, sem.at[1])
    residual.start()
    activation.start()
    residual.wait()
    activation.wait()


def per_device(
    queries,
    prefix_keys,
    prefix_values,
    suffix_keys,
    suffix_values,
    new_keys,
    new_values,
    hidden,
    adapter_ids,
    suffix_lengths,
    kv_scales,
    ffn_scales,
    out_weight,
    norm_gain,
    gate_up,
):
    pre_n = lax.axis_size("pre")
    row_n = lax.axis_size("row")
    row_local = queries.shape[0]
    rs = row_local * STEPS
    hs = hidden.shape[0] * STEPS
    kv_width = prefix_keys.shape[1]
    adapters, ff = ffn_scales.shape
    block, cols = out_weight.shape
    depth = gate_up.shape[0]
    out_width = min(cols, 512)
    n_out = cols // out_width
    unit = max(width for width in UNIT_WIDTHS if ff % width == 0)
    units_ff = ff // unit
    early = int(units_ff * EARLY_SHARE) if n_out % 2 == 0 else 0
    n_tiles = ff // LANES
    everyone = row_n * rs
    dma = pltpu.SemaphoreType.DMA
    vmem = pl.BlockSpec(memory_space=pltpu.VMEM)
    hbm = pl.BlockSpec(memory_space=pltpu.HBM)
    scratch = [
        pltpu.SMEM(adapter_ids.shape, jnp.int32),
        pltpu.SMEM(suffix_lengths.shape, jnp.int32),
        pltpu.VMEM(queries.shape, bf16),
        pltpu.VMEM(prefix_keys.shape, bf16),
        pltpu.VMEM(prefix_values.shape, bf16),
        pltpu.VMEM(suffix_keys.shape, bf16),
        pltpu.VMEM(suffix_values.shape, bf16),
        pltpu.VMEM(new_keys.shape, bf16),
        pltpu.VMEM(new_values.shape, bf16),
        pltpu.VMEM(hidden.shape, bf16),
        pltpu.VMEM(kv_scales.shape, bf16),
        pltpu.VMEM(norm_gain.shape, bf16),
        pltpu.VMEM((n_out, block, out_width), bf16),
        pltpu.VMEM((n_tiles, 2 * depth, LANES), bf16),
        pltpu.VMEM((adapters, ff), bf16),
        pltpu.VMEM((rs, D), f32),
        pltpu.VMEM((rs, kv_width), f32),
        pltpu.VMEM((rs, kv_width), f32),
        pltpu.VMEM((rs, kv_width), f32),
        pltpu.VMEM((rs, kv_width), f32),
        pltpu.VMEM((pre_n, rs, block), bf16),
        pltpu.VMEM((pre_n - 1, rs, block), bf16),
        pltpu.VMEM((pre_n, rs, LANES), f32),
        pltpu.VMEM((pre_n - 1, rs, LANES), f32),
        pltpu.VMEM((row_n, rs, block), bf16),
        pltpu.VMEM((everyone, block), bf16),
        pltpu.VMEM((n_out, pre_n, hs, out_width), bf16),
        pltpu.VMEM((n_out, pre_n, hs, out_width), f32),
        pltpu.VMEM((n_out, pre_n - 1, hs, out_width), bf16),
        pltpu.VMEM((pre_n, hs, cols), bf16),
        pltpu.VMEM((2 * everyone, 2 * depth), bf16),
        pltpu.VMEM((units_ff, row_n, 2 * rs, unit), bf16),
        pltpu.VMEM((units_ff, row_n, 2 * rs, unit), f32),
        pltpu.VMEM((units_ff, row_n - 1, 2 * rs, unit), bf16),
        pltpu.VMEM((max(early, 1), 2 * everyone, unit), f32),
        pltpu.VMEM((row_n, rs, LANES), f32),
        pltpu.VMEM((row_n - 1, rs, LANES), f32),
        pltpu.VMEM((rs, ff), f32),
        dma((12,)),
        dma,
        dma,
        dma,
        dma((2,)),
        dma((2,)),
        dma((2,)),
        dma((1 + n_out,)),
        dma((1 + n_out,)),
        dma((1 + units_ff,)),
        dma((2,)),
    ]
    outputs = pl.pallas_call(
        functools.partial(layer_kernel, (pre_n, row_n, units_ff, early)),
        out_shape=(
            jax.ShapeDtypeStruct(hidden.shape, bf16),
            jax.ShapeDtypeStruct((row_local, STEPS, ff), bf16),
        ),
        in_specs=[hbm] * 15,
        out_specs=(vmem, vmem),
        scratch_shapes=scratch,
        compiler_params=pltpu.CompilerParams(
            collective_id=0, has_side_effects=True, vmem_limit_bytes=GRANT * 1024 * 1024
        ),
    )(
        *(
            pltpu.with_memory_space_constraint(operand, pltpu.HBM)
            for operand in (
                adapter_ids,
                suffix_lengths,
                queries,
                prefix_keys,
                prefix_values,
                suffix_keys,
                suffix_values,
                new_keys,
                new_values,
                hidden,
                kv_scales,
                norm_gain,
                ffn_scales,
                out_weight,
                gate_up,
            )
        )
    )
    return pl.pallas_call(
        hand_on,
        out_shape=tuple(jax.ShapeDtypeStruct(value.shape, value.dtype) for value in outputs),
        in_specs=[vmem, vmem],
        out_specs=(hbm, hbm),
        scratch_shapes=[dma((2,))],
        compiler_params=pltpu.CompilerParams(vmem_limit_bytes=1024 * 1024),
    )(*outputs)


def solution(mesh):
    placed = (
        P(("grp", "row"), None, None),
        P(("grp", "pre"), None),
        P(("grp", "pre"), None),
        P(("grp", "row"), "pre", None),
        P(("grp", "row"), "pre", None),
        P(("grp", "row"), None, None),
        P(("grp", "row"), None, None),
        P(("grp", "pre"), None, "row"),
        P(("grp", "row")),
        P(("grp", "row")),
        P(),
        P(None, "pre"),
        P("pre", "row"),
        P("row"),
        P("row", None, "pre"),
    )
    return jax.shard_map(
        per_device,
        mesh=mesh,
        in_specs=placed,
        out_specs=(P(("grp", "pre"), None, "row"), P(("grp", "row"), None, "pre")),
        check_vma=False,
    )
```

```python
import functools

import jax
import jax.numpy as jnp
from jax import lax
from jax.experimental import pallas as pl
from jax.experimental.pallas import tpu as pltpu
from jax.sharding import PartitionSpec as P

D = 8192
HEADS = 64
KV_HEADS = 8
HD = 128
STEPS = 2
GROUP = HEADS // KV_HEADS
LANES = 128
UNIT_WIDTHS = (128, 256, 512)
EARLY_SHARE = 0.45

GRANT = 52

masked_score = -1e30
f32 = jnp.float32
bf16 = jnp.bfloat16


def iota(shape, axis):
    return lax.broadcasted_iota(jnp.int32, shape, axis)


def layer_kernel(
    sizes,
    ids_hbm,
    lens_hbm,
    q_hbm,
    pk_hbm,
    pv_hbm,
    sk_hbm,
    sv_hbm,
    nk_hbm,
    nv_hbm,
    hid_hbm,
    kvs_hbm,
    gain_hbm,
    ffs_hbm,
    ow_hbm,
    gu_hbm,
    res_out,
    act_out,
    ids_ref,
    lens_ref,
    q_ref,
    pk_ref,
    pv_ref,
    sk_ref,
    sv_ref,
    nk_ref,
    nv_ref,
    hid_ref,
    kvs_ref,
    gain_ref,
    ow,
    gu,
    ffs,
    q8,
    ks8,
    vs8,
    fk8,
    fv8,
    acc_s,
    acc_r,
    stat_s,
    stat_r,
    mix_g,
    mix_x,
    prod_s,
    prod_f,
    prod_r,
    res_g,
    x_exp,
    gate_s,
    gate_f,
    gate_r,
    gate_h,
    sq_s,
    sq_r,
    ffn8,
    in_sem,
    ow_sem,
    gu_sem,
    ffs_sem,
    acc_sem,
    stat_sem,
    mix_sem,
    prod_sem,
    res_sem,
    gate_sem,
    sq_sem,
):
    pre_n, row_n, units_ff, early = sizes
    pre = lax.axis_index("pre")
    row = lax.axis_index("row")
    row_local = q_hbm.shape[0]
    rs = row_local * STEPS
    hid_local = hid_ref.shape[0]
    hs = hid_local * STEPS
    suffix_local = sk_ref.shape[1]
    kv_width = pk_ref.shape[1]
    adapters = kvs_ref.shape[0]
    block = D // pre_n
    heads_block = block // HD
    cols = ow_hbm.shape[1]
    depth = gu_hbm.shape[0]
    ff = gu_hbm.shape[2]
    score_scale = HD ** (-0.5)
    n_out, _, out_width = ow.shape
    n_tiles = gu.shape[0]
    unit = gate_s.shape[3]
    unit_tiles = unit // LANES
    halves = 2 if n_out % 2 == 0 else 1
    half_chunks = n_out // halves
    half_depth = 2 * depth // halves
    everyone = row_n * rs

    gu_rows = gu_hbm.reshape(2 * depth, ff)

    def ow_copy(c):
        return pltpu.make_async_copy(
            ow_hbm.at[:, pl.ds(c * out_width, out_width)], ow.at[c], ow_sem
        )

    def gu_copy(c):
        return pltpu.make_async_copy(
            gu_rows.at[:, pl.ds(c * LANES, LANES)],
            gu.at[c],
            gu_sem,
        )

    staged = [
        (ids_hbm, ids_ref),
        (lens_hbm, lens_ref),
        (kvs_hbm, kvs_ref),
        (q_hbm, q_ref),
        (nk_hbm, nk_ref),
        (nv_hbm, nv_ref),
        (sk_hbm, sk_ref),
        (pk_hbm, pk_ref),
        (sv_hbm, sv_ref),
        (pv_hbm, pv_ref),
        (hid_hbm, hid_ref),
        (gain_hbm, gain_ref),
    ]
    staged = [
        pltpu.make_async_copy(source, target, in_sem.at[i])
        for i, (source, target) in enumerate(staged)
    ]
    for copy in staged:
        copy.start()
    ffs_copy = pltpu.make_async_copy(ffs_hbm, ffs, ffs_sem)

    def landed(ref, sem):
        pltpu.make_async_copy(ref, ref, sem).wait()

    barrier = pltpu.get_barrier_semaphore()
    for d in range(1, pre_n):
        pl.semaphore_signal(
            barrier,
            inc=1,
            device_id={"pre": lax.rem(pre + d, pre_n)},
            device_id_type=pl.DeviceIdType.MESH,
        )
    for d in range(1, row_n):
        pl.semaphore_signal(
            barrier,
            inc=1,
            device_id={"row": lax.rem(row + d, row_n)},
            device_id_type=pl.DeviceIdType.MESH,
        )
    def remote(src, dst, sems, axis, target):
        return pltpu.make_async_remote_copy(
            src_ref=src,
            dst_ref=dst,
            send_sem=sems[0],
            recv_sem=sems[1],
            device_id={axis: target},
            device_id_type=pl.DeviceIdType.MESH,
        )

    def pair(sem, at=0):
        return sem.at[0], sem.at[1 + at]

    def ahead(d):
        return lax.rem(pre + d, pre_n)

    def beside(d):
        return lax.rem(row + d, row_n)

    def farthest(at, count):
        order = []
        for k in range(count - 1):
            down = jnp.where(count - 1 - k > at, count - 1 - k, count - 2 - k)
            up = jnp.where(k < at, k, k + 1)
            target = jnp.where(2 * at < count, down, up)
            order.append(lax.rem(target - at + count, count))
        return order

    far_pre = farthest(pre, pre_n)
    far_row = farthest(row, row_n)

    def acc_copy(d):
        return remote(acc_s.at[ahead(d)], acc_r.at[d - 1], pair(acc_sem), "pre", ahead(d))

    def stat_copy(d):
        return remote(stat_s.at[ahead(d)], stat_r.at[d - 1], pair(stat_sem), "pre", ahead(d))

    def mix_copy(d):
        return remote(mix_g.at[row], mix_g.at[row], pair(mix_sem), "row", beside(d))

    def prod_copy(c, d):
        return remote(
            prod_s.at[c, ahead(d)], prod_r.at[c, d - 1], pair(prod_sem, c), "pre", ahead(d)
        )

    def res_copy(c, d):
        block_at = res_g.at[pre, :, pl.ds(c * out_width, out_width)]
        return remote(block_at, block_at, pair(res_sem, c), "pre", ahead(d))

    def sq_copy(d):
        return remote(sq_s.at[beside(d)], sq_r.at[d - 1], pair(sq_sem), "row", beside(d))

    def gate_copy(g, d):
        return remote(
            gate_s.at[g, beside(d)], gate_r.at[g, d - 1], pair(gate_sem, g), "row", beside(d)
        )

    def per_row(ref, shape):
        which = iota(shape, 0) // STEPS
        out = jnp.full(shape, ref[0], jnp.int32)
        for r in range(1, row_local):
            out = jnp.where(which == r, ref[r], out)
        return out

    for copy in staged[:6]:
        copy.wait()
    adapter = per_row(ids_ref, (rs, 2 * adapters))
    lane = iota((rs, 2 * adapters), 1)
    pick_key = jnp.where(lane == 2 * adapter, 1.0, 0.0)
    pick_value = jnp.where(lane == 2 * adapter + 1, 1.0, 0.0)
    pick = jnp.concatenate([pick_key, pick_value], axis=0).astype(bf16)
    scales = jnp.dot(
        pick, kvs_ref[...].reshape(2 * adapters, kv_width), preferred_element_type=f32
    )
    ks8[...] = scales[:rs]
    vs8[...] = scales[rs:]
    fk8[...] = nk_ref[...].astype(f32).reshape(rs, kv_width) * scales[:rs]
    fv8[...] = nv_ref[...].astype(f32).reshape(rs, kv_width) * scales[rs:]
    q8[...] = q_ref[...].astype(f32).reshape(rs, D)

    unit_heads = min(GROUP, heads_block)
    units = heads_block // unit_heads
    unit_rows = unit_heads * rs
    suffix_rows = row_local * suffix_local
    own_rows = -(-(suffix_rows + rs) // LANES) * LANES
    pad = own_rows - suffix_rows - rs
    at_row = lax.rem(iota((unit_rows, own_rows), 0), rs)
    at_col = iota((unit_rows, own_rows), 1)
    lens = per_row(lens_ref, (rs, own_rows))
    lens = jnp.concatenate([lens] * unit_heads, axis=0)
    query_row = at_row // STEPS
    query_step = lax.rem(at_row, STEPS)
    position = pre * suffix_local + lax.rem(at_col, suffix_local)
    fresh_at = at_col - suffix_rows
    in_suffix = (at_col < suffix_rows) & (at_col // suffix_local == query_row) & (position < lens)
    in_new = (
        (fresh_at >= 0)
        & (fresh_at < rs)
        & (fresh_at // STEPS == query_row)
        & (lax.rem(fresh_at, STEPS) <= query_step)
        & (pre == 0)
    )
    mask = in_suffix | in_new
    stat_lane = iota((rs, LANES), 1)
    transposed = (((1,), (1,)), ((), ()))

    def with_fresh(old, fresh):
        tail = jnp.concatenate([fresh, jnp.zeros((pad, HD), f32)], axis=0) if pad else fresh
        return jnp.concatenate([old.reshape(suffix_rows, HD), tail.astype(bf16)], axis=0)

    def scores_of(first):
        kv = pl.ds(pl.multiple_of(first // GROUP * HD, HD), HD)
        pieces = [
            q8[:, pl.ds(pl.multiple_of((first + g) * HD, HD), HD)] for g in range(unit_heads)
        ]
        key_scale = ks8[:, kv]
        query = jnp.concatenate(pieces, axis=0).astype(bf16)
        scaled = jnp.concatenate([piece * key_scale for piece in pieces], axis=0).astype(bf16)
        own_keys = with_fresh(sk_ref[:, :, kv], fk8[:, kv])
        prefix_scores = lax.dot_general(
            scaled, pk_ref[:, kv], transposed, preferred_element_type=f32
        )
        own_scores = lax.dot_general(query, own_keys, transposed, preferred_element_type=f32)
        return prefix_scores, own_scores

    def weights_of(prefix_scores, own_scores):
        prefix_scores = prefix_scores * score_scale
        own_scores = jnp.where(mask, own_scores * score_scale, masked_score)
        peak = jnp.maximum(
            jnp.max(prefix_scores, axis=1, keepdims=True),
            jnp.max(own_scores, axis=1, keepdims=True),
        )
        prefix_weight = jnp.exp(prefix_scores - peak).astype(bf16)
        own_weight = jnp.where(mask, jnp.exp(own_scores - peak), 0.0).astype(bf16)
        total = jnp.sum(prefix_weight.astype(f32), axis=1, keepdims=True) + jnp.sum(
            own_weight.astype(f32), axis=1, keepdims=True
        )
        return peak, total, prefix_weight, own_weight

    def values_of(first, prefix_weight, own_weight):
        kv = pl.ds(pl.multiple_of(first // GROUP * HD, HD), HD)
        own_values = with_fresh(sv_ref[:, :, kv], fv8[:, kv])
        value_scale = jnp.concatenate([vs8[:, kv]] * unit_heads, axis=0)
        prefix_part = jnp.dot(prefix_weight, pv_ref[:, kv], preferred_element_type=f32)
        own_part = jnp.dot(own_weight, own_values, preferred_element_type=f32)
        return prefix_part * value_scale + own_part

    def attend(b, finish):
        firsts = [b * heads_block + i * unit_heads for i in range(units)]
        scores = [scores_of(first) for first in firsts]
        weights = [weights_of(*score) for score in scores]
        numerators = [values_of(first, *w[2:]) for first, w in zip(firsts, weights)]
        stat = jnp.ones((rs, LANES), f32)
        for i in range(units):
            for g in range(unit_heads):
                j = i * unit_heads + g
                part = slice(g * rs, (g + 1) * rs)
                stat = jnp.where(stat_lane == j, weights[i][0][part], stat)
                stat = jnp.where(stat_lane == heads_block + j, weights[i][1][part], stat)
                acc_s[b, :, j * HD : (j + 1) * HD] = numerators[i][part].astype(bf16)
        stat_s[b] = stat
        finish()

    for copy in staged[6:10]:
        copy.wait()
    for c in range(n_out):
        ow_copy(c).start()
    for k in range(pre_n):

        def finish(k=k):
            if k == 0:
                pl.semaphore_wait(barrier, pre_n + row_n - 2)
            if k < pre_n - 1:
                stat_copy(far_pre[k]).start()
                acc_copy(far_pre[k]).start()

        attend(ahead(far_pre[k]) if k < pre_n - 1 else pre, finish)

    ffs_copy.start()
    for c in range(n_tiles):
        gu_copy(c).start()
    landed(stat_r, stat_sem.at[1])
    stat_of = [stat_s[pre]] + [stat_r[d - 1] for d in range(1, pre_n)]
    peak_of = [stat[:, :heads_block] for stat in stat_of]
    total_of = [stat[:, heads_block : 2 * heads_block] for stat in stat_of]
    highest = functools.reduce(jnp.maximum, peak_of)
    factor_of = [jnp.exp(peak - highest) for peak in peak_of]
    weight_sum = sum(factor * total for factor, total in zip(factor_of, total_of))
    factor_of = [factor / weight_sum for factor in factor_of]
    landed(acc_r, acc_sem.at[1])
    for j in range(heads_block):
        part = slice(j * HD, (j + 1) * HD)
        value = acc_s[pre, :, part].astype(f32) * factor_of[0][:, j : j + 1]
        for d in range(1, pre_n):
            value = value + acc_r[d - 1, :, part].astype(f32) * factor_of[d][:, j : j + 1]
        mix_g[row, :, part] = value.astype(bf16)
    for d in far_row:
        mix_copy(d).start()
    landed(ow, ow_sem)
    landed(mix_g.at[pl.ds(0, row_n - 1)], mix_sem.at[1])
    mix_x[...] = mix_g[...].astype(f32).reshape(everyone, block).astype(bf16)

    def project(c, carry):
        product = jnp.dot(mix_x[...], ow[c], preferred_element_type=f32)
        for p in range(pre_n):
            part = product[p * hs : (p + 1) * hs]
            prod_f[c, p] = part
            prod_s[c, p] = part.astype(bf16)
        for d in far_pre:
            prod_copy(c, d).start()
        return carry

    lax.fori_loop(0, n_out, project, 0)
    for copy in staged[10:]:
        copy.wait()
    for c in range(n_out):
        part = slice(c * out_width, (c + 1) * out_width)
        value = hid_ref[:, :, part].astype(f32).reshape(hs, out_width) + prod_f[c, pre]
        landed(prod_r.at[c], prod_sem.at[1 + c])
        for d in range(1, pre_n):
            value = value + prod_r[c, d - 1].astype(f32)
        res_g[pre, :, part] = value.astype(bf16)
        for d in far_pre:
            res_copy(c, d).start()
        res_out[:, :, part] = value.reshape(hid_local, STEPS, out_width).astype(bf16)
    ffs_copy.wait()
    ffn_pick = jnp.where(
        iota((rs, adapters), 1) == per_row(ids_ref, (rs, adapters)), 1.0, 0.0
    ).astype(bf16)
    ffn8[...] = jnp.dot(ffn_pick, ffs[...], preferred_element_type=f32)

    spread_from = iota((LANES, 4 * LANES), 0)
    spread_to = iota((LANES, 4 * LANES), 1)
    spread = jnp.where(
        spread_to
        == jnp.where(spread_to < 2 * LANES, 2 * spread_from, 2 * LANES + 2 * spread_from + 1),
        1.0,
        0.0,
    ).astype(bf16)

    def spread_chunk(c):
        at = slice(c * out_width, (c + 1) * out_width)
        residual = res_g[:, :, at].astype(f32).reshape(everyone, out_width)
        gain = gain_ref[at].astype(f32).reshape(1, out_width)
        normed = (residual * gain).astype(bf16)
        blocks = out_width // LANES
        stacked = jnp.concatenate(
            [normed[:, k * LANES : (k + 1) * LANES] for k in range(blocks)], axis=0
        )
        parts = jnp.dot(stacked, spread, preferred_element_type=f32).astype(bf16)
        for k in range(blocks):
            part = parts[k * everyone : (k + 1) * everyone]
            to = 2 * (c * out_width + k * LANES)
            x_exp[:everyone, to : to + 2 * LANES] = part[:, : 2 * LANES]
            x_exp[everyone:, to : to + 2 * LANES] = part[:, 2 * LANES :]
        return jnp.sum(residual * residual, axis=1, keepdims=True)

    def gather_chunks(first, last):
        for c in range(first, last):
            landed(
                res_g.at[pl.ds(0, pre_n - 1), :, pl.ds(0, out_width)], res_sem.at[1 + c]
            )
        return sum(spread_chunk(c) for c in range(first, last))

    def unit_product(g, first, last):
        at = slice(first * half_depth, last * half_depth)
        weights = [gu[g * unit_tiles + t, at] for t in range(unit_tiles)]
        weight = jnp.concatenate(weights, axis=1) if unit_tiles > 1 else weights[0]
        return jnp.dot(x_exp[:, at], weight, preferred_element_type=f32)

    def first_half(g, carry):
        gate_h[g] = unit_product(g, 0, 1)
        return carry

    def send_unit(g, product):
        for r in range(row_n):
            gate = product[r * rs : (r + 1) * rs]
            up = product[everyone + r * rs : everyone + (r + 1) * rs]
            both = jnp.concatenate([gate, up], axis=0)
            gate_f[g, r] = both
            gate_s[g, r] = both.astype(bf16)
        for d in far_row:
            gate_copy(g, d).start()

    def second_half(g, carry):
        send_unit(g, gate_h[g] + unit_product(g, 1, 2))
        return carry

    def whole_unit(g, carry):
        send_unit(g, unit_product(g, 0, halves))
        return carry

    squares = gather_chunks(0, half_chunks)
    landed(gu, gu_sem)
    if early > 0:
        lax.fori_loop(0, early, first_half, 0)
        squares = squares + gather_chunks(half_chunks, n_out)
    for r in range(row_n):
        sq_s[r] = jnp.broadcast_to(squares[r * rs : (r + 1) * rs], (rs, LANES))
    for d in range(1, row_n):
        sq_copy(d).start()
    if early > 0:
        lax.fori_loop(0, early, second_half, 0)
    for g in range(early, units_ff):
        whole_unit(g, 0)

    square_sum = sq_s[row]
    landed(sq_r, sq_sem.at[1])
    for d in range(1, row_n):
        square_sum = square_sum + sq_r[d - 1]
    inverse = lax.rsqrt(square_sum[:, :1] / D + 1e-05)

    def activate(both, at):
        gate = both[:rs] * inverse
        up = both[rs:] * inverse
        part = pl.ds(pl.multiple_of(at, LANES), unit)
        value = gate / (1.0 + jnp.exp(-gate)) * up * ffn8[:, part]
        act_out[:, :, part] = value.reshape(row_local, STEPS, unit).astype(bf16)

    def finish_unit(g, carry):
        landed(gate_r.at[g], gate_sem.at[1 + g])
        both = gate_f[g, row]
        for d in range(1, row_n):
            both = both + gate_r[g, d - 1].astype(f32)
        activate(both, g * unit)
        return carry

    for g in range(units_ff):
        finish_unit(g, 0)

    landed(stat_r, stat_sem.at[0])
    landed(acc_r, acc_sem.at[0])
    landed(mix_g.at[pl.ds(0, row_n - 1)], mix_sem.at[0])
    landed(prod_r, prod_sem.at[0])
    landed(res_g.at[pl.ds(0, pre_n - 1)], res_sem.at[0])
    landed(sq_r, sq_sem.at[0])
    landed(gate_r, gate_sem.at[0])


def hand_on(residual_ref, activation_ref, residual_out, activation_out, sem):
    residual = pltpu.make_async_copy(residual_ref, residual_out, sem.at[0])
    activation = pltpu.make_async_copy(activation_ref, activation_out, sem.at[1])
    residual.start()
    activation.start()
    residual.wait()
    activation.wait()


def per_device(
    queries,
    prefix_keys,
    prefix_values,
    suffix_keys,
    suffix_values,
    new_keys,
    new_values,
    hidden,
    adapter_ids,
    suffix_lengths,
    kv_scales,
    ffn_scales,
    out_weight,
    norm_gain,
    gate_up,
):
    pre_n = lax.axis_size("pre")
    row_n = lax.axis_size("row")
    row_local = queries.shape[0]
    rs = row_local * STEPS
    hs = hidden.shape[0] * STEPS
    kv_width = prefix_keys.shape[1]
    adapters, ff = ffn_scales.shape
    block, cols = out_weight.shape
    depth = gate_up.shape[0]
    out_width = min(cols, 512)
    n_out = cols // out_width
    unit = max(width for width in UNIT_WIDTHS if ff % width == 0)
    units_ff = ff // unit
    early = int(units_ff * EARLY_SHARE) if n_out % 2 == 0 else 0
    n_tiles = ff // LANES
    everyone = row_n * rs
    dma = pltpu.SemaphoreType.DMA
    vmem = pl.BlockSpec(memory_space=pltpu.VMEM)
    hbm = pl.BlockSpec(memory_space=pltpu.HBM)
    scratch = [
        pltpu.SMEM(adapter_ids.shape, jnp.int32),
        pltpu.SMEM(suffix_lengths.shape, jnp.int32),
        pltpu.VMEM(queries.shape, bf16),
        pltpu.VMEM(prefix_keys.shape, bf16),
        pltpu.VMEM(prefix_values.shape, bf16),
        pltpu.VMEM(suffix_keys.shape, bf16),
        pltpu.VMEM(suffix_values.shape, bf16),
        pltpu.VMEM(new_keys.shape, bf16),
        pltpu.VMEM(new_values.shape, bf16),
        pltpu.VMEM(hidden.shape, bf16),
        pltpu.VMEM(kv_scales.shape, bf16),
        pltpu.VMEM(norm_gain.shape, bf16),
        pltpu.VMEM((n_out, block, out_width), bf16),
        pltpu.VMEM((n_tiles, 2 * depth, LANES), bf16),
        pltpu.VMEM((adapters, ff), bf16),
        pltpu.VMEM((rs, D), f32),
        pltpu.VMEM((rs, kv_width), f32),
        pltpu.VMEM((rs, kv_width), f32),
        pltpu.VMEM((rs, kv_width), f32),
        pltpu.VMEM((rs, kv_width), f32),
        pltpu.VMEM((pre_n, rs, block), bf16),
        pltpu.VMEM((pre_n - 1, rs, block), bf16),
        pltpu.VMEM((pre_n, rs, LANES), f32),
        pltpu.VMEM((pre_n - 1, rs, LANES), f32),
        pltpu.VMEM((row_n, rs, block), bf16),
        pltpu.VMEM((everyone, block), bf16),
        pltpu.VMEM((n_out, pre_n, hs, out_width), bf16),
        pltpu.VMEM((n_out, pre_n, hs, out_width), f32),
        pltpu.VMEM((n_out, pre_n - 1, hs, out_width), bf16),
        pltpu.VMEM((pre_n, hs, cols), bf16),
        pltpu.VMEM((2 * everyone, 2 * depth), bf16),
        pltpu.VMEM((units_ff, row_n, 2 * rs, unit), bf16),
        pltpu.VMEM((units_ff, row_n, 2 * rs, unit), f32),
        pltpu.VMEM((units_ff, row_n - 1, 2 * rs, unit), bf16),
        pltpu.VMEM((max(early, 1), 2 * everyone, unit), f32),
        pltpu.VMEM((row_n, rs, LANES), f32),
        pltpu.VMEM((row_n - 1, rs, LANES), f32),
        pltpu.VMEM((rs, ff), f32),
        dma((12,)),
        dma,
        dma,
        dma,
        dma((2,)),
        dma((2,)),
        dma((2,)),
        dma((1 + n_out,)),
        dma((1 + n_out,)),
        dma((1 + units_ff,)),
        dma((2,)),
    ]
    outputs = pl.pallas_call(
        functools.partial(layer_kernel, (pre_n, row_n, units_ff, early)),
        out_shape=(
            jax.ShapeDtypeStruct(hidden.shape, bf16),
            jax.ShapeDtypeStruct((row_local, STEPS, ff), bf16),
        ),
        in_specs=[hbm] * 15,
        out_specs=(vmem, vmem),
        scratch_shapes=scratch,
        compiler_params=pltpu.CompilerParams(
            collective_id=0, has_side_effects=True, vmem_limit_bytes=GRANT * 1024 * 1024
        ),
    )(
        *(
            pltpu.with_memory_space_constraint(operand, pltpu.HBM)
            for operand in (
                adapter_ids,
                suffix_lengths,
                queries,
                prefix_keys,
                prefix_values,
                suffix_keys,
                suffix_values,
                new_keys,
                new_values,
                hidden,
                kv_scales,
                norm_gain,
                ffn_scales,
                out_weight,
                gate_up,
            )
        )
    )
    return pl.pallas_call(
        hand_on,
        out_shape=tuple(jax.ShapeDtypeStruct(value.shape, value.dtype) for value in outputs),
        in_specs=[vmem, vmem],
        out_specs=(hbm, hbm),
        scratch_shapes=[dma((2,))],
        compiler_params=pltpu.CompilerParams(vmem_limit_bytes=1024 * 1024),
    )(*outputs)


def solution(mesh):
    placed = (
        P(("grp", "row"), None, None),
        P(("grp", "pre"), None),
        P(("grp", "pre"), None),
        P(("grp", "row"), "pre", None),
        P(("grp", "row"), "pre", None),
        P(("grp", "row"), None, None),
        P(("grp", "row"), None, None),
        P(("grp", "pre"), None, "row"),
        P(("grp", "row")),
        P(("grp", "row")),
        P(),
        P(None, "pre"),
        P("pre", "row"),
        P("row"),
        P("row", None, "pre"),
    )
    return jax.shard_map(
        per_device,
        mesh=mesh,
        in_specs=placed,
        out_specs=(P(("grp", "pre"), None, "row"), P(("grp", "row"), None, "pre")),
        check_vma=False,
    )
```
